32 devices in a mesh: photo: 4 (over y, x), worker: 8 (over z, core).
Axes of the slice: x: 2, y: 2, z: 4, core: 2. Of those that a mesh axis runs over, the one named last changes fastest.
Arguments:
- descriptors: bfloat16 [128, 1024, 256], P(('photo', 'worker'))
- key_counts: int32 [128], replicated, may hold values from 256 to 1024
- pair_list: int32 [128, 2], P(('photo', 'worker')), may hold values from 0 to 127, as said below
- w_qk: bfloat16 [256, 256], replicated, may hold values from -0.375 to 0.375
- w_value: bfloat16 [256, 256], replicated, may hold values from -0.375 to 0.375
- w_out: bfloat16 [256, 256], replicated, may hold values from -0.375 to 0.375
- w_up: bfloat16 [512, 512], replicated, may hold values from -0.25 to 0.25
- b_up: float32 [512], replicated, may hold values from -3 to 3
- ln_gain: float32 [512], replicated, may hold values from 0.5 to 1.5
- ln_bias: float32 [512], replicated, may hold values from -3 to 3
- w_down: bfloat16 [512, 256], replicated, may hold values from -0.25 to 0.25
- b_down: float32 [256], replicated, may hold values from -3 to 3
Outputs:
- pair_states: bfloat16 [128, 2, 1024, 256], P(('photo', 'worker'))
- pooled_update: float32 [128, 1024, 256], P(('photo', 'worker'))
The draws below stay inside these ranges and needn't reach their ends.
Inputs may be any that keep to these rules, and one draw needn't show every extreme that they name: `pair_list`: on pair p the first image is (p // 4) * 4 + p % 4; the second is a different image whose index divided by 4 differs from that of the first by at most one, and both differences of one occur.
All inputs are finite; a program needn't handle non-finite values.
Results may differ from the reference program's by a relative error of at most 0.007.
Values may be sent and summed in bfloat16 or wider, within the bound.
No kernel may reach another device: no remote copies, remote signals or barrier semaphores. Data moves between devices by JAX's collectives and lax.ppermute only.
A program may use at most 128 MiB of HBM per device.

```python
import jax
import jax.numpy as jnp
from jax import lax

D = 256
HEAD_DIM = 64
MLP_WIDTH = 512
K = 1024
IMG_DEV = 4
PAIR_DEV = 4
IMAGES = 128
PAIRS = 128


def draw_descriptors(key, part):
    keys = jax.random.split(jax.random.fold_in(key, 37), 5)
    devices_all = IMAGES // IMG_DEV
    pool = max(K // 4, 1)
    landmarks = jnp.clip(jax.random.normal(keys[0], (devices_all, pool, D), jnp.float32), -6.0, 6.0)
    fresh = jnp.clip(jax.random.normal(keys[1], (IMAGES, K, D), jnp.float32), -6.0, 6.0)
    owner = jnp.arange(IMAGES, dtype=jnp.int32) // IMG_DEV
    side = jax.random.randint(keys[2], (IMAGES, K), -1, 2)
    source = jnp.clip(owner[:, None] + side, 0, devices_all - 1)
    landmark_slot = jax.random.randint(keys[3], (IMAGES, K), 0, pool)
    copied = landmarks[source, landmark_slot] + 0.3 * fresh
    keep = jax.random.randint(keys[4], (IMAGES, K), 0, 5) < 3
    values = jnp.where(keep[:, :, None], copied, fresh)
    return values.astype(jnp.bfloat16)


def draw_key_counts(key, part):
    first_key, second_key, third_key = jax.random.split(jax.random.fold_in(key, 11), 3)
    counts = jax.random.randint(first_key, (IMAGES,), K // 4, K + 1)
    top_place = jax.random.randint(second_key, (), 0, IMAGES)
    low_place = (top_place + 1 + jax.random.randint(third_key, (), 0, IMAGES - 1)) % IMAGES
    counts = counts.at[top_place].set(K)
    counts = counts.at[low_place].set(K // 4)
    return counts.astype(jnp.int32)


def draw_pair_list(key, part):
    first_key, second_key, third_key = jax.random.split(jax.random.fold_in(key, 23), 3)
    devices_all = PAIRS // PAIR_DEV
    index = jnp.arange(PAIRS, dtype=jnp.int32)
    device = index // PAIR_DEV
    slot = index % PAIR_DEV
    owned = device * IMG_DEV + slot % IMG_DEV
    drift = jax.random.randint(first_key, (PAIRS,), -1, 2)
    side = jnp.where(slot == 0, 1, jnp.where(slot == 1, -1, drift))
    side = jnp.where(device + side > devices_all - 1, -1, side)
    side = jnp.where(device + side < 0, 1, side)
    partner = (device + side) * IMG_DEV + jax.random.randint(second_key, (PAIRS,), 0, IMG_DEV)
    other_local = (slot % IMG_DEV + 1 + jax.random.randint(third_key, (PAIRS,), 0, IMG_DEV - 1)) % IMG_DEV
    partner = jnp.where(side == 0, device * IMG_DEV + other_local, partner)
    return jnp.stack([owned, partner], axis=-1).astype(jnp.int32)


def bell_draw(key, extent, deviation, bound, held_as=jnp.bfloat16):
    array = jax.random.normal(key, extent, jnp.float32) * deviation
    return jnp.minimum(jnp.maximum(array, -bound), bound).astype(held_as)


def setup_inputs(seed: int = 0) -> dict:
    seeds = jax.random.split(jax.random.key(seed), 13)
    descriptors = draw_descriptors(jax.random.fold_in(seeds[12], 71), 0)
    key_counts = draw_key_counts(jax.random.fold_in(seeds[12], 71), 0)
    pair_list = draw_pair_list(jax.random.fold_in(seeds[12], 71), 0)
    w_qk = bell_draw(seeds[3], (D, D), D ** -0.5, 0.375)
    w_value = bell_draw(seeds[4], (D, D), D ** -0.5, 0.375)
    w_out = bell_draw(seeds[5], (D, D), D ** -0.5, 0.375)
    w_up = bell_draw(seeds[6], (MLP_WIDTH, MLP_WIDTH), MLP_WIDTH ** -0.5, 0.25)
    b_up = bell_draw(seeds[7], (MLP_WIDTH,), 0.5, 3.0, jnp.float32)
    ln_gain = jnp.clip(1.0 + 0.1 * jax.random.normal(seeds[8], (MLP_WIDTH,), jnp.float32), 0.5, 1.5)
    ln_bias = bell_draw(seeds[9], (MLP_WIDTH,), 0.5, 3.0, jnp.float32)
    w_down = bell_draw(seeds[10], (MLP_WIDTH, D), MLP_WIDTH ** -0.5, 0.25)
    b_down = bell_draw(seeds[11], (D,), 0.5, 3.0, jnp.float32)
    return dict(descriptors=descriptors, key_counts=key_counts, pair_list=pair_list, w_qk=w_qk, w_value=w_value, w_out=w_out, w_up=w_up, b_up=b_up, ln_gain=ln_gain, ln_bias=ln_bias, w_down=w_down, b_down=b_down)


def attend(queries, keys, values, count):
    heads = queries.shape[1] // HEAD_DIM
    query_heads = queries.astype(jnp.float32).reshape(K, heads, HEAD_DIM)
    key_heads = keys.astype(jnp.float32).reshape(K, heads, HEAD_DIM)
    value_heads = values.astype(jnp.float32).reshape(K, heads, HEAD_DIM)
    scores = jnp.einsum('qhd,khd->hqk', query_heads, key_heads) * HEAD_DIM ** (-0.5)
    valid = jnp.arange(K, dtype=jnp.int32) < count
    scores = jnp.where(valid[None, None, :], scores, -jnp.inf)
    weights = jax.nn.softmax(scores, axis=-1).astype(jnp.bfloat16).astype(jnp.float32)
    mixed = jnp.einsum('hqk,khd->qhd', weights, value_heads)
    return mixed.reshape(K, heads * HEAD_DIM).astype(jnp.bfloat16)

def refine(start, message, w_out, w_up, b_up, ln_gain, ln_bias, w_down, b_down):
    sent = jnp.dot(message, w_out, preferred_element_type=jnp.float32).astype(jnp.bfloat16)
    joined = jnp.concatenate([start, sent], axis=-1)
    hidden = jnp.dot(joined, w_up, preferred_element_type=jnp.float32) + b_up
    center = lax.optimization_barrier(jnp.mean(hidden, axis=-1, keepdims=True))
    spread = lax.optimization_barrier(jnp.mean((hidden - center) ** 2, axis=-1, keepdims=True))
    normed = (hidden - center) * lax.rsqrt(spread + 1e-05) * ln_gain + ln_bias
    act = jax.nn.gelu(normed, approximate=False).astype(jnp.bfloat16)
    delta = jnp.dot(act, w_down, preferred_element_type=jnp.float32) + b_down
    return ((start.astype(jnp.float32) + delta).astype(jnp.bfloat16), delta)

def reference(descriptors, key_counts, pair_list, w_qk, w_value, w_out, w_up, b_up, ln_gain, ln_bias, w_down, b_down):

    def step(pooled, pair_row):
        first = pair_row[0].astype(jnp.int32)
        second = pair_row[1].astype(jnp.int32)
        x_first = lax.dynamic_index_in_dim(descriptors, first, 0, keepdims=False)
        x_second = lax.dynamic_index_in_dim(descriptors, second, 0, keepdims=False)
        count_first = lax.dynamic_index_in_dim(key_counts, first, 0, keepdims=False)
        count_second = lax.dynamic_index_in_dim(key_counts, second, 0, keepdims=False)
        qk_first = jnp.dot(x_first, w_qk, preferred_element_type=jnp.float32).astype(jnp.bfloat16)
        qk_second = jnp.dot(x_second, w_qk, preferred_element_type=jnp.float32).astype(jnp.bfloat16)
        val_first = jnp.dot(x_first, w_value, preferred_element_type=jnp.float32).astype(jnp.bfloat16)
        val_second = jnp.dot(x_second, w_value, preferred_element_type=jnp.float32).astype(jnp.bfloat16)
        msg_first = attend(qk_first, qk_second, val_second, count_second)
        msg_second = attend(qk_second, qk_first, val_first, count_first)
        new_first, delta_first = refine(x_first, msg_first, w_out, w_up, b_up, ln_gain, ln_bias, w_down, b_down)
        new_second, delta_second = refine(x_second, msg_second, w_out, w_up, b_up, ln_gain, ln_bias, w_down, b_down)
        pooled = pooled.at[first].add(delta_first)
        pooled = pooled.at[second].add(delta_second)
        return (pooled, jnp.stack([new_first, new_second], axis=0))
    pooled0 = jnp.zeros((IMAGES, K, D), jnp.float32)
    pooled, pair_states = lax.scan(step, pooled0, pair_list)
    return (pair_states, pooled)
```

```python
import jax
import jax.numpy as jnp
from jax import lax
from jax.experimental import pallas as pl
from jax.experimental.pallas import tpu as pltpu
from jax.sharding import PartitionSpec as P

HEAD_DIM = 64
LANES = 128
F32 = jnp.float32
BF16 = jnp.bfloat16
LOG2E = 1.4426950408889634
AXES = ("photo", "worker")
EXPONENT_BOUND = 96.0
VALUE_BOUND = 2.0**18


def dot(a, b):
    return jnp.dot(a, b, preferred_element_type=F32)


def dot_rows(a, b):
    return lax.dot_general(a, b, (((1,), (1,)), ((), ())), preferred_element_type=F32)


def dot_columns(a, b):
    return lax.dot_general(a, b, (((0,), (0,)), ((), ())), preferred_element_type=F32)


def rows_of(index, size):
    return pl.ds(pl.multiple_of(index * size, size), size)


def refine(start, message, w_out, w_up, b_up, ln_gain, ln_bias, w_down, b_down):
    width = start.shape[1]
    sent = dot(message, w_out[...]).astype(BF16)
    hidden = dot(start, w_up[:width, :]) + dot(sent, w_up[width:, :]) + b_up[...]
    center = jnp.mean(hidden, axis=-1, keepdims=True)
    shifted = hidden - center
    spread = jnp.mean(shifted * shifted, axis=-1, keepdims=True)
    normed = shifted * lax.rsqrt(spread + 1e-05) * ln_gain[...] + ln_bias[...]
    act = (0.5 * normed * (1.0 + lax.erf(normed * (0.5**0.5)))).astype(BF16)
    return dot(act, w_down[...]) + b_down[...]


def pair_kernel(
    slot, chained, images,
    pairs, counts, place, own, lower, upper,
    w_qk, w_value, w_out, w_up, b_up, ln_gain, ln_bias, w_down, b_down,
    *refs,
):
    refs = refs[2:] if chained else refs
    (
        states, first_delta, second_delta,
        x_first, x_second, q_first, k_first, k_second, v_first, v_second,
        weights, m_first, m_second, copies,
    ) = refs
    slots, width = x_first.shape
    heads = width // HEAD_DIM
    first = pairs[slot, 0]
    second = pairs[slot, 1]
    base = place[0] * images
    count_first = counts[first]
    count_second = counts[second]
    local = second - base
    load = pltpu.make_async_copy(own.at[first - base], x_first, copies.at[0])
    load.start()

    @pl.when((local >= 0) & (local < images))
    def _():
        pltpu.make_async_copy(own.at[jnp.clip(local, 0, images - 1)], x_second, copies.at[1]).start()

    @pl.when(local < 0)
    def _():
        pltpu.make_async_copy(lower, x_second, copies.at[1]).start()

    @pl.when(local >= images)
    def _():
        pltpu.make_async_copy(upper, x_second, copies.at[1]).start()

    load.wait()
    pltpu.make_async_copy(lower, x_second, copies.at[1]).wait()

    block = min(512, slots)
    lane = lax.broadcasted_iota(jnp.int32, (block, LANES), 1)
    halves = (lane < HEAD_DIM, lane >= HEAD_DIM)

    def project(index, bounds):
        rows = rows_of(index, block)
        row = lax.broadcasted_iota(jnp.int32, (block, LANES), 0) + index * block
        query = dot(x_first[rows, :], w_qk[...])
        key = dot(x_second[rows, :], w_qk[...])
        k_first[rows, :] = query.astype(BF16)
        k_second[rows, :] = key.astype(BF16)
        scaled = query * (HEAD_DIM**-0.5 * LOG2E)
        value_one = dot(x_first[rows, :], w_value[...])
        value_two = dot(x_second[rows, :], w_value[...])
        empty = jnp.zeros((block, LANES), BF16)
        for head in range(heads):
            start = head * HEAD_DIM // LANES * LANES
            columns = slice(start, start + LANES)
            half = halves[head % 2]
            for other in range(0, width, LANES):
                if other != start:
                    q_first[head, rows, other : other + LANES] = empty
            q_first[head, rows, columns] = jnp.where(half, scaled[:, columns], 0.0).astype(BF16)
            for value, held, count in (
                (value_one, v_first, count_first),
                (value_two, v_second, count_second),
            ):
                valid = half & (row < count)
                held[head, rows, :LANES] = jnp.where(valid, value[:, columns], 0.0).astype(BF16)
                held[head, rows, LANES:] = jnp.where(valid, 1.0, 0.0).astype(BF16)
        query_norm = jnp.max(jnp.sum(scaled * scaled, axis=-1, keepdims=True))
        key_norm = jnp.max(jnp.sum(key * key, axis=-1, keepdims=True))
        largest = jnp.maximum(jnp.max(jnp.abs(value_one)), jnp.max(jnp.abs(value_two)))
        return (
            jnp.maximum(bounds[0], query_norm),
            jnp.maximum(bounds[1], key_norm),
            jnp.maximum(bounds[2], largest),
        )

    zero = jnp.float32(0.0)
    query_norm, key_norm, largest = lax.fori_loop(0, slots // block, project, (zero, zero, zero))
    in_range = (query_norm * key_norm <= EXPONENT_BOUND**2) & (largest <= VALUE_BOUND)

    @pl.when(in_range)
    def _():
        tile = min(256, slots)
        for start in range(0, heads, 2):
            columns = slice(start * HEAD_DIM, start * HEAD_DIM + LANES)

            def score(index, carry):
                rows = rows_of(index, tile)
                for side in range(2):
                    scores = dot_rows(q_first[start + side], k_second[rows, :])
                    weights[side, :, rows] = jnp.exp2(scores).astype(BF16)
                return carry

            lax.fori_loop(0, slots // tile, score, 0)
            total = dot(weights[0], v_second[start]) + dot(weights[1], v_second[start + 1])
            m_first[:, columns] = (total[:, :LANES] / total[:, LANES:]).astype(BF16)
            total = dot_columns(weights[0], v_first[start]) + dot_columns(weights[1], v_first[start + 1])
            m_second[:, columns] = (total[:, :LANES] / total[:, LANES:]).astype(BF16)

    @pl.when(jnp.logical_not(in_range))
    def _():
        tile = min(128, slots)
        position = lax.broadcasted_iota(jnp.int32, (tile, slots), 1)
        column = lax.broadcasted_iota(jnp.int32, (tile, width), 1)

        def attend(index, carry):
            rows = rows_of(index, tile)
            for queries, keys, held, message, count in (
                (k_first, k_second, v_second, m_first, count_second),
                (k_second, k_first, v_first, m_second, count_first),
            ):
                for start in range(0, heads, 2):
                    columns = slice(start * HEAD_DIM, start * HEAD_DIM + LANES)
                    total = jnp.zeros((tile, 2 * LANES), F32)
                    for head in (start, start + 1):
                        query = queries[rows, :].astype(F32)
                        query = jnp.where(column // HEAD_DIM == head, query, 0.0).astype(BF16)
                        scores = dot_rows(query, keys[...]) * HEAD_DIM**-0.5
                        scores = jnp.where(position < count, scores, -jnp.inf)
                        scores = jnp.exp(scores - jnp.max(scores, axis=-1, keepdims=True))
                        scores = scores / jnp.sum(scores, axis=-1, keepdims=True)
                        total = total + dot(scores.astype(BF16), held[head])
                    message[rows, columns] = total[:, :LANES].astype(BF16)
            return carry

        lax.fori_loop(0, slots // tile, attend, 0)

    for side, start, message, delta in (
        (1, x_second, m_second, second_delta),
        (0, x_first, m_first, first_delta),
    ):
        tile = min(512, slots)
        for row in range(0, slots, tile):
            rows = slice(row, row + tile)
            here = start[rows, :]
            update = refine(here, message[rows, :], w_out, w_up, b_up, ln_gain, ln_bias, w_down, b_down)
            delta[rows, :] = update.astype(delta.dtype)
            states[side, rows, :] = (here.astype(F32) + update).astype(BF16)


def process(slot, held, pairs, counts, place, own, lower, upper, parameters):
    images, slots, width = own.shape
    pairs_here = pairs.shape[0]
    heads = width // HEAD_DIM
    chained = held is not None
    memory = pl.BlockSpec(memory_space=pl.ANY)
    scalars = pl.BlockSpec(memory_space=pltpu.SMEM)
    whole = pl.BlockSpec(memory_space=pltpu.VMEM)
    hidden = parameters[3].shape[1]
    flops = 2 * slots * (4 * width * width + 6 * slots * width + 2 * (width * width + 2 * width * hidden + hidden * width))

    def body(*refs):
        pair_kernel(slot, chained, images, *refs)

    return pl.pallas_call(
        body,
        grid=(1,),
        in_specs=[scalars] * 3 + [memory] * 3 + [whole] * len(parameters) + ([memory] * 2 if chained else []),
        out_specs=[
            pl.BlockSpec((pl.Squeezed(), 2, slots, width), lambda i: (slot, 0, 0, 0)),
            pl.BlockSpec((pl.Squeezed(), slots, width), lambda i: (slot, 0, 0)),
            pl.BlockSpec((slots, width), lambda i: (0, 0)),
        ],
        out_shape=[
            jax.ShapeDtypeStruct((pairs_here, 2, slots, width), BF16),
            jax.ShapeDtypeStruct((images, slots, width), F32),
            jax.ShapeDtypeStruct((slots, width), BF16),
        ],
        scratch_shapes=[
            pltpu.VMEM((slots, width), BF16),
            pltpu.VMEM((slots, width), BF16),
            pltpu.VMEM((heads, slots, width), BF16),
            pltpu.VMEM((slots, width), BF16),
            pltpu.VMEM((slots, width), BF16),
            pltpu.VMEM((heads, slots, 2 * LANES), BF16),
            pltpu.VMEM((heads, slots, 2 * LANES), BF16),
            pltpu.VMEM((2, slots, slots), BF16),
            pltpu.VMEM((slots, width), BF16),
            pltpu.VMEM((slots, width), BF16),
            pltpu.SemaphoreType.DMA((2,)),
        ],
        input_output_aliases={6 + len(parameters): 0, 7 + len(parameters): 1} if chained else {},
        compiler_params=pltpu.CompilerParams(vmem_limit_bytes=56 * 1024 * 1024),
        cost_estimate=pl.CostEstimate(flops=flops, bytes_accessed=8 * slots * width * 2, transcendentals=slots * slots * heads),
        name=f"pair_{slot}",
    )(pairs, counts, place, own, lower, upper, *parameters, *(held or ()))


def combine_kernel(order, images, pairs, below, above, place, *refs):
    terms = refs[1:-1]
    held, out = refs[0], refs[-1]
    image = place[0] * images + pl.program_id(1)
    out[...] = held[...]
    for (source, slot), term in zip(order, terms):
        listed = (pairs, below, above)[source]
        here = listed[slot, 1] == image
        if source == 1:
            here = here & (place[0] > 0)
        if source == 2:
            here = here & (place[0] < place[1] - 1)

        @pl.when(here)
        def _():
            out[...] += term[...].astype(F32)


def combine(order, held, terms, pairs, below, above, place):
    images, slots, width = held.shape
    tile = min(256, slots)
    scalars = pl.BlockSpec(memory_space=pltpu.SMEM)
    spread = pl.BlockSpec((pl.Squeezed(), tile, width), lambda r, g: (g, r, 0))

    def body(*refs):
        combine_kernel(order, images, *refs)

    return pl.pallas_call(
        body,
        grid=(slots // tile, images),
        in_specs=[scalars] * 4 + [spread] + [pl.BlockSpec((tile, width), lambda r, g: (r, 0))] * len(terms),
        out_specs=spread,
        out_shape=jax.ShapeDtypeStruct(held.shape, F32),
        input_output_aliases={4: 0},
        cost_estimate=pl.CostEstimate(flops=len(terms) * slots * width, bytes_accessed=held.size * 8 + len(terms) * slots * width * 2, transcendentals=0),
        name=f"combine_{len(terms)}",
    )(pairs, below, above, place, held, *terms)


def local(descriptors, key_counts, pair_list, w_qk, w_value, w_out, w_up, b_up, ln_gain, ln_bias, w_down, b_down):
    images = descriptors.shape[0]
    pairs_here = pair_list.shape[0]
    peers = lax.axis_size(AXES)
    position = lax.axis_index(AXES)
    up = [(i, i + 1) for i in range(peers - 1)]
    down = [(j, i) for i, j in up]
    place = jnp.stack([position, jnp.int32(peers)]).astype(jnp.int32)
    base = position * images
    below = lax.ppermute(pair_list, AXES, up)
    above = lax.ppermute(pair_list, AXES, down)
    wanted_above = jnp.clip(above[:, 1] - base, 0, images - 1)
    wanted_below = jnp.clip(below[:, 1] - base, 0, images - 1)
    parameters = (
        w_qk, w_value, w_out, w_up, b_up[None, :], ln_gain[None, :], ln_bias[None, :], w_down, b_down[None, :],
    )
    arrived = []
    for slot in range(pairs_here):
        to_above = lax.dynamic_index_in_dim(descriptors, wanted_above[slot], 0, keepdims=False)
        to_below = lax.dynamic_index_in_dim(descriptors, wanted_below[slot], 0, keepdims=False)
        arrived.append((lax.ppermute(to_above, AXES, up), lax.ppermute(to_below, AXES, down)))
    held = None
    early, late, early_order, late_order = ([], [], [], [])
    for slot in range(pairs_here):
        lower, upper = arrived[slot]
        states, totals, update = process(
            slot, held, pair_list, key_counts, place, descriptors, lower, upper, parameters
        )
        held = (states, totals)
        early.append(update)
        early_order.append((0, slot))
        last = slot == pairs_here - 1
        terms, order = (late, late_order) if last else (early, early_order)
        terms.append(lax.ppermute(update, AXES, up))
        order.append((1, slot))
        terms.append(lax.ppermute(update, AXES, down))
        order.append((2, slot))
    states, totals = held
    totals = combine(early_order, totals, early, pair_list, below, above, place)
    totals = combine(late_order, totals, late, pair_list, below, above, place)
    return (states, totals)


def solution(mesh):
    in_specs = (P(AXES, None, None), P(), P(AXES, None)) + (P(),) * 9
    out_specs = (P(AXES, None, None, None), P(AXES, None, None))
    return jax.shard_map(local, mesh=mesh, in_specs=in_specs, out_specs=out_specs, check_vma=False)
```

```python
import jax
import jax.numpy as jnp
from jax import lax
from jax.experimental import pallas as pl
from jax.experimental.pallas import tpu as pltpu
from jax.sharding import PartitionSpec as P

HEAD_DIM = 64
LANES = 128
F32 = jnp.float32
BF16 = jnp.bfloat16
LOG2E = 1.4426950408889634
AXES = ("photo", "worker")
EXPONENT_BOUND = 96.0
VALUE_BOUND = 2.0**18


def dot(a, b):
    return jnp.dot(a, b, preferred_element_type=F32)


def dot_rows(a, b):
    return lax.dot_general(a, b, (((1,), (1,)), ((), ())), preferred_element_type=F32)


def dot_columns(a, b):
    return lax.dot_general(a, b, (((0,), (0,)), ((), ())), preferred_element_type=F32)


def rows_of(index, size):
    return pl.ds(pl.multiple_of(index * size, size), size)


def refine(start, message, w_out, w_up, b_up, ln_gain, ln_bias, w_down, b_down):
    width = start.shape[1]
    sent = dot(message, w_out[...]).astype(BF16)
    hidden = dot(start, w_up[:width, :]) + dot(sent, w_up[width:, :]) + b_up[...]
    center = jnp.mean(hidden, axis=-1, keepdims=True)
    shifted = hidden - center
    spread = jnp.mean(shifted * shifted, axis=-1, keepdims=True)
    normed = shifted * lax.rsqrt(spread + 1e-05) * ln_gain[...] + ln_bias[...]
    act = (0.5 * normed * (1.0 + lax.erf(normed * (0.5**0.5)))).astype(BF16)
    return dot(act, w_down[...]) + b_down[...]


def across(position):
    return jnp.where(position % 2 == 1, position + 1, position - 1)


def arrange(pairs, count, base, images):
    hits = [(pairs[s, 1] >= base) & (pairs[s, 1] < base + images) for s in range(count)]
    hits = [h.astype(jnp.int32) for h in hits]
    inside = count - sum(hits)
    places, seen_in, seen_out = ([], jnp.int32(0), jnp.int32(0))
    for hit in hits:
        places.append(jnp.where(hit == 1, inside + seen_out, seen_in))
        seen_out = seen_out + hit
        seen_in = seen_in + 1 - hit
    return (hits, places, inside)


def chosen(pairs, count, base, images, step):
    hits, places, inside = arrange(pairs, count, base, images)
    turn = jnp.int32(0) if step == 0 else step - 1 + jnp.minimum(inside, 1)
    exists = (inside > 0) if step == 0 else (turn < count)
    row = sum(jnp.where(p == turn, s, 0) for s, p in enumerate(places))
    hit = sum(jnp.where(p == turn, h, 0) for h, p in zip(hits, places))
    return (row, exists, hit == 1, inside)


def ranks(pairs, count, base, images):
    firsts = []
    for image in range(images):
        first = jnp.int32(count + image)
        for slot in reversed(range(count)):
            first = jnp.where(pairs[slot, 1] == base + image, slot, first)
        firsts.append(first)
    return [
        sum((other < first).astype(jnp.int32) for other in firsts) for first in firsts
    ]


def pick(values, index):
    return sum(jnp.where(index == i, v, 0) for i, v in enumerate(values))


def step_kernel(
    step, images, rounds,
    pairs, partner, counts, place, own, beside, *refs,
):
    crossed, refs = refs[: len(rounds)], refs[len(rounds) :]
    (
        w_qk, w_value, w_out, w_up, b_up, ln_gain, ln_bias, w_down, b_down,
    ), refs = refs[:9], refs[9:]
    (
        states, totals, update,
        x_first, x_second, q_first, k_first, k_second, v_first, v_second,
        weights, m_first, m_second, new_states, new_delta, new_update, copies, sends,
    ) = refs[-18:]
    slots, width = x_first.shape
    heads = width // HEAD_DIM
    count = pairs.shape[0]
    position = place[0]
    base = position * images
    beside_base = (position + 1 - 2 * (position % 2)) * images
    other = across(position)
    other_base = other * images
    paired = (other >= 0) & (other < place[1])
    first_load = pltpu.make_async_copy(own.at[0], x_first, copies.at[0])
    second_load = pltpu.make_async_copy(own.at[0], x_second, copies.at[1])

    def load_across(rank, held, copy):
        offset = 0
        for ref in crossed:
            size = ref.shape[0]

            @pl.when((rank >= offset) & (rank < offset + size))
            def _():
                pltpu.make_async_copy(ref.at[jnp.clip(rank - offset, 0, size - 1)], held, copies.at[copy]).start()

            offset += size

    def run(first, second, row, ours):
        count_first = counts[first]
        count_second = counts[second]
        block = min(512, slots)
        lane = lax.broadcasted_iota(jnp.int32, (block, LANES), 1)
        halves = (lane < HEAD_DIM, lane >= HEAD_DIM)
        first_load.wait()
        second_load.wait()

        def project(index, bounds):
            rows = rows_of(index, block)
            line = lax.broadcasted_iota(jnp.int32, (block, LANES), 0) + index * block
            query = dot(x_first[rows, :], w_qk[...])
            key = dot(x_second[rows, :], w_qk[...])
            k_first[rows, :] = query.astype(BF16)
            k_second[rows, :] = key.astype(BF16)
            scaled = query * (HEAD_DIM**-0.5 * LOG2E)
            value_one = dot(x_first[rows, :], w_value[...])
            value_two = dot(x_second[rows, :], w_value[...])
            empty = jnp.zeros((block, LANES), BF16)
            for head in range(heads):
                start = head * HEAD_DIM // LANES * LANES
                columns = slice(start, start + LANES)
                half = halves[head % 2]
                for gap in range(0, width, LANES):
                    if gap != start:
                        q_first[head, rows, gap : gap + LANES] = empty
                q_first[head, rows, columns] = jnp.where(half, scaled[:, columns], 0.0).astype(BF16)
                for value, held, limit in (
                    (value_one, v_first, count_first),
                    (value_two, v_second, count_second),
                ):
                    valid = half & (line < limit)
                    held[head, rows, :LANES] = jnp.where(valid, value[:, columns], 0.0).astype(BF16)
                    held[head, rows, LANES:] = jnp.where(valid, 1.0, 0.0).astype(BF16)
            query_norm = jnp.max(jnp.sum(scaled * scaled, axis=-1, keepdims=True))
            key_norm = jnp.max(jnp.sum(key * key, axis=-1, keepdims=True))
            largest = jnp.maximum(jnp.max(jnp.abs(value_one)), jnp.max(jnp.abs(value_two)))
            return (
                jnp.maximum(bounds[0], query_norm),
                jnp.maximum(bounds[1], key_norm),
                jnp.maximum(bounds[2], largest),
            )

        zero = jnp.float32(0.0)
        query_norm, key_norm, largest = lax.fori_loop(0, slots // block, project, (zero, zero, zero))
        in_range = (query_norm * key_norm <= EXPONENT_BOUND**2) & (largest <= VALUE_BOUND)

        @pl.when(in_range)
        def _():
            tile = min(256, slots)
            for start in range(0, heads, 2):
                columns = slice(start * HEAD_DIM, start * HEAD_DIM + LANES)

                def score(index, carry):
                    rows = rows_of(index, tile)
                    for side in range(2):
                        scores = dot_rows(q_first[start + side], k_second[rows, :])
                        weights[side, :, rows] = jnp.exp2(scores).astype(BF16)
                    return carry

                lax.fori_loop(0, slots // tile, score, 0)
                total = dot(weights[0], v_second[start]) + dot(weights[1], v_second[start + 1])
                m_first[:, columns] = (total[:, :LANES] / total[:, LANES:]).astype(BF16)
                total = dot_columns(weights[0], v_first[start]) + dot_columns(weights[1], v_first[start + 1])
                m_second[:, columns] = (total[:, :LANES] / total[:, LANES:]).astype(BF16)

        @pl.when(jnp.logical_not(in_range))
        def _():
            tile = min(64, slots)
            spot = lax.broadcasted_iota(jnp.int32, (tile, slots), 1)
            column = lax.broadcasted_iota(jnp.int32, (tile, width), 1)
            for queries, keys, held, message, limit in (
                (k_first, k_second, v_second, m_first, count_second),
                (k_second, k_first, v_first, m_second, count_first),
            ):
                def attend(index, carry):
                    rows = rows_of(index, tile)
                    query_rows = queries[rows, :].astype(F32)
                    for start in range(0, heads, 2):
                        columns = slice(start * HEAD_DIM, start * HEAD_DIM + LANES)

                        def one_head(head, total):
                            query = jnp.where(column // HEAD_DIM == head, query_rows, 0.0).astype(BF16)
                            scores = dot_rows(query, keys[...]) * HEAD_DIM**-0.5
                            scores = jnp.where(spot < limit, scores, -jnp.inf)
                            scores = jnp.exp(scores - jnp.max(scores, axis=-1, keepdims=True))
                            scores = scores / jnp.sum(scores, axis=-1, keepdims=True)
                            return total + dot(scores.astype(BF16), held[head])

                        total = lax.fori_loop(start, start + 2, one_head, jnp.zeros((tile, 2 * LANES), F32))
                        message[rows, columns] = total[:, :LANES].astype(BF16)
                    return carry

                lax.fori_loop(0, slots // tile, attend, 0)

        tile = min(1024, slots)

        def finish(side, start, message):
            def one(index, carry):
                rows = rows_of(index, tile)
                here = start[rows, :]
                change = refine(here, message[rows, :], w_out, w_up, b_up, ln_gain, ln_bias, w_down, b_down)
                new_states[side, rows, :] = (here.astype(F32) + change).astype(BF16)
                if side == 1:
                    new_update[rows, :] = change.astype(BF16)
                else:
                    new_delta[rows, :] = change
                return carry

            lax.fori_loop(0, slots // tile, one, 0)

        finish(1, x_second, m_second)
        shared = not ours or step < count
        if shared:
            send_update = pltpu.make_async_copy(new_update, update, sends.at[0])
            send_update.start()
        if ours:
            send_states = pltpu.make_async_copy(new_states, states.at[row], sends.at[1])
            send_delta = pltpu.make_async_copy(new_delta, totals.at[first - base], sends.at[2])
            finish(0, x_first, m_first)
            send_states.start()
            send_delta.start()
            send_states.wait()
            send_delta.wait()
        if shared:
            send_update.wait()

    row, exists, is_across, inside = chosen(pairs, count, other_base, images, step)
    first = base + jnp.clip(pairs[row, 0] - base, 0, images - 1)
    second = pairs[row, 1]

    @pl.when(exists)
    def _():
        pltpu.make_async_copy(own.at[first - base], x_first, copies.at[0]).start()
        near = second - base
        next_to = second - beside_base

        @pl.when((near >= 0) & (near < images))
        def _():
            pltpu.make_async_copy(own.at[jnp.clip(near, 0, images - 1)], x_second, copies.at[1]).start()

        @pl.when((next_to >= 0) & (next_to < images))
        def _():
            pltpu.make_async_copy(beside.at[jnp.clip(next_to, 0, images - 1)], x_second, copies.at[1]).start()

        if step > 0:
            @pl.when(is_across)
            def _():
                sent = ranks(pairs, count, other_base, images)
                load_across(pick(sent, second - other_base), x_second, 1)

        run(first, second, row, True)

    if step == count:
        _, _, their_inside = arrange(partner, count, base, images)
        again = paired & (their_inside == 0)

        @pl.when(again)
        def _():
            theirs = partner[count - 1, 0]
            mine = partner[count - 1, 1]
            sent = ranks(pairs, count, other_base, images)
            pltpu.make_async_copy(own.at[jnp.clip(mine - base, 0, images - 1)], x_second, copies.at[1]).start()
            load_across(pick(sent, theirs - other_base), x_first, 0)
            run(theirs, mine, 0, False)


def take_step(step, held, index, depth, pairs, partner, counts, place, own, beside, crossed, parameters):
    images, slots, width = own.shape
    pairs_here = pairs.shape[0]
    heads = width // HEAD_DIM
    memory = pl.BlockSpec(memory_space=pl.ANY)
    scalars = pl.BlockSpec(memory_space=pltpu.SMEM)
    whole = pl.BlockSpec(memory_space=pltpu.VMEM)
    hidden = parameters[3].shape[1]
    flops = 2 * slots * (4 * width * width + 6 * slots * width + 2 * (width * width + 2 * width * hidden + hidden * width))
    flops = flops if step < pairs_here else 1000
    operands = (pairs, partner, counts, place, own, beside, *crossed, *parameters)
    chained = [(i, a) for i, a in enumerate(held) if a is not None]
    aliases = {len(operands) + n: i for n, (i, _) in enumerate(chained)}
    shapes = (
        jax.ShapeDtypeStruct((pairs_here, 2, slots, width), BF16),
        jax.ShapeDtypeStruct((images, slots, width), F32),
        jax.ShapeDtypeStruct((depth, slots, width), BF16),
    )
    fixed = len(operands)

    def body(*refs):
        refs = refs[:fixed] + refs[fixed + len(chained) :]
        states, totals, updates = refs[fixed : fixed + 3]
        step_kernel(
            step, images, crossed, *refs[:fixed], states, totals, updates.at[index], *refs[fixed + 3 :]
        )

    return pl.pallas_call(
        body,
        in_specs=[scalars] * 4 + [memory] * (2 + len(crossed)) + [whole] * len(parameters) + [memory] * len(chained),
        out_specs=[memory] * 3,
        out_shape=shapes,
        scratch_shapes=[
            pltpu.VMEM((slots, width), BF16),
            pltpu.VMEM((slots, width), BF16),
            pltpu.VMEM((heads, slots, width), BF16),
            pltpu.VMEM((slots, width), BF16),
            pltpu.VMEM((slots, width), BF16),
            pltpu.VMEM((heads, slots, 2 * LANES), BF16),
            pltpu.VMEM((heads, slots, 2 * LANES), BF16),
            pltpu.VMEM((2, slots, slots), BF16),
            pltpu.VMEM((slots, width), BF16),
            pltpu.VMEM((slots, width), BF16),
            pltpu.VMEM((2, slots, width), BF16),
            pltpu.VMEM((slots, width), F32),
            pltpu.VMEM((slots, width), BF16),
            pltpu.SemaphoreType.DMA((2,)),
            pltpu.SemaphoreType.DMA((3,)),
        ],
        input_output_aliases=aliases,
        compiler_params=pltpu.CompilerParams(vmem_limit_bytes=44 * 1024 * 1024),
        cost_estimate=pl.CostEstimate(flops=flops, bytes_accessed=8 * slots * width * 2, transcendentals=slots * slots * heads),
        name=f"step_{step}",
    )(*operands, *(a for _, a in chained))


def pack(first_round, last_round, wanted, place, own):
    images, slots, width = own.shape
    count = wanted.shape[0]

    def source(i, pairs, spot):
        sent = ranks(pairs, count, spot[0] * images, images)
        return (sum(jnp.where(rank == i + first_round, image, 0) for image, rank in enumerate(sent)), 0, 0)

    def body(pairs, spot, x, out):
        out[...] = x[...]

    return pl.pallas_call(
        body,
        grid_spec=pltpu.PrefetchScalarGridSpec(
            num_scalar_prefetch=2,
            grid=(last_round - first_round,),
            in_specs=[pl.BlockSpec((pl.Squeezed(), slots, width), source)],
            out_specs=pl.BlockSpec((pl.Squeezed(), slots, width), lambda i, pairs, spot: (i, 0, 0)),
        ),
        out_shape=jax.ShapeDtypeStruct((last_round - first_round, slots, width), own.dtype),
        name=f"pack_{first_round}",
    )(wanted, place, own)


def add_kernel(entries, images, pairs, beside, partner, place, *refs):
    terms, (out, held, copies) = refs[1:-3], refs[-3:]
    count = pairs.shape[0]
    position = place[0]
    base = position * images
    other = across(position)
    next_to = position + 1 - 2 * (position % 2)
    paired = (other >= 0) & (other < place[1])
    targets = []
    for source, step in entries:
        if step == count:
            _, _, inside = arrange(partner, count, base, images)
            row, valid = (count - 1, paired & (inside == 0))
            listed = partner
        else:
            listed = (pairs, beside, partner)[source]
            theirs = (other * images, across(next_to) * images, base)[source]
            row, valid, _, _ = chosen(listed, count, theirs, images, step)
            if source == 2:
                valid = valid & paired
        targets.append(jnp.where(valid, listed[row, 1] - base, -1))
    slots = held.shape[1]
    tile = min(256, slots)
    for image in range(images):
        touched = sum((t == image).astype(jnp.int32) for t in targets) > 0

        @pl.when(touched)
        def _():
            pltpu.make_async_copy(out.at[image], held.at[image], copies.at[image]).start()

    for image in range(images):
        touched = sum((t == image).astype(jnp.int32) for t in targets) > 0

        @pl.when(touched)
        def _():
            pltpu.make_async_copy(out.at[image], held.at[image], copies.at[image]).wait()
            for term, target in zip(terms, targets):
                @pl.when(target == image)
                def _():
                    def one(index, carry):
                        rows = rows_of(index, tile)
                        held[image, rows, :] += term[rows, :].astype(F32)
                        return carry

                    lax.fori_loop(0, slots // tile, one, 0)

            pltpu.make_async_copy(held.at[image], out.at[image], copies.at[image]).start()

    for image in range(images):
        touched = sum((t == image).astype(jnp.int32) for t in targets) > 0

        @pl.when(touched)
        def _():
            pltpu.make_async_copy(held.at[image], out.at[image], copies.at[image]).wait()


def add_updates(groups, totals, pairs, beside, partner, place):
    images, slots, width = totals.shape
    entries = [entry for order, _ in groups for entry in order]
    buffers = [buffer for _, buffer in groups]
    scalars = pl.BlockSpec(memory_space=pltpu.SMEM)
    memory = pl.BlockSpec(memory_space=pl.ANY)

    def body(*refs):
        terms = [ref.at[i] for ref in refs[5 : 5 + len(buffers)] for i in range(ref.shape[0])]
        add_kernel(entries, images, *refs[:5], *terms, *refs[5 + len(buffers) :])

    return pl.pallas_call(
        body,
        in_specs=[scalars] * 4 + [memory] + [pl.BlockSpec(memory_space=pltpu.VMEM)] * len(buffers),
        out_specs=memory,
        out_shape=jax.ShapeDtypeStruct(totals.shape, F32),
        scratch_shapes=[pltpu.VMEM(totals.shape, F32), pltpu.SemaphoreType.DMA((images,))],
        input_output_aliases={4: 0},
        compiler_params=pltpu.CompilerParams(vmem_limit_bytes=24 * 1024 * 1024),
        cost_estimate=pl.CostEstimate(flops=1000, bytes_accessed=totals.size * 4, transcendentals=0),
        name=f"add_{len(entries)}",
    )(pairs, beside, partner, place, totals, *buffers)


def local(descriptors, key_counts, pair_list, w_qk, w_value, w_out, w_up, b_up, ln_gain, ln_bias, w_down, b_down):
    images, slots, width = descriptors.shape
    count = pair_list.shape[0]
    peers = lax.axis_size(AXES)
    position = lax.axis_index(AXES)
    on_chip = [(i, i + 1 - 2 * (i % 2)) for i in range(peers)]
    off_chip = [(i, i + 1) for i in range(1, peers - 1, 2)]
    off_chip = off_chip + [(j, i) for i, j in off_chip]
    place = jnp.stack([position, jnp.int32(peers)]).astype(jnp.int32)
    partner = lax.ppermute(pair_list, AXES, off_chip)
    beside_list = lax.ppermute(pair_list, AXES, on_chip)
    beside = lax.ppermute(descriptors, AXES, on_chip)
    parameters = (
        w_qk, w_value, w_out, w_up, b_up[None, :], ln_gain[None, :], ln_bias[None, :], w_down, b_down[None, :],
    )
    split = (images + 1) // 2
    crossed = []
    for first, last in ((0, split), (split, images)):
        crossed.append(lax.ppermute(pack(first, last, partner, place, descriptors), AXES, off_chip))
    given = (pair_list, partner, key_counts, place, descriptors, beside)
    groups = [(0, 1), (1, split + 1), (split + 1, count), (count, count + 1)]
    states = totals = None
    early, late = ([], [])
    for number, (first, last) in enumerate(groups):
        updates = None
        for step in range(first, last):
            needed = [] if step == 0 else (crossed[:1] if step <= split else crossed)
            states, totals, updates = take_step(
                step, (states, totals, updates), step - first, last - first, *given, needed, parameters
            )
        steps = range(first, last)
        if step == count:
            early.append(([(2, count)], updates))
            continue
        early.append(([(0, s) for s in steps], updates))
        final = number == 2
        (late if final else early).append(([(1, s) for s in steps], lax.ppermute(updates, AXES, on_chip)))
        if step > 0:
            (late if final else early).append(([(2, s) for s in steps], lax.ppermute(updates, AXES, off_chip)))
    totals = add_updates(early, totals, pair_list, beside_list, partner, place)
    totals = add_updates(late, totals, pair_list, beside_list, partner, place)
    return (states, totals)


def solution(mesh):
    in_specs = (P(AXES, None, None), P(), P(AXES, None)) + (P(),) * 9
    out_specs = (P(AXES, None, None, None), P(AXES, None, None))
    return jax.shard_map(local, mesh=mesh, in_specs=in_specs, out_specs=out_specs, check_vma=False)
```

```python
import jax
import jax.numpy as jnp
from jax import lax
from jax.experimental import pallas as pl
from jax.experimental.pallas import tpu as pltpu
from jax.sharding import PartitionSpec as P

HEAD_DIM = 64
LANES = 128
F32 = jnp.float32
BF16 = jnp.bfloat16
LOG2E = 1.4426950408889634
AXES = ("photo", "worker")
EXPONENT_BOUND = 96.0
VALUE_BOUND = 2.0**18


def dot(a, b):
    return jnp.dot(a, b, preferred_element_type=F32)


def dot_rows(a, b):
    return lax.dot_general(a, b, (((1,), (1,)), ((), ())), preferred_element_type=F32)


def dot_columns(a, b):
    return lax.dot_general(a, b, (((0,), (0,)), ((), ())), preferred_element_type=F32)


def rows_of(index, size):
    return pl.ds(pl.multiple_of(index * size, size), size)


def refine(start, message, w_out, w_up, b_up, ln_gain, ln_bias, w_down, b_down):
    width = start.shape[1]
    sent = dot(message, w_out[...]).astype(BF16)
    hidden = dot(start, w_up[:width, :]) + dot(sent, w_up[width:, :]) + b_up[...]
    center = jnp.mean(hidden, axis=-1, keepdims=True)
    shifted = hidden - center
    spread = jnp.mean(shifted * shifted, axis=-1, keepdims=True)
    normed = shifted * lax.rsqrt(spread + 1e-05) * ln_gain[...] + ln_bias[...]
    act = (0.5 * normed * (1.0 + lax.erf(normed * (0.5**0.5)))).astype(BF16)
    return dot(act, w_down[...]) + b_down[...]


def across(position):
    return jnp.where(position % 2 == 1, position + 1, position - 1)


def arrange(pairs, count, base, images):
    hits = [(pairs[s, 1] >= base) & (pairs[s, 1] < base + images) for s in range(count)]
    hits = [h.astype(jnp.int32) for h in hits]
    inside = count - sum(hits)
    places, seen_in, seen_out = ([], jnp.int32(0), jnp.int32(0))
    for hit in hits:
        places.append(jnp.where(hit == 1, inside + seen_out, seen_in))
        seen_out = seen_out + hit
        seen_in = seen_in + 1 - hit
    return (hits, places, inside)


def chosen(arranged, count, step):
    hits, places, inside = arranged
    turn = jnp.where(step == 0, 0, step - 1 + jnp.minimum(inside, 1))
    exists = jnp.where(step == 0, inside > 0, turn < count)
    row = sum(jnp.where(p == turn, s, 0) for s, p in enumerate(places))
    hit = sum(jnp.where(p == turn, h, 0) for h, p in zip(hits, places))
    return (row, exists, hit == 1)


def ranks(pairs, count, base, images):
    firsts = []
    for image in range(images):
        first = jnp.int32(count + image)
        for slot in reversed(range(count)):
            first = jnp.where(pairs[slot, 1] == base + image, slot, first)
        firsts.append(first)
    return [sum((other < first).astype(jnp.int32) for other in firsts) for first in firsts]


def pick(values, index):
    return sum(jnp.where(index == i, v, 0) for i, v in enumerate(values))


def in_place(index, low, length):
    return (index >= low) & (index < low + length)


def fetch_scalars(sources, targets, semaphores):
    moves = [pltpu.make_async_copy(s, t, semaphores.at[i]) for i, (s, t) in enumerate(zip(sources, targets))]
    for move in moves:
        move.start()
    for move in moves:
        move.wait()


def group_kernel(first_step, last_step, images, peers, sizes, refs):
    refs = list(refs)
    take = lambda n: [refs.pop(0) for _ in range(n)]
    hbm_pairs, hbm_partner, hbm_counts, own, beside = take(5)
    crossed = take(sizes["crossed"])
    parameters = take(9)
    states, totals = take(2)
    outputs = take(sizes["outputs"])
    pairs, partner, counts = take(3)
    held_parameters = take(9)
    (
        x_first, x_second, q_first, k_first, k_second, v_first, v_second,
        weights_even, weights_odd, sum_first, sum_second, m_first, m_second,
        new_states, new_delta, new_update, loads, sends, others,
    ) = refs
    w_qk, w_value, w_out, w_up, b_up, ln_gain, ln_bias, w_down, b_down = held_parameters
    slots, width = x_first.shape[1:]
    heads = width // HEAD_DIM
    count = pairs.shape[0]
    steps = last_step - first_step
    moves = [pltpu.make_async_copy(s, t, others.at[i]) for i, (s, t) in enumerate(zip(parameters, held_parameters))]
    fetch_scalars((hbm_pairs, hbm_partner, hbm_counts), (pairs, partner, counts), others.at[pl.ds(9, 3)])
    for move in moves:
        move.start()
    position = lax.axis_index(AXES)
    base = position * images
    beside_base = (position + 1 - 2 * (position % 2)) * images
    other = across(position)
    other_base = other * images
    paired = (other >= 0) & (other < peers)
    arranged = arrange(pairs, count, other_base, images)
    sent = ranks(pairs, count, other_base, images)
    _, _, their_inside = arrange(partner, count, base, images)
    can_repeat = last_step > count

    def describe(step):
        row, exists, _ = chosen(arranged, count, step)
        first = base + jnp.clip(pairs[row, 0] - base, 0, images - 1)
        second = pairs[row, 1]
        if can_repeat:
            again = step > count
            exists = jnp.where(again, paired & (their_inside == 0), exists)
            first = jnp.where(again, other_base + jnp.clip(partner[count - 1, 0] - other_base, 0, images - 1), first)
            second = jnp.where(again, partner[count - 1, 1], second)
        return (row, exists, first, second)

    def load(image, held, semaphore):
        for source, low in ((own, base), (beside, beside_base)):
            @pl.when(in_place(image, low, images))
            def _():
                pltpu.make_async_copy(source.at[jnp.clip(image - low, 0, images - 1)], held, semaphore).start()

        rank = jnp.where(in_place(image, other_base, images), pick(sent, image - other_base), -1)
        offset = 0
        for source in crossed:
            length = source.shape[0]

            @pl.when(in_place(rank, offset, length))
            def _():
                pltpu.make_async_copy(source.at[jnp.clip(rank - offset, 0, length - 1)], held, semaphore).start()

            offset += length

    def fetch(step, turn):
        _, exists, first, second = describe(step)

        @pl.when(exists)
        def _():
            load(first, x_first.at[turn], loads.at[turn, 0])
            load(second, x_second.at[turn], loads.at[turn, 1])

    def attention(first, second, one, two):
        count_first = counts[first]
        count_second = counts[second]
        lane = lax.broadcasted_iota(jnp.int32, (slots, LANES), 1)
        line = lax.broadcasted_iota(jnp.int32, (slots, LANES), 0)
        halves = (lane < HEAD_DIM, lane >= HEAD_DIM)
        query = dot(one[...], w_qk[...])
        key = dot(two[...], w_qk[...])
        k_first[...] = query.astype(BF16)
        k_second[...] = key.astype(BF16)
        scaled = query * (HEAD_DIM**-0.5 * LOG2E)
        value_one = dot(one[...], w_value[...])
        value_two = dot(two[...], w_value[...])
        empty = jnp.zeros((slots, LANES), BF16)
        for head in range(heads):
            start = head * HEAD_DIM // LANES * LANES
            columns = slice(start, start + LANES)
            half = halves[head % 2]
            for gap in range(0, width, LANES):
                if gap != start:
                    q_first[head, :, gap : gap + LANES] = empty
            q_first[head, :, columns] = jnp.where(half, scaled[:, columns], 0.0).astype(BF16)
            for value, held, limit in ((value_one, v_first, count_first), (value_two, v_second, count_second)):
                valid = half & (line < limit)
                held[head, :, :LANES] = jnp.where(valid, value[:, columns], 0.0).astype(BF16)
                held[head, :, LANES:] = jnp.where(valid, 1.0, 0.0).astype(BF16)
        query_norm = jnp.max(jnp.sum(scaled * scaled, axis=-1, keepdims=True))
        key_norm = jnp.max(jnp.sum(key * key, axis=-1, keepdims=True))
        largest = jnp.maximum(jnp.max(jnp.abs(value_one)), jnp.max(jnp.abs(value_two)))
        in_range = (query_norm * key_norm <= EXPONENT_BOUND**2) & (largest <= VALUE_BOUND)

        @pl.when(in_range)
        def _():
            tile = min(256, slots)
            weights = (weights_even, weights_odd)

            def score(head):
                for start in range(0, slots, tile):
                    scores = dot_rows(q_first[head], k_second[start : start + tile, :])
                    weights[head % 2][:, start : start + tile] = jnp.exp2(scores).astype(BF16)

            def mix(head):
                group = head // 2
                part_first = dot(weights[head % 2][...], v_second[head])
                part_second = dot_columns(weights[head % 2][...], v_first[head])
                if head % 2 == 0:
                    sum_first[group] = part_first
                    sum_second[group] = part_second
                else:
                    sum_first[group] += part_first
                    sum_second[group] += part_second

            score(0)
            for head in range(1, heads):
                score(head)
                mix(head - 1)
            mix(heads - 1)
            for group in range(heads // 2):
                columns = slice(group * LANES, (group + 1) * LANES)
                for total, message in ((sum_first, m_first), (sum_second, m_second)):
                    message[:, columns] = (total[group, :, :LANES] / total[group, :, LANES:]).astype(BF16)

        @pl.when(jnp.logical_not(in_range))
        def _():
            tile = min(64, slots)
            spot = lax.broadcasted_iota(jnp.int32, (tile, slots), 1)
            column = lax.broadcasted_iota(jnp.int32, (tile, width), 1)
            for queries, keys, held, message, limit in (
                (k_first, k_second, v_second, m_first, count_second),
                (k_second, k_first, v_first, m_second, count_first),
            ):
                def attend(index, carry):
                    rows = rows_of(index, tile)
                    query_rows = queries[rows, :].astype(F32)
                    for start in range(0, heads, 2):
                        columns = slice(start * HEAD_DIM, start * HEAD_DIM + LANES)

                        def one_head(head, total):
                            query = jnp.where(column // HEAD_DIM == head, query_rows, 0.0).astype(BF16)
                            scores = dot_rows(query, keys[...]) * HEAD_DIM**-0.5
                            scores = jnp.where(spot < limit, scores, -jnp.inf)
                            scores = jnp.exp(scores - jnp.max(scores, axis=-1, keepdims=True))
                            scores = scores / jnp.sum(scores, axis=-1, keepdims=True)
                            return total + dot(scores.astype(BF16), held[head])

                        total = lax.fori_loop(start, start + 2, one_head, jnp.zeros((tile, 2 * LANES), F32))
                        message[rows, columns] = total[:, :LANES].astype(BF16)
                    return carry

                lax.fori_loop(0, slots // tile, attend, 0)

    def change_of(start, message):
        return refine(start[...], message[...], w_out, w_up, b_up, ln_gain, ln_bias, w_down, b_down)

    def one_step(turn, carry):
        step = first_step + turn
        now = turn % 2
        row, exists, first, second = describe(step)
        one, two = (x_first.at[now], x_second.at[now])

        @pl.when(exists)
        def _():
            pltpu.make_async_copy(own.at[0], one, loads.at[now, 0]).wait()
            pltpu.make_async_copy(own.at[0], two, loads.at[now, 1]).wait()

        if steps > 1:
            @pl.when(turn + 1 < steps)
            def _():
                fetch(step + 1, (turn + 1) % 2)

        @pl.when(turn == 0)
        def _():
            for move in moves:
                move.wait()

        def for_update(start):
            for slot, (output, low, high) in enumerate(zip(outputs, sizes["lows"], sizes["highs"])):
                @pl.when(in_place(step, low, high - low))
                def _():
                    move = pltpu.make_async_copy(
                        new_update, output.at[jnp.clip(step - low + sizes["skips"][slot], 0, output.shape[0] - 1)], sends.at[slot]
                    )
                    move.start() if start else move.wait()

        @pl.when(exists)
        def _():
            attention(first, second, one, two)
            change = change_of(two, m_second)
            new_update[...] = change.astype(BF16)
            new_states[1] = (two[...].astype(F32) + change).astype(BF16)
            for_update(True)

            @pl.when(step <= count)
            def _():
                change = change_of(one, m_first)
                new_delta[...] = change
                new_states[0] = (one[...].astype(F32) + change).astype(BF16)
                send_states = pltpu.make_async_copy(new_states, states.at[row], sends.at[2])
                send_delta = pltpu.make_async_copy(new_delta, totals.at[jnp.clip(first - base, 0, images - 1)], sends.at[3])
                send_states.start()
                send_delta.start()
                send_states.wait()
                send_delta.wait()

            for_update(False)

        return carry

    fetch(first_step, 0)
    lax.fori_loop(0, steps, one_step, 0)


def take_steps(first_step, last_step, held, outputs, given, crossed, parameters, extra):
    pairs, partner, counts, own, beside = given
    images, slots, width = own.shape
    count = pairs.shape[0]
    heads = width // HEAD_DIM
    peers = lax.axis_size(AXES)
    memory = pl.BlockSpec(memory_space=pltpu.HBM)
    hidden = parameters[3].shape[1]
    flops = 2 * slots * (4 * width * width + 6 * slots * width + 2 * (width * width + 2 * width * hidden + hidden * width))
    operands = (pairs, partner, counts, own, beside, *crossed, *parameters)
    fixed = len(operands)
    chained = [(i, a) for i, a in enumerate((*held, *(o[0] for o in outputs))) if a is not None]
    aliases = {fixed + n: i for n, (i, _) in enumerate(chained)}
    passed = fixed + len(chained) + len(extra)
    shapes = [
        jax.ShapeDtypeStruct((count, 2, slots, width), BF16),
        jax.ShapeDtypeStruct((images, slots, width), F32),
    ] + [jax.ShapeDtypeStruct((o[1], slots, width), BF16) for o in outputs]
    sizes = {
        "crossed": len(crossed),
        "outputs": len(outputs),
        "skips": [o[2] for o in outputs],
        "lows": [o[3] for o in outputs],
        "highs": [o[4] for o in outputs],
    }

    def body(*refs):
        group_kernel(first_step, last_step, images, peers, sizes, refs[:fixed] + refs[passed:])

    return pl.pallas_call(
        body,
        in_specs=[memory] * passed,
        out_specs=[memory] * len(shapes),
        out_shape=shapes,
        scratch_shapes=[
            pltpu.SMEM(pairs.shape, jnp.int32),
            pltpu.SMEM(partner.shape, jnp.int32),
            pltpu.SMEM(counts.shape, jnp.int32),
            *(pltpu.VMEM(p.shape, p.dtype) for p in parameters),
            pltpu.VMEM((2, slots, width), BF16),
            pltpu.VMEM((2, slots, width), BF16),
            pltpu.VMEM((heads, slots, width), BF16),
            pltpu.VMEM((slots, width), BF16),
            pltpu.VMEM((slots, width), BF16),
            pltpu.VMEM((heads, slots, 2 * LANES), BF16),
            pltpu.VMEM((heads, slots, 2 * LANES), BF16),
            pltpu.VMEM((slots, slots), BF16),
            pltpu.VMEM((slots, slots), BF16),
            pltpu.VMEM((heads // 2, slots, 2 * LANES), F32),
            pltpu.VMEM((heads // 2, slots, 2 * LANES), F32),
            pltpu.VMEM((slots, width), BF16),
            pltpu.VMEM((slots, width), BF16),
            pltpu.VMEM((2, slots, width), BF16),
            pltpu.VMEM((slots, width), F32),
            pltpu.VMEM((slots, width), BF16),
            pltpu.SemaphoreType.DMA((2, 2)),
            pltpu.SemaphoreType.DMA((4,)),
            pltpu.SemaphoreType.DMA((12,)),
        ],
        input_output_aliases=aliases,
        compiler_params=pltpu.CompilerParams(vmem_limit_bytes=56 * 1024 * 1024),
        cost_estimate=pl.CostEstimate(
            flops=flops * (min(last_step, count) - first_step), bytes_accessed=8 * slots * width * 2, transcendentals=slots * slots * heads
        ),
        name=f"steps_{first_step}",
    )(*operands, *(a for _, a in chained), *extra)


def pack(partner, own, split):
    images, slots, width = own.shape
    count = partner.shape[0]
    memory = pl.BlockSpec(memory_space=pltpu.HBM)

    def body(hbm_pairs, source, early, late, pairs, buffer, semaphores):
        fetch_scalars((hbm_pairs,), (pairs,), semaphores)
        base = lax.axis_index(AXES) * images
        sent = ranks(pairs, count, base, images)
        loads, stores = ([], [])
        for turn in range(images):
            image = sum(jnp.where(rank == turn, i, 0) for i, rank in enumerate(sent))
            loads.append(pltpu.make_async_copy(source.at[image], buffer.at[turn], semaphores.at[1 + turn]))
            target = early.at[turn] if turn < split else late.at[turn - split]
            stores.append(pltpu.make_async_copy(buffer.at[turn], target, semaphores.at[1 + images + turn]))
        for move in loads:
            move.start()
        for one, two in zip(loads, stores):
            one.wait()
            two.start()
        for move in stores:
            move.wait()

    return pl.pallas_call(
        body,
        in_specs=[memory] * 2,
        out_specs=[memory] * 2,
        out_shape=[jax.ShapeDtypeStruct((n, slots, width), own.dtype) for n in (split, images - split)],
        scratch_shapes=[
            pltpu.SMEM(partner.shape, jnp.int32),
            pltpu.VMEM((images, slots, width), own.dtype),
            pltpu.SemaphoreType.DMA((1 + 2 * images,)),
        ],
        name="pack",
    )(partner, own)


def add_kernel(entries, images, peers, refs):
    hbm_lists, _, terms = refs[:3], refs[3], refs[4 : 4 + len(entries)]
    out, pairs, beside, partner, held, buffer, copies, loads, scalars = refs[4 + len(entries) :]
    fetch_scalars(hbm_lists, (pairs, beside, partner), scalars)
    count = pairs.shape[0]
    position = lax.axis_index(AXES)
    base = position * images
    other = across(position)
    next_to = position + 1 - 2 * (position % 2)
    paired = (other >= 0) & (other < peers)
    lists = (pairs, beside, partner)
    bases = (other * images, across(next_to) * images, base)
    arranged = [arrange(p, count, b, images) for p, b in zip(lists, bases)]
    targets = []
    for source, step in entries:
        if step > count:
            row, valid = (count - 1, paired & (arranged[2][2] == 0))
        else:
            row, valid, _ = chosen(arranged[source], count, jnp.int32(step))
            if source == 2:
                valid = valid & paired
        target = lists[source][row, 1] - base
        targets.append(jnp.where(valid & in_place(target, 0, images), target, -1))
    slots = held.shape[1]
    tile = min(256, slots)
    touched = [sum((t == image).astype(jnp.int32) for t in targets) > 0 for image in range(images)]
    for image in range(images):
        @pl.when(touched[image])
        def _():
            pltpu.make_async_copy(out.at[image], held.at[image], copies.at[image]).start()

    for number, (term, target) in enumerate(zip(terms, targets)):
        @pl.when(target >= 0)
        def _():
            pltpu.make_async_copy(term, buffer.at[number], loads.at[number]).start()

    for image in range(images):
        @pl.when(touched[image])
        def _():
            pltpu.make_async_copy(out.at[image], held.at[image], copies.at[image]).wait()

            def one_term(number, carry):
                @pl.when(pick(targets, number) == image)
                def _():
                    pltpu.make_async_copy(terms[0], buffer.at[number], loads.at[number]).wait()

                    def one(index, inner):
                        rows = rows_of(index, tile)
                        held[image, rows, :] += buffer[number, rows, :].astype(F32)
                        return inner

                    lax.fori_loop(0, slots // tile, one, 0)

                return carry

            lax.fori_loop(0, len(entries), one_term, 0)
            pltpu.make_async_copy(held.at[image], out.at[image], copies.at[image]).start()

    for image in range(images):
        @pl.when(touched[image])
        def _():
            pltpu.make_async_copy(held.at[image], out.at[image], copies.at[image]).wait()


def add_updates(groups, totals, pairs, beside, partner):
    images, slots, width = totals.shape
    entries = [entry for order, _ in groups for entry in order]
    buffers = [buffer for _, buffer in groups]
    memory = pl.BlockSpec(memory_space=pltpu.HBM)
    peers = lax.axis_size(AXES)
    split = 4 + len(buffers)

    def body(*refs):
        terms = [ref.at[i] for ref in refs[4:split] for i in range(ref.shape[0])]
        add_kernel(entries, images, peers, (*refs[:4], *terms, *refs[split:]))

    return pl.pallas_call(
        body,
        in_specs=[memory] * split,
        out_specs=memory,
        out_shape=jax.ShapeDtypeStruct(totals.shape, F32),
        scratch_shapes=[
            *(pltpu.SMEM(p.shape, jnp.int32) for p in (pairs, beside, partner)),
            pltpu.VMEM(totals.shape, F32),
            pltpu.VMEM((len(entries), slots, width), BF16),
            pltpu.SemaphoreType.DMA((images,)),
            pltpu.SemaphoreType.DMA((len(entries),)),
            pltpu.SemaphoreType.DMA((3,)),
        ],
        input_output_aliases={3: 0},
        compiler_params=pltpu.CompilerParams(vmem_limit_bytes=24 * 1024 * 1024),
        cost_estimate=pl.CostEstimate(flops=1000, bytes_accessed=totals.size * 4, transcendentals=0),
        name=f"add_{len(entries)}",
    )(pairs, beside, partner, totals, *buffers)


def local(descriptors, key_counts, pair_list, w_qk, w_value, w_out, w_up, b_up, ln_gain, ln_bias, w_down, b_down):
    images, slots, width = descriptors.shape
    count = pair_list.shape[0]
    peers = lax.axis_size(AXES)
    on_chip = [(i, i + 1 - 2 * (i % 2)) for i in range(peers)]
    off_chip = [(i, i + 1) for i in range(1, peers - 1, 2)]
    off_chip = off_chip + [(j, i) for i, j in off_chip]
    partner = lax.ppermute(pair_list, AXES, off_chip)
    beside_list = lax.ppermute(pair_list, AXES, on_chip)
    beside = lax.ppermute(descriptors, AXES, on_chip)
    parameters = (
        w_qk, w_value, w_out, w_up, b_up[None, :], ln_gain[None, :], ln_bias[None, :], w_down, b_down[None, :],
    )
    split = (images + 1) // 2
    crossed = [lax.ppermute(x, AXES, off_chip) for x in pack(partner, descriptors, split)]
    given = (pair_list, partner, key_counts, descriptors, beside)
    middle = split + 1
    states, totals, near = take_steps(
        0, 1, (None, None), [(None, middle, 0, 0, 1)], given, [], parameters, [beside_list]
    )
    states, totals, near, far = take_steps(
        1, middle, (states, totals), [(near, middle, 1, 1, middle), (None, split, 0, 1, middle)],
        given, crossed[:1], parameters, [],
    )
    near_back = lax.ppermute(near, AXES, on_chip)
    far_back = lax.ppermute(far, AXES, off_chip)
    states, totals, last, repeat = take_steps(
        middle, count + 2, (states, totals), [(None, count - middle, 0, middle, count), (None, 1, 0, count + 1, count + 2)],
        given, crossed, parameters, [],
    )
    last_near = lax.ppermute(last, AXES, on_chip)
    last_far = lax.ppermute(last, AXES, off_chip)
    early = [
        ([(0, s) for s in range(middle)], near),
        ([(0, s) for s in range(middle, count)], last),
        ([(2, count + 1)], repeat),
        ([(1, s) for s in range(middle)], near_back),
        ([(2, s) for s in range(1, middle)], far_back),
    ]
    late = [
        ([(1, s) for s in range(middle, count)], last_near),
        ([(2, s) for s in range(middle, count)], last_far),
    ]
    totals = add_updates(early, totals, pair_list, beside_list, partner)
    totals = add_updates(late, totals, pair_list, beside_list, partner)
    return (states, totals)


def solution(mesh):
    in_specs = (P(AXES, None, None), P(), P(AXES, None)) + (P(),) * 9
    out_specs = (P(AXES, None, None, None), P(AXES, None, None))
    return jax.shard_map(local, mesh=mesh, in_specs=in_specs, out_specs=out_specs, check_vma=False)
```

```python
import jax
import jax.numpy as jnp
from jax import lax
from jax.experimental import pallas as pl
from jax.experimental.pallas import tpu as pltpu
from jax.sharding import PartitionSpec as P

HEAD_DIM = 64
LANES = 128
F32 = jnp.float32
BF16 = jnp.bfloat16
LOG2E = 1.4426950408889634
AXES = ("photo", "worker")
EXPONENT_BOUND = 96.0
VALUE_BOUND = 2.0**18


def dot(a, b):
    return jnp.dot(a, b, preferred_element_type=F32)


def dot_rows(a, b):
    return lax.dot_general(a, b, (((1,), (1,)), ((), ())), preferred_element_type=F32)


def dot_columns(a, b):
    return lax.dot_general(a, b, (((0,), (0,)), ((), ())), preferred_element_type=F32)


def rows_of(index, size):
    return pl.ds(pl.multiple_of(index * size, size), size)


def refine(start, message, w_out, w_up, b_up, ln_gain, ln_bias, w_down, b_down):
    width = start.shape[1]
    sent = dot(message, w_out[...]).astype(BF16)
    hidden = dot(start, w_up[:width, :]) + dot(sent, w_up[width:, :]) + b_up[...]
    center = jnp.mean(hidden, axis=-1, keepdims=True)
    shifted = hidden - center
    spread = jnp.mean(shifted * shifted, axis=-1, keepdims=True)
    normed = shifted * lax.rsqrt(spread + 1e-05) * ln_gain[...] + ln_bias[...]
    act = (0.5 * normed * (1.0 + lax.erf(normed * (0.5**0.5)))).astype(BF16)
    return dot(act, w_down[...]) + b_down[...]


def across(position):
    return jnp.where(position % 2 == 1, position + 1, position - 1)


def arrange(pairs, count, base, images):
    hits = [(pairs[s, 1] >= base) & (pairs[s, 1] < base + images) for s in range(count)]
    hits = [h.astype(jnp.int32) for h in hits]
    inside = count - sum(hits)
    places, seen_in, seen_out = ([], jnp.int32(0), jnp.int32(0))
    for hit in hits:
        places.append(jnp.where(hit == 1, inside + seen_out, seen_in))
        seen_out = seen_out + hit
        seen_in = seen_in + 1 - hit
    return (hits, places, inside)


def chosen(arranged, count, step):
    hits, places, inside = arranged
    turn = jnp.where(step == 0, 0, step - 1 + jnp.minimum(inside, 1))
    exists = jnp.where(step == 0, inside > 0, turn < count)
    row = sum(jnp.where(p == turn, s, 0) for s, p in enumerate(places))
    hit = sum(jnp.where(p == turn, h, 0) for h, p in zip(hits, places))
    return (row, exists, hit == 1)


def ranks(pairs, count, base, images):
    firsts = []
    for image in range(images):
        first = jnp.int32(count + image)
        for slot in reversed(range(count)):
            first = jnp.where(pairs[slot, 1] == base + image, slot, first)
        firsts.append(first)
    return [sum((other < first).astype(jnp.int32) for other in firsts) for first in firsts]


def pick(values, index):
    return sum(jnp.where(index == i, v, 0) for i, v in enumerate(values))


def in_place(index, low, length):
    return (index >= low) & (index < low + length)


def fetch_scalars(sources, targets, semaphores):
    moves = [pltpu.make_async_copy(s, t, semaphores.at[i]) for i, (s, t) in enumerate(zip(sources, targets))]
    for move in moves:
        move.start()
    for move in moves:
        move.wait()


def group_kernel(first_step, last_step, images, peers, sizes, refs):
    refs = list(refs)
    take = lambda n: [refs.pop(0) for _ in range(n)]
    hbm_pairs, hbm_partner, hbm_counts, own, beside = take(5)
    crossed = take(sizes["crossed"])
    parameters = take(9)
    states, totals = take(2)
    outputs = take(sizes["outputs"])
    pairs, partner, counts = take(3)
    held_parameters = take(9)
    (
        x_both, q_first, k_both, v_both,
        weights_even, weights_odd, sum_first, sum_second, m_first, m_second,
        new_states, new_delta, new_update, loads, sends, others,
    ) = refs
    w_qk, w_value, w_out, w_up, b_up, ln_gain, ln_bias, w_down, b_down = held_parameters
    slots, width = x_both.shape[2:]
    k_second, v_first, v_second = (k_both.at[1], v_both.at[0], v_both.at[1])
    heads = width // HEAD_DIM
    count = pairs.shape[0]
    steps = last_step - first_step
    moves = [pltpu.make_async_copy(s, t, others.at[i]) for i, (s, t) in enumerate(zip(parameters, held_parameters))]
    for move in moves:
        move.start()
    fetch_scalars((hbm_pairs, hbm_partner, hbm_counts), (pairs, partner, counts), others.at[pl.ds(9, 3)])
    position = lax.axis_index(AXES)
    base = position * images
    beside_base = (position + 1 - 2 * (position % 2)) * images
    other = across(position)
    other_base = other * images
    paired = (other >= 0) & (other < peers)
    arranged = arrange(pairs, count, other_base, images)
    sent = ranks(pairs, count, other_base, images)
    _, _, their_inside = arrange(partner, count, base, images)
    can_repeat = last_step > count

    def describe(step):
        row, exists, _ = chosen(arranged, count, step)
        first = base + jnp.clip(pairs[row, 0] - base, 0, images - 1)
        second = pairs[row, 1]
        if can_repeat:
            again = step > count
            exists = jnp.where(again, paired & (their_inside == 0), exists)
            first = jnp.where(again, other_base + jnp.clip(partner[count - 1, 0] - other_base, 0, images - 1), first)
            second = jnp.where(again, partner[count - 1, 1], second)
        return (row, exists, first, second)

    def load(image, held, semaphore):
        for source, low in ((own, base), (beside, beside_base)):
            @pl.when(in_place(image, low, images))
            def _():
                pltpu.make_async_copy(source.at[jnp.clip(image - low, 0, images - 1)], held, semaphore).start()

        rank = jnp.where(in_place(image, other_base, images), pick(sent, image - other_base), -1)
        offset = 0
        for source in crossed:
            length = source.shape[0]

            @pl.when(in_place(rank, offset, length))
            def _():
                pltpu.make_async_copy(source.at[jnp.clip(rank - offset, 0, length - 1)], held, semaphore).start()

            offset += length

    def fetch(step, turn):
        _, exists, first, second = describe(step)

        @pl.when(exists)
        def _():
            load(first, x_both.at[turn, 0], loads.at[turn, 0])
            load(second, x_both.at[turn, 1], loads.at[turn, 1])

    def refined(start, message):
        return refine(start, message, w_out, w_up, b_up, ln_gain, ln_bias, w_down, b_down)

    def unshifted(first, second, one, two, now):
        count_first = counts[first]
        count_second = counts[second]
        lane = lax.broadcasted_iota(jnp.int32, (slots, LANES), 1)
        line = lax.broadcasted_iota(jnp.int32, (slots, LANES), 0)
        halves = (lane < HEAD_DIM, lane >= HEAD_DIM)
        scaled = dot(one[...], w_qk[...]) * (HEAD_DIM**-0.5 * LOG2E)
        key = dot(two[...], w_qk[...])
        k_second[...] = key.astype(BF16)
        value_one = dot(one[...], w_value[...])
        value_two = dot(two[...], w_value[...])
        empty = jnp.zeros((slots, LANES), BF16)
        for head in range(heads):
            start = head * HEAD_DIM // LANES * LANES
            columns = slice(start, start + LANES)
            half = halves[head % 2]
            for gap in range(0, width, LANES):
                if gap != start:
                    q_first[head, :, gap : gap + LANES] = empty
            q_first[head, :, columns] = jnp.where(half, scaled[:, columns], 0.0).astype(BF16)
            for value, held, limit in ((value_one, v_first, count_first), (value_two, v_second, count_second)):
                valid = half & (line < limit)
                held[head, :, :LANES] = jnp.where(valid, value[:, columns], 0.0).astype(BF16)
                held[head, :, LANES:] = jnp.where(valid, 1.0, 0.0).astype(BF16)
        query_norm = jnp.max(jnp.sum(scaled * scaled, axis=-1, keepdims=True))
        key_norm = jnp.max(jnp.sum(key * key, axis=-1, keepdims=True))
        largest = jnp.max(jnp.maximum(jnp.abs(value_one), jnp.abs(value_two)))
        tile = min(256, slots)
        weights = (weights_even, weights_odd)

        def score(head):
            for start in range(0, slots, tile):
                scores = dot_rows(q_first[head], k_second[start : start + tile, :])
                weights[head % 2][:, start : start + tile] = jnp.exp2(scores).astype(BF16)

        def mix(head):
            group = head // 2
            part_first = dot(weights[head % 2][...], v_second[head])
            part_second = dot_columns(weights[head % 2][...], v_first[head])
            if head % 2 == 0:
                sum_first[group] = part_first
                sum_second[group] = part_second
            else:
                sum_first[group] += part_first
                sum_second[group] += part_second

        score(0)
        for head in range(1, heads):
            score(head)
            mix(head - 1)
        mix(heads - 1)
        for group in range(heads // 2):
            columns = slice(group * LANES, (group + 1) * LANES)
            for total, message in ((sum_first, m_first), (sum_second, m_second)):
                message[:, columns] = (total[group, :, :LANES] / total[group, :, LANES:]).astype(BF16)
        here = two[...]
        change = refined(here, m_second[...])
        new_update[now] = change.astype(BF16)
        new_states[now, 1] = (here.astype(F32) + change).astype(BF16)
        here = one[...]
        change = refined(here, m_first[...])
        new_delta[now] = change
        new_states[now, 0] = (here.astype(F32) + change).astype(BF16)
        return (query_norm * key_norm <= EXPONENT_BOUND**2) & (largest <= VALUE_BOUND)

    def shifted(first, second, now):
        tile = min(16, slots)
        spot = lax.broadcasted_iota(jnp.int32, (tile, slots), 1)
        column = lax.broadcasted_iota(jnp.int32, (tile, width), 1)

        def fill(index, carry):
            rows = rows_of(index, tile)
            k_both[0, rows, :] = dot(x_both[now, 0, rows, :], w_qk[...]).astype(BF16)
            return carry

        lax.fori_loop(0, slots // tile, fill, 0)

        def attend(index, carry):
            side = index % 2
            rows = rows_of(index // 2, tile)
            limit = jnp.where(side == 0, counts[second], counts[first])
            query_rows = k_both[side, rows, :].astype(F32)

            def one_head(head, parts):
                query = jnp.where(column // HEAD_DIM == head, query_rows, 0.0).astype(BF16)
                scores = dot_rows(query, k_both[1 - side]) * HEAD_DIM**-0.5
                scores = jnp.where(spot < limit, scores, -jnp.inf)
                scores = jnp.exp(scores - jnp.max(scores, axis=-1, keepdims=True))
                scores = scores / jnp.sum(scores, axis=-1, keepdims=True)
                part = dot(scores.astype(BF16), v_both[1 - side, head, :, :LANES])
                return tuple(p + jnp.where(head // 2 == i, part, 0.0) for i, p in enumerate(parts))

            nothing = jnp.zeros((tile, LANES), F32)
            parts = lax.fori_loop(0, heads, one_head, (nothing,) * (heads // 2))
            here = x_both[now, side, rows, :]
            change = refined(here, jnp.concatenate(parts, axis=-1).astype(BF16))
            new_states[now, side, rows, :] = (here.astype(F32) + change).astype(BF16)

            @pl.when(side == 1)
            def _():
                new_update[now, rows, :] = change.astype(BF16)

            @pl.when(side == 0)
            def _():
                new_delta[now, rows, :] = change

            return carry

        lax.fori_loop(0, 2 * (slots // tile), attend, 0)

    def deliver(step, now, begin):
        row, exists, first, _ = describe(step)

        @pl.when(exists)
        def _():
            for slot, (output, low, high) in enumerate(zip(outputs, sizes["lows"], sizes["highs"])):
                @pl.when(in_place(step, low, high - low))
                def _():
                    place = jnp.clip(step - low + sizes["skips"][slot], 0, output.shape[0] - 1)
                    move = pltpu.make_async_copy(new_update.at[now], output.at[place], sends.at[now, slot])
                    move.start() if begin else move.wait()

            @pl.when(step <= count)
            def _():
                place = jnp.clip(first - base, 0, images - 1)
                for move in (
                    pltpu.make_async_copy(new_states.at[now], states.at[row], sends.at[now, 2]),
                    pltpu.make_async_copy(new_delta.at[now], totals.at[place], sends.at[now, 3]),
                ):
                    move.start() if begin else move.wait()

    def one_step(turn, carry):
        step = first_step + turn
        now = turn % 2
        _, exists, first, second = describe(step)
        one, two = (x_both.at[now, 0], x_both.at[now, 1])

        @pl.when(exists)
        def _():
            pltpu.make_async_copy(own.at[0], one, loads.at[now, 0]).wait()
            pltpu.make_async_copy(own.at[0], two, loads.at[now, 1]).wait()

        if steps > 1:
            @pl.when(turn + 1 < steps)
            def _():
                fetch(step + 1, (turn + 1) % 2)

        @pl.when(turn == 0)
        def _():
            for move in moves:
                move.wait()

        @pl.when(exists)
        def _():
            in_range = unshifted(first, second, one, two, now)

            @pl.when(jnp.logical_not(in_range))
            def _():
                shifted(first, second, now)

        deliver(step, now, True)
        if steps > 1:
            @pl.when(turn > 0)
            def _():
                deliver(step - 1, 1 - now, False)

        return carry

    fetch(first_step, 0)
    lax.fori_loop(0, steps, one_step, 0)
    deliver(jnp.int32(last_step - 1), (steps - 1) % 2, False)


def take_steps(first_step, last_step, held, outputs, given, crossed, parameters, extra):
    pairs, partner, counts, own, beside = given
    images, slots, width = own.shape
    count = pairs.shape[0]
    heads = width // HEAD_DIM
    peers = lax.axis_size(AXES)
    memory = pl.BlockSpec(memory_space=pl.ANY)
    hbm = pl.BlockSpec(memory_space=pltpu.HBM)
    hidden = parameters[3].shape[1]
    flops = 2 * slots * (4 * width * width + 6 * slots * width + 2 * (width * width + 2 * width * hidden + hidden * width))
    operands = (pairs, partner, counts, own, beside, *crossed, *parameters)
    fixed = len(operands)
    chained = [(i, a) for i, a in enumerate((*held, *(o[0] for o in outputs))) if a is not None]
    aliases = {fixed + n: i for n, (i, _) in enumerate(chained)}
    passed = fixed + len(chained) + len(extra)
    shapes = [
        jax.ShapeDtypeStruct((count, 2, slots, width), BF16),
        jax.ShapeDtypeStruct((images, slots, width), F32),
    ] + [jax.ShapeDtypeStruct((o[1], slots, width), BF16) for o in outputs]
    sizes = {
        "crossed": len(crossed),
        "outputs": len(outputs),
        "skips": [o[2] for o in outputs],
        "lows": [o[3] for o in outputs],
        "highs": [o[4] for o in outputs],
    }

    def body(*refs):
        group_kernel(first_step, last_step, images, peers, sizes, refs[:fixed] + refs[passed:])

    return pl.pallas_call(
        body,
        in_specs=[hbm] * 3 + [memory] * (2 + len(crossed)) + [hbm] * len(parameters) + [memory] * (len(chained) + len(extra)),
        out_specs=[memory] * len(shapes),
        out_shape=shapes,
        scratch_shapes=[
            pltpu.SMEM(pairs.shape, jnp.int32),
            pltpu.SMEM(partner.shape, jnp.int32),
            pltpu.SMEM(counts.shape, jnp.int32),
            *(pltpu.VMEM(p.shape, p.dtype) for p in parameters),
            pltpu.VMEM((2, 2, slots, width), BF16),
            pltpu.VMEM((heads, slots, width), BF16),
            pltpu.VMEM((2, slots, width), BF16),
            pltpu.VMEM((2, heads, slots, 2 * LANES), BF16),
            pltpu.VMEM((slots, slots), BF16),
            pltpu.VMEM((slots, slots), BF16),
            pltpu.VMEM((heads // 2, slots, 2 * LANES), F32),
            pltpu.VMEM((heads // 2, slots, 2 * LANES), F32),
            pltpu.VMEM((slots, width), BF16),
            pltpu.VMEM((slots, width), BF16),
            pltpu.VMEM((2, 2, slots, width), BF16),
            pltpu.VMEM((2, slots, width), F32),
            pltpu.VMEM((2, slots, width), BF16),
            pltpu.SemaphoreType.DMA((2, 2)),
            pltpu.SemaphoreType.DMA((2, 4)),
            pltpu.SemaphoreType.DMA((12,)),
        ],
        input_output_aliases=aliases,
        compiler_params=pltpu.CompilerParams(vmem_limit_bytes=60 * 1024 * 1024),
        cost_estimate=pl.CostEstimate(
            flops=flops * (min(last_step, count) - first_step), bytes_accessed=8 * slots * width * 2, transcendentals=slots * slots * heads
        ),
        name=f"steps_{first_step}",
    )(*operands, *(a for _, a in chained), *extra)


def pack(partner, own, split):
    images, slots, width = own.shape
    count = partner.shape[0]
    memory = pl.BlockSpec(memory_space=pl.ANY)

    def body(hbm_pairs, source, early, late, pairs, buffer, semaphores):
        fetch_scalars((hbm_pairs,), (pairs,), semaphores)
        base = lax.axis_index(AXES) * images
        sent = ranks(pairs, count, base, images)
        loads, stores = ([], [])
        for turn in range(images):
            image = sum(jnp.where(rank == turn, i, 0) for i, rank in enumerate(sent))
            loads.append(pltpu.make_async_copy(source.at[image], buffer.at[turn], semaphores.at[1 + turn]))
            target = early.at[turn] if turn < split else late.at[turn - split]
            stores.append(pltpu.make_async_copy(buffer.at[turn], target, semaphores.at[1 + images + turn]))
        for move in loads:
            move.start()
        for one, two in zip(loads, stores):
            one.wait()
            two.start()
        for move in stores:
            move.wait()

    return pl.pallas_call(
        body,
        in_specs=[memory] * 2,
        out_specs=[memory] * 2,
        out_shape=[jax.ShapeDtypeStruct((n, slots, width), own.dtype) for n in (split, images - split)],
        scratch_shapes=[
            pltpu.SMEM(partner.shape, jnp.int32),
            pltpu.VMEM((images, slots, width), own.dtype),
            pltpu.SemaphoreType.DMA((1 + 2 * images,)),
        ],
        compiler_params=pltpu.CompilerParams(vmem_limit_bytes=60 * 1024 * 1024),
        name="pack",
    )(partner, own)


def add_kernel(entries, images, peers, refs):
    hbm_lists, _, terms = refs[:3], refs[3], refs[4 : 4 + len(entries)]
    out, pairs, beside, partner, held, buffer, copies, loads, scalars = refs[4 + len(entries) :]
    fetch_scalars(hbm_lists, (pairs, beside, partner), scalars)
    count = pairs.shape[0]
    position = lax.axis_index(AXES)
    base = position * images
    other = across(position)
    next_to = position + 1 - 2 * (position % 2)
    paired = (other >= 0) & (other < peers)
    lists = (pairs, beside, partner)
    bases = (other * images, across(next_to) * images, base)
    arranged = [arrange(p, count, b, images) for p, b in zip(lists, bases)]
    targets = []
    for source, step in entries:
        if step > count:
            row, valid = (count - 1, paired & (arranged[2][2] == 0))
        else:
            row, valid, _ = chosen(arranged[source], count, jnp.int32(step))
            if source == 2:
                valid = valid & paired
        target = lists[source][row, 1] - base
        targets.append(jnp.where(valid & in_place(target, 0, images), target, -1))
    slots = held.shape[1]
    tile = min(256, slots)
    touched = [sum((t == image).astype(jnp.int32) for t in targets) > 0 for image in range(images)]
    for image in range(images):
        @pl.when(touched[image])
        def _():
            pltpu.make_async_copy(out.at[image], held.at[image], copies.at[image]).start()

    for number, (term, target) in enumerate(zip(terms, targets)):
        @pl.when(target >= 0)
        def _():
            pltpu.make_async_copy(term, buffer.at[number], loads.at[number]).start()

    for image in range(images):
        @pl.when(touched[image])
        def _():
            pltpu.make_async_copy(out.at[image], held.at[image], copies.at[image]).wait()

            def one_term(number, carry):
                @pl.when(pick(targets, number) == image)
                def _():
                    pltpu.make_async_copy(terms[0], buffer.at[number], loads.at[number]).wait()

                    def one(index, inner):
                        rows = rows_of(index, tile)
                        held[image, rows, :] += buffer[number, rows, :].astype(F32)
                        return inner

                    lax.fori_loop(0, slots // tile, one, 0)

                return carry

            lax.fori_loop(0, len(entries), one_term, 0)
            pltpu.make_async_copy(held.at[image], out.at[image], copies.at[image]).start()

    for image in range(images):
        @pl.when(touched[image])
        def _():
            pltpu.make_async_copy(held.at[image], out.at[image], copies.at[image]).wait()


def add_updates(groups, totals, pairs, beside, partner):
    images, slots, width = totals.shape
    entries = [entry for order, _ in groups for entry in order]
    buffers = [buffer for _, buffer in groups]
    memory = pl.BlockSpec(memory_space=pl.ANY)
    peers = lax.axis_size(AXES)
    split = 4 + len(buffers)

    def body(*refs):
        terms = [ref.at[i] for ref in refs[4:split] for i in range(ref.shape[0])]
        add_kernel(entries, images, peers, (*refs[:4], *terms, *refs[split:]))

    return pl.pallas_call(
        body,
        in_specs=[memory] * split,
        out_specs=memory,
        out_shape=jax.ShapeDtypeStruct(totals.shape, F32),
        scratch_shapes=[
            *(pltpu.SMEM(p.shape, jnp.int32) for p in (pairs, beside, partner)),
            pltpu.VMEM(totals.shape, F32),
            pltpu.VMEM((len(entries), slots, width), BF16),
            pltpu.SemaphoreType.DMA((images,)),
            pltpu.SemaphoreType.DMA((len(entries),)),
            pltpu.SemaphoreType.DMA((3,)),
        ],
        input_output_aliases={3: 0},
        compiler_params=pltpu.CompilerParams(vmem_limit_bytes=16 * 1024 * 1024),
        cost_estimate=pl.CostEstimate(flops=1000, bytes_accessed=totals.size * 4, transcendentals=0),
        name=f"add_{len(entries)}",
    )(pairs, beside, partner, totals, *buffers)


def local(descriptors, key_counts, pair_list, w_qk, w_value, w_out, w_up, b_up, ln_gain, ln_bias, w_down, b_down):
    images, slots, width = descriptors.shape
    count = pair_list.shape[0]
    peers = lax.axis_size(AXES)
    on_chip = [(i, i + 1 - 2 * (i % 2)) for i in range(peers)]
    off_chip = [(i, i + 1) for i in range(1, peers - 1, 2)]
    off_chip = off_chip + [(j, i) for i, j in off_chip]
    partner = lax.ppermute(pair_list, AXES, off_chip)
    beside_list = lax.ppermute(pair_list, AXES, on_chip)
    beside = lax.ppermute(descriptors, AXES, on_chip)
    parameters = (
        w_qk, w_value, w_out, w_up, b_up[None, :], ln_gain[None, :], ln_bias[None, :], w_down, b_down[None, :],
    )
    split = (images + 1) // 2
    crossed = [lax.ppermute(x, AXES, off_chip) for x in pack(partner, descriptors, split)]
    given = (pair_list, partner, key_counts, descriptors, beside)
    middle = split + 1
    states, totals, near = take_steps(
        0, 1, (None, None), [(None, middle, 0, 0, 1)], given, [], parameters, [beside_list]
    )
    states, totals, near, far = take_steps(
        1, middle, (states, totals), [(near, middle, 1, 1, middle), (None, split, 0, 1, middle)],
        given, crossed[:1], parameters, [],
    )
    near_back = lax.ppermute(near, AXES, on_chip)
    far_back = lax.ppermute(far, AXES, off_chip)
    states, totals, last, repeat = take_steps(
        middle, count + 2, (states, totals), [(None, count - middle, 0, middle, count), (None, 1, 0, count + 1, count + 2)],
        given, crossed, parameters, [],
    )
    last_near = lax.ppermute(last, AXES, on_chip)
    last_far = lax.ppermute(last, AXES, off_chip)
    early = [
        ([(0, s) for s in range(middle)], near),
        ([(0, s) for s in range(middle, count)], last),
        ([(2, count + 1)], repeat),
        ([(1, s) for s in range(middle)], near_back),
        ([(2, s) for s in range(1, middle)], far_back),
    ]
    late = [
        ([(1, s) for s in range(middle, count)], last_near),
        ([(2, s) for s in range(middle, count)], last_far),
    ]
    totals = add_updates(early, totals, pair_list, beside_list, partner)
    totals = add_updates(late, totals, pair_list, beside_list, partner)
    return (states, totals)


def solution(mesh):
    in_specs = (P(AXES, None, None), P(), P(AXES, None)) + (P(),) * 9
    out_specs = (P(AXES, None, None, None), P(AXES, None, None))
    return jax.shard_map(local, mesh=mesh, in_specs=in_specs, out_specs=out_specs, check_vma=False)
```

```python
import jax
import jax.numpy as jnp
from jax import lax
from jax.experimental import pallas as pl
from jax.experimental.pallas import tpu as pltpu
from jax.sharding import PartitionSpec as P

HEAD_DIM = 64
LANES = 128
F32 = jnp.float32
BF16 = jnp.bfloat16
LOG2E = 1.4426950408889634
AXES = ("photo", "worker")
EXPONENT_BOUND = 96.0
VALUE_BOUND = 2.0**18


def dot(a, b):
    return jnp.dot(a, b, preferred_element_type=F32)


def dot_rows(a, b):
    return lax.dot_general(a, b, (((1,), (1,)), ((), ())), preferred_element_type=F32)


def dot_columns(a, b):
    return lax.dot_general(a, b, (((0,), (0,)), ((), ())), preferred_element_type=F32)


def rows_of(index, size):
    return pl.ds(pl.multiple_of(index * size, size), size)


def refine(start, message, w_out, w_up, b_up, ln_gain, ln_bias, w_down, b_down):
    width = start.shape[1]
    sent = dot(message, w_out[...]).astype(BF16)
    hidden = dot(start, w_up[:width, :]) + dot(sent, w_up[width:, :]) + b_up[...]
    center = jnp.mean(hidden, axis=-1, keepdims=True)
    shifted = hidden - center
    spread = jnp.mean(shifted * shifted, axis=-1, keepdims=True)
    normed = shifted * lax.rsqrt(spread + 1e-05) * ln_gain[...] + ln_bias[...]
    act = (0.5 * normed * (1.0 + lax.erf(normed * (0.5**0.5)))).astype(BF16)
    return dot(act, w_down[...]) + b_down[...]


def across(position):
    return jnp.where(position % 2 == 1, position + 1, position - 1)


def arrange(pairs, count, base, images):
    hits = [(pairs[s, 1] >= base) & (pairs[s, 1] < base + images) for s in range(count)]
    hits = [h.astype(jnp.int32) for h in hits]
    inside = count - sum(hits)
    places, seen_in, seen_out = ([], jnp.int32(0), jnp.int32(0))
    for hit in hits:
        places.append(jnp.where(hit == 1, inside + seen_out, seen_in))
        seen_out = seen_out + hit
        seen_in = seen_in + 1 - hit
    return (hits, places, inside)


def chosen(arranged, count, step):
    hits, places, inside = arranged
    turn = jnp.where(step == 0, 0, step - 1 + jnp.minimum(inside, 1))
    exists = jnp.where(step == 0, inside > 0, turn < count)
    row = sum(jnp.where(p == turn, s, 0) for s, p in enumerate(places))
    hit = sum(jnp.where(p == turn, h, 0) for h, p in zip(hits, places))
    return (row, exists, hit == 1)


def ranks(pairs, count, base, images):
    firsts = []
    for image in range(images):
        first = jnp.int32(count + image)
        for slot in reversed(range(count)):
            first = jnp.where(pairs[slot, 1] == base + image, slot, first)
        firsts.append(first)
    return [sum((other < first).astype(jnp.int32) for other in firsts) for first in firsts]


def pick(values, index):
    return sum(jnp.where(index == i, v, 0) for i, v in enumerate(values))


def in_place(index, low, length):
    return (index >= low) & (index < low + length)


def fetch_scalars(sources, targets, semaphores):
    moves = [pltpu.make_async_copy(s, t, semaphores.at[i]) for i, (s, t) in enumerate(zip(sources, targets))]
    for move in moves:
        move.start()
    for move in moves:
        move.wait()


def group_kernel(first_step, last_step, images, peers, sizes, refs):
    refs = list(refs)
    take = lambda n: [refs.pop(0) for _ in range(n)]
    hbm_pairs, hbm_partner, hbm_counts, own, beside = take(5)
    crossed = take(sizes["crossed"])
    parameters = take(9)
    states, totals = take(2)
    outputs = take(sizes["outputs"])
    pairs, partner, counts = take(3)
    held_parameters = take(9)
    (
        x_both, q_first, k_both, v_both,
        weights_even, weights_odd, sum_first, sum_second, m_first, m_second,
        new_states, new_delta, new_update, loads, sends, others,
    ) = refs
    w_qk, w_value, w_out, w_up, b_up, ln_gain, ln_bias, w_down, b_down = held_parameters
    slots, width = x_both.shape[2:]
    k_second, v_first, v_second = (k_both.at[1], v_both.at[0], v_both.at[1])
    heads = width // HEAD_DIM
    count = pairs.shape[0]
    steps = last_step - first_step
    moves = [pltpu.make_async_copy(s, t, others.at[i]) for i, (s, t) in enumerate(zip(parameters, held_parameters))]
    for move in moves:
        move.start()
    fetch_scalars((hbm_pairs, hbm_partner, hbm_counts), (pairs, partner, counts), others.at[pl.ds(9, 3)])
    position = lax.axis_index(AXES)
    base = position * images
    beside_base = (position + 1 - 2 * (position % 2)) * images
    other = across(position)
    other_base = other * images
    paired = (other >= 0) & (other < peers)
    arranged = arrange(pairs, count, other_base, images)
    sent = ranks(pairs, count, other_base, images)
    _, _, their_inside = arrange(partner, count, base, images)
    can_repeat = last_step > count

    def describe(step):
        row, exists, _ = chosen(arranged, count, step)
        first = base + jnp.clip(pairs[row, 0] - base, 0, images - 1)
        second = pairs[row, 1]
        if can_repeat:
            again = step > count
            exists = jnp.where(again, paired & (their_inside == 0), exists)
            first = jnp.where(again, other_base + jnp.clip(partner[count - 1, 0] - other_base, 0, images - 1), first)
            second = jnp.where(again, partner[count - 1, 1], second)
        return (row, exists, first, second)

    def load(image, held, semaphore):
        for source, low in ((own, base), (beside, beside_base)):
            @pl.when(in_place(image, low, images))
            def _():
                pltpu.make_async_copy(source.at[jnp.clip(image - low, 0, images - 1)], held, semaphore).start()

        rank = jnp.where(in_place(image, other_base, images), pick(sent, image - other_base), -1)
        offset = 0
        for source in crossed:
            length = source.shape[0]

            @pl.when(in_place(rank, offset, length))
            def _():
                pltpu.make_async_copy(source.at[jnp.clip(rank - offset, 0, length - 1)], held, semaphore).start()

            offset += length

    def fetch(step, turn):
        _, exists, first, second = describe(step)

        @pl.when(exists)
        def _():
            load(first, x_both.at[turn, 0], loads.at[turn, 0])
            load(second, x_both.at[turn, 1], loads.at[turn, 1])

    def refined(start, message):
        return refine(start, message, w_out, w_up, b_up, ln_gain, ln_bias, w_down, b_down)

    def unshifted(first, second, one, two, now):
        count_first = counts[first]
        count_second = counts[second]
        lane = lax.broadcasted_iota(jnp.int32, (slots, LANES), 1)
        line = lax.broadcasted_iota(jnp.int32, (slots, LANES), 0)
        halves = (lane < HEAD_DIM, lane >= HEAD_DIM)
        scaled = dot(one[...], w_qk[...]) * (HEAD_DIM**-0.5 * LOG2E)
        key = dot(two[...], w_qk[...])
        k_second[...] = key.astype(BF16)
        value_one = dot(one[...], w_value[...])
        value_two = dot(two[...], w_value[...])
        empty = jnp.zeros((slots, LANES), BF16)
        for head in range(heads):
            start = head * HEAD_DIM // LANES * LANES
            columns = slice(start, start + LANES)
            half = halves[head % 2]
            for gap in range(0, width, LANES):
                if gap != start:
                    q_first[head, :, gap : gap + LANES] = empty
            q_first[head, :, columns] = jnp.where(half, scaled[:, columns], 0.0).astype(BF16)
            for value, held, limit in ((value_one, v_first, count_first), (value_two, v_second, count_second)):
                valid = half & (line < limit)
                held[head, :, :LANES] = jnp.where(valid, value[:, columns], 0.0).astype(BF16)
                held[head, :, LANES:] = jnp.where(valid, 1.0, 0.0).astype(BF16)
        query_norm = jnp.max(jnp.sum(scaled * scaled, axis=-1, keepdims=True))
        key_norm = jnp.max(jnp.sum(key * key, axis=-1, keepdims=True))
        largest = jnp.max(jnp.maximum(jnp.abs(value_one), jnp.abs(value_two)))
        tile = min(256, slots)
        weights = (weights_even, weights_odd)

        def score(head):
            for start in range(0, slots, tile):
                scores = dot_rows(q_first[head], k_second[start : start + tile, :])
                weights[head % 2][:, start : start + tile] = jnp.exp2(scores).astype(BF16)

        def mix(head):
            group = head // 2
            part_first = dot(weights[head % 2][...], v_second[head])
            part_second = dot_columns(weights[head % 2][...], v_first[head])
            if head % 2 == 0:
                sum_first[group] = part_first
                sum_second[group] = part_second
            else:
                sum_first[group] += part_first
                sum_second[group] += part_second

        score(0)
        for head in range(1, heads):
            score(head)
            mix(head - 1)
        mix(heads - 1)
        for group in range(heads // 2):
            columns = slice(group * LANES, (group + 1) * LANES)
            for total, message in ((sum_first, m_first), (sum_second, m_second)):
                message[:, columns] = (total[group, :, :LANES] / total[group, :, LANES:]).astype(BF16)
        here = two[...]
        change = refined(here, m_second[...])
        new_update[now] = change.astype(BF16)
        new_states[now, 1] = (here.astype(F32) + change).astype(BF16)
        here = one[...]
        change = refined(here, m_first[...])
        new_delta[now] = change
        new_states[now, 0] = (here.astype(F32) + change).astype(BF16)
        return (query_norm * key_norm <= EXPONENT_BOUND**2) & (largest <= VALUE_BOUND)

    def shifted(first, second, now):
        tile = min(16, slots)
        spot = lax.broadcasted_iota(jnp.int32, (tile, slots), 1)
        column = lax.broadcasted_iota(jnp.int32, (tile, width), 1)

        def fill(index, carry):
            rows = rows_of(index, tile)
            k_both[0, rows, :] = dot(x_both[now, 0, rows, :], w_qk[...]).astype(BF16)
            return carry

        lax.fori_loop(0, slots // tile, fill, 0)

        def attend(index, carry):
            side = index % 2
            rows = rows_of(index // 2, tile)
            limit = jnp.where(side == 0, counts[second], counts[first])
            query_rows = k_both[side, rows, :].astype(F32)

            def one_head(head, parts):
                query = jnp.where(column // HEAD_DIM == head, query_rows, 0.0).astype(BF16)
                scores = dot_rows(query, k_both[1 - side]) * HEAD_DIM**-0.5
                scores = jnp.where(spot < limit, scores, -jnp.inf)
                scores = jnp.exp(scores - jnp.max(scores, axis=-1, keepdims=True))
                scores = scores / jnp.sum(scores, axis=-1, keepdims=True)
                part = dot(scores.astype(BF16), v_both[1 - side, head, :, :LANES])
                return tuple(p + jnp.where(head // 2 == i, part, 0.0) for i, p in enumerate(parts))

            nothing = jnp.zeros((tile, LANES), F32)
            parts = lax.fori_loop(0, heads, one_head, (nothing,) * (heads // 2))
            here = x_both[now, side, rows, :]
            change = refined(here, jnp.concatenate(parts, axis=-1).astype(BF16))
            new_states[now, side, rows, :] = (here.astype(F32) + change).astype(BF16)

            @pl.when(side == 1)
            def _():
                new_update[now, rows, :] = change.astype(BF16)

            @pl.when(side == 0)
            def _():
                new_delta[now, rows, :] = change

            return carry

        lax.fori_loop(0, 2 * (slots // tile), attend, 0)

    def deliver(step, now, begin):
        row, exists, first, _ = describe(step)

        @pl.when(exists)
        def _():
            for slot, (output, low, high) in enumerate(zip(outputs, sizes["lows"], sizes["highs"])):
                @pl.when(in_place(step, low, high - low))
                def _():
                    place = jnp.clip(step - low + sizes["skips"][slot], 0, output.shape[0] - 1)
                    move = pltpu.make_async_copy(new_update.at[now], output.at[place], sends.at[now, slot])
                    move.start() if begin else move.wait()

            @pl.when(step <= count)
            def _():
                place = jnp.clip(first - base, 0, images - 1)
                for move in (
                    pltpu.make_async_copy(new_states.at[now], states.at[row], sends.at[now, 2]),
                    pltpu.make_async_copy(new_delta.at[now], totals.at[place], sends.at[now, 3]),
                ):
                    move.start() if begin else move.wait()

    def one_step(turn, carry):
        step = first_step + turn
        now = turn % 2
        _, exists, first, second = describe(step)
        one, two = (x_both.at[now, 0], x_both.at[now, 1])

        @pl.when(exists)
        def _():
            pltpu.make_async_copy(own.at[0], one, loads.at[now, 0]).wait()
            pltpu.make_async_copy(own.at[0], two, loads.at[now, 1]).wait()

        if steps > 1:
            @pl.when(turn + 1 < steps)
            def _():
                fetch(step + 1, (turn + 1) % 2)

        @pl.when(turn == 0)
        def _():
            for move in moves:
                move.wait()

        @pl.when(exists)
        def _():
            in_range = unshifted(first, second, one, two, now)

            @pl.when(jnp.logical_not(in_range))
            def _():
                shifted(first, second, now)

        deliver(step, now, True)
        if steps > 1:
            @pl.when(turn > 0)
            def _():
                deliver(step - 1, 1 - now, False)

        return carry

    fetch(first_step, 0)
    lax.fori_loop(0, steps, one_step, 0)
    deliver(jnp.int32(last_step - 1), (steps - 1) % 2, False)


def take_steps(first_step, last_step, held, outputs, given, crossed, parameters, extra):
    pairs, partner, counts, own, beside = given
    images, slots, width = own.shape
    count = pairs.shape[0]
    heads = width // HEAD_DIM
    peers = lax.axis_size(AXES)
    memory = pl.BlockSpec(memory_space=pl.ANY)
    hbm = pl.BlockSpec(memory_space=pltpu.HBM)
    hidden = parameters[3].shape[1]
    flops = 2 * slots * (4 * width * width + 6 * slots * width + 2 * (width * width + 2 * width * hidden + hidden * width))
    operands = (pairs, partner, counts, own, beside, *crossed, *parameters)
    fixed = len(operands)
    chained = [(i, a) for i, a in enumerate((*held, *(o[0] for o in outputs))) if a is not None]
    aliases = {fixed + n: i for n, (i, _) in enumerate(chained)}
    passed = fixed + len(chained) + len(extra)
    shapes = [
        jax.ShapeDtypeStruct((count, 2, slots, width), BF16),
        jax.ShapeDtypeStruct((images, slots, width), F32),
    ] + [jax.ShapeDtypeStruct((o[1], slots, width), BF16) for o in outputs]
    sizes = {
        "crossed": len(crossed),
        "outputs": len(outputs),
        "skips": [o[2] for o in outputs],
        "lows": [o[3] for o in outputs],
        "highs": [o[4] for o in outputs],
    }

    def body(*refs):
        group_kernel(first_step, last_step, images, peers, sizes, refs[:fixed] + refs[passed:])

    return pl.pallas_call(
        body,
        in_specs=[hbm] * 3 + [memory] * (2 + len(crossed)) + [hbm] * len(parameters) + [memory] * (len(chained) + len(extra)),
        out_specs=[memory] * len(shapes),
        out_shape=shapes,
        scratch_shapes=[
            pltpu.SMEM(pairs.shape, jnp.int32),
            pltpu.SMEM(partner.shape, jnp.int32),
            pltpu.SMEM(counts.shape, jnp.int32),
            *(pltpu.VMEM(p.shape, p.dtype) for p in parameters),
            pltpu.VMEM((2, 2, slots, width), BF16),
            pltpu.VMEM((heads, slots, width), BF16),
            pltpu.VMEM((2, slots, width), BF16),
            pltpu.VMEM((2, heads, slots, 2 * LANES), BF16),
            pltpu.VMEM((slots, slots), BF16),
            pltpu.VMEM((slots, slots), BF16),
            pltpu.VMEM((heads // 2, slots, 2 * LANES), F32),
            pltpu.VMEM((heads // 2, slots, 2 * LANES), F32),
            pltpu.VMEM((slots, width), BF16),
            pltpu.VMEM((slots, width), BF16),
            pltpu.VMEM((2, 2, slots, width), BF16),
            pltpu.VMEM((2, slots, width), F32),
            pltpu.VMEM((2, slots, width), BF16),
            pltpu.SemaphoreType.DMA((2, 2)),
            pltpu.SemaphoreType.DMA((2, 4)),
            pltpu.SemaphoreType.DMA((12,)),
        ],
        input_output_aliases=aliases,
        compiler_params=pltpu.CompilerParams(vmem_limit_bytes=67043328),
        cost_estimate=pl.CostEstimate(
            flops=flops * (min(last_step, count) - first_step), bytes_accessed=8 * slots * width * 2, transcendentals=slots * slots * heads
        ),
        name=f"steps_{first_step}",
    )(*operands, *(a for _, a in chained), *extra)


def pack(partner, own, split):
    images, slots, width = own.shape
    count = partner.shape[0]
    memory = pl.BlockSpec(memory_space=pl.ANY)

    def body(hbm_pairs, source, early, late, pairs, buffer, semaphores):
        fetch_scalars((hbm_pairs,), (pairs,), semaphores)
        base = lax.axis_index(AXES) * images
        sent = ranks(pairs, count, base, images)
        loads, stores = ([], [])
        for turn in range(images):
            image = sum(jnp.where(rank == turn, i, 0) for i, rank in enumerate(sent))
            loads.append(pltpu.make_async_copy(source.at[image], buffer.at[turn], semaphores.at[1 + turn]))
            target = early.at[turn] if turn < split else late.at[turn - split]
            stores.append(pltpu.make_async_copy(buffer.at[turn], target, semaphores.at[1 + images + turn]))
        for move in loads:
            move.start()
        for one, two in zip(loads, stores):
            one.wait()
            two.start()
        for move in stores:
            move.wait()

    return pl.pallas_call(
        body,
        in_specs=[memory] * 2,
        out_specs=[memory] * 2,
        out_shape=[jax.ShapeDtypeStruct((n, slots, width), own.dtype) for n in (split, images - split)],
        scratch_shapes=[
            pltpu.SMEM(partner.shape, jnp.int32),
            pltpu.VMEM((images, slots, width), own.dtype),
            pltpu.SemaphoreType.DMA((1 + 2 * images,)),
        ],
        compiler_params=pltpu.CompilerParams(vmem_limit_bytes=67043328),
        name="pack",
    )(partner, own)


def add_kernel(entries, images, peers, refs):
    hbm_lists, _, terms = refs[:3], refs[3], refs[4 : 4 + len(entries)]
    out, pairs, beside, partner, held, buffer, copies, loads, scalars = refs[4 + len(entries) :]
    fetch_scalars(hbm_lists, (pairs, beside, partner), scalars)
    count = pairs.shape[0]
    position = lax.axis_index(AXES)
    base = position * images
    other = across(position)
    next_to = position + 1 - 2 * (position % 2)
    paired = (other >= 0) & (other < peers)
    lists = (pairs, beside, partner)
    bases = (other * images, across(next_to) * images, base)
    arranged = [arrange(p, count, b, images) for p, b in zip(lists, bases)]
    targets = []
    for source, step in entries:
        if step > count:
            row, valid = (count - 1, paired & (arranged[2][2] == 0))
        else:
            row, valid, _ = chosen(arranged[source], count, jnp.int32(step))
            if source == 2:
                valid = valid & paired
        target = lists[source][row, 1] - base
        targets.append(jnp.where(valid & in_place(target, 0, images), target, -1))
    slots = held.shape[1]
    tile = min(256, slots)
    touched = [sum((t == image).astype(jnp.int32) for t in targets) > 0 for image in range(images)]
    for image in range(images):
        @pl.when(touched[image])
        def _():
            pltpu.make_async_copy(out.at[image], held.at[image], copies.at[image]).start()

    for number, (term, target) in enumerate(zip(terms, targets)):
        @pl.when(target >= 0)
        def _():
            pltpu.make_async_copy(term, buffer.at[number], loads.at[number]).start()

    for image in range(images):
        @pl.when(touched[image])
        def _():
            pltpu.make_async_copy(out.at[image], held.at[image], copies.at[image]).wait()

            def one_term(number, carry):
                @pl.when(pick(targets, number) == image)
                def _():
                    pltpu.make_async_copy(terms[0], buffer.at[number], loads.at[number]).wait()

                    def one(index, inner):
                        rows = rows_of(index, tile)
                        held[image, rows, :] += buffer[number, rows, :].astype(F32)
                        return inner

                    lax.fori_loop(0, slots // tile, one, 0)

                return carry

            lax.fori_loop(0, len(entries), one_term, 0)
            pltpu.make_async_copy(held.at[image], out.at[image], copies.at[image]).start()

    for image in range(images):
        @pl.when(touched[image])
        def _():
            pltpu.make_async_copy(held.at[image], out.at[image], copies.at[image]).wait()


def add_updates(groups, totals, pairs, beside, partner):
    images, slots, width = totals.shape
    entries = [entry for order, _ in groups for entry in order]
    buffers = [buffer for _, buffer in groups]
    memory = pl.BlockSpec(memory_space=pl.ANY)
    peers = lax.axis_size(AXES)
    split = 4 + len(buffers)

    def body(*refs):
        terms = [ref.at[i] for ref in refs[4:split] for i in range(ref.shape[0])]
        add_kernel(entries, images, peers, (*refs[:4], *terms, *refs[split:]))

    return pl.pallas_call(
        body,
        in_specs=[memory] * split,
        out_specs=memory,
        out_shape=jax.ShapeDtypeStruct(totals.shape, F32),
        scratch_shapes=[
            *(pltpu.SMEM(p.shape, jnp.int32) for p in (pairs, beside, partner)),
            pltpu.VMEM(totals.shape, F32),
            pltpu.VMEM((len(entries), slots, width), BF16),
            pltpu.SemaphoreType.DMA((images,)),
            pltpu.SemaphoreType.DMA((len(entries),)),
            pltpu.SemaphoreType.DMA((3,)),
        ],
        input_output_aliases={3: 0},
        compiler_params=pltpu.CompilerParams(vmem_limit_bytes=16 * 1024 * 1024),
        cost_estimate=pl.CostEstimate(flops=1000, bytes_accessed=totals.size * 4, transcendentals=0),
        name=f"add_{len(entries)}",
    )(pairs, beside, partner, totals, *buffers)


def local(descriptors, key_counts, pair_list, w_qk, w_value, w_out, w_up, b_up, ln_gain, ln_bias, w_down, b_down):
    images, slots, width = descriptors.shape
    count = pair_list.shape[0]
    peers = lax.axis_size(AXES)
    on_chip = [(i, i + 1 - 2 * (i % 2)) for i in range(peers)]
    off_chip = [(i, i + 1) for i in range(1, peers - 1, 2)]
    off_chip = off_chip + [(j, i) for i, j in off_chip]
    partner = lax.ppermute(pair_list, AXES, off_chip)
    beside_list = lax.ppermute(pair_list, AXES, on_chip)
    beside = lax.ppermute(descriptors, AXES, on_chip)
    parameters = (
        w_qk, w_value, w_out, w_up, b_up[None, :], ln_gain[None, :], ln_bias[None, :], w_down, b_down[None, :],
    )
    split = (images + 1) // 2
    crossed = [lax.ppermute(x, AXES, off_chip) for x in pack(partner, descriptors, split)]
    given = (pair_list, partner, key_counts, descriptors, beside)
    middle = split + 1
    states, totals, near = take_steps(
        0, 1, (None, None), [(None, middle, 0, 0, 1)], given, [], parameters, [beside_list]
    )
    states, totals, near, far = take_steps(
        1, middle, (states, totals), [(near, middle, 1, 1, middle), (None, split, 0, 1, middle)],
        given, crossed[:1], parameters, [],
    )
    near_back = lax.ppermute(near, AXES, on_chip)
    far_back = lax.ppermute(far, AXES, off_chip)
    states, totals, last, repeat = take_steps(
        middle, count + 2, (states, totals), [(None, count - middle, 0, middle, count), (None, 1, 0, count + 1, count + 2)],
        given, crossed, parameters, [],
    )
    last_near = lax.ppermute(last, AXES, on_chip)
    last_far = lax.ppermute(last, AXES, off_chip)
    early = [
        ([(0, s) for s in range(middle)], near),
        ([(0, s) for s in range(middle, count)], last),
        ([(2, count + 1)], repeat),
        ([(1, s) for s in range(middle)], near_back),
        ([(2, s) for s in range(1, middle)], far_back),
    ]
    late = [
        ([(1, s) for s in range(middle, count)], last_near),
        ([(2, s) for s in range(middle, count)], last_far),
    ]
    totals = add_updates(early, totals, pair_list, beside_list, partner)
    totals = add_updates(late, totals, pair_list, beside_list, partner)
    return (states, totals)


def solution(mesh):
    in_specs = (P(AXES, None, None), P(), P(AXES, None)) + (P(),) * 9
    out_specs = (P(AXES, None, None, None), P(AXES, None, None))
    return jax.shard_map(local, mesh=mesh, in_specs=in_specs, out_specs=out_specs, check_vma=False)
```

```python
import jax
import jax.numpy as jnp
from jax import lax
from jax.experimental import pallas as pl
from jax.experimental.pallas import tpu as pltpu
from jax.sharding import PartitionSpec as P

HEAD_DIM = 64
LANES = 128
F32 = jnp.float32
BF16 = jnp.bfloat16
LOG2E = 1.4426950408889634
AXES = ("photo", "worker")
EXPONENT_BOUND = 96.0
VALUE_BOUND = 2.0**18


def dot(a, b):
    return jnp.dot(a, b, preferred_element_type=F32)


def dot_rows(a, b):
    return lax.dot_general(a, b, (((1,), (1,)), ((), ())), preferred_element_type=F32)


def dot_columns(a, b):
    return lax.dot_general(a, b, (((0,), (0,)), ((), ())), preferred_element_type=F32)


def rows_of(index, size):
    return pl.ds(pl.multiple_of(index * size, size), size)


def refine(start, message, w_out, w_up, b_up, ln_gain, ln_bias, w_down, b_down):
    width = start.shape[1]
    sent = dot(message, w_out[...]).astype(BF16)
    hidden = dot(start, w_up[:width, :]) + dot(sent, w_up[width:, :]) + b_up[...]
    center = jnp.mean(hidden, axis=-1, keepdims=True)
    shifted = hidden - center
    spread = jnp.mean(shifted * shifted, axis=-1, keepdims=True)
    normed = shifted * lax.rsqrt(spread + 1e-05) * ln_gain[...] + ln_bias[...]
    act = (0.5 * normed * (1.0 + lax.erf(normed * (0.5**0.5)))).astype(BF16)
    return dot(act, w_down[...]) + b_down[...]


def across(position):
    return jnp.where(position % 2 == 1, position + 1, position - 1)


def arrange(pairs, count, base, images):
    hits = [(pairs[s, 1] >= base) & (pairs[s, 1] < base + images) for s in range(count)]
    hits = [h.astype(jnp.int32) for h in hits]
    inside = count - sum(hits)
    places, seen_in, seen_out = ([], jnp.int32(0), jnp.int32(0))
    for hit in hits:
        places.append(jnp.where(hit == 1, inside + seen_out, seen_in))
        seen_out = seen_out + hit
        seen_in = seen_in + 1 - hit
    return (hits, places, inside)


def chosen(arranged, count, step):
    hits, places, inside = arranged
    turn = jnp.where(step == 0, 0, step - 1 + jnp.minimum(inside, 1))
    exists = jnp.where(step == 0, inside > 0, turn < count)
    row = sum(jnp.where(p == turn, s, 0) for s, p in enumerate(places))
    hit = sum(jnp.where(p == turn, h, 0) for h, p in zip(hits, places))
    return (row, exists, hit == 1)


def ranks(pairs, count, base, images):
    firsts = []
    for image in range(images):
        first = jnp.int32(count + image)
        for slot in reversed(range(count)):
            first = jnp.where(pairs[slot, 1] == base + image, slot, first)
        firsts.append(first)
    return [sum((other < first).astype(jnp.int32) for other in firsts) for first in firsts]


def pick(values, index):
    return sum(jnp.where(index == i, v, 0) for i, v in enumerate(values))


def in_place(index, low, length):
    return (index >= low) & (index < low + length)


def fetch_scalars(sources, targets, semaphores):
    moves = [pltpu.make_async_copy(s, t, semaphores.at[i]) for i, (s, t) in enumerate(zip(sources, targets))]
    for move in moves:
        move.start()
    for move in moves:
        move.wait()


def group_kernel(first_step, last_step, images, peers, sizes, refs):
    refs = list(refs)
    take = lambda n: [refs.pop(0) for _ in range(n)]
    hbm_pairs, hbm_partner, hbm_counts, own, beside = take(5)
    crossed = take(sizes["crossed"])
    parameters = take(9)
    states, totals = take(2)
    outputs = take(sizes["outputs"])
    pairs, partner, counts = take(3)
    held_parameters = take(9)
    (
        x_both, q_first, k_both, v_both,
        weights_even, weights_odd, sum_first, sum_second, m_first, m_second,
        new_states, new_delta, new_update, loads, sends, others,
    ) = refs
    w_qk, w_value, w_out, w_up, b_up, ln_gain, ln_bias, w_down, b_down = held_parameters
    slots, width = x_both.shape[2:]
    k_second, v_first, v_second = (k_both.at[1], v_both.at[0], v_both.at[1])
    heads = width // HEAD_DIM
    count = pairs.shape[0]
    steps = last_step - first_step
    moves = [pltpu.make_async_copy(s, t, others.at[i]) for i, (s, t) in enumerate(zip(parameters, held_parameters))]
    for move in moves:
        move.start()
    fetch_scalars((hbm_pairs, hbm_partner, hbm_counts), (pairs, partner, counts), others.at[pl.ds(9, 3)])
    position = lax.axis_index(AXES)
    base = position * images
    beside_base = (position + 1 - 2 * (position % 2)) * images
    other = across(position)
    other_base = other * images
    paired = (other >= 0) & (other < peers)
    arranged = arrange(pairs, count, other_base, images)
    sent = ranks(pairs, count, other_base, images)
    theirs = arrange(partner, count, base, images)
    swapped = paired & ((arranged[2] == 0) | (theirs[2] == 0))

    def describe(step):
        row, exists, _ = chosen(arranged, count, step)
        first = base + jnp.clip(pairs[row, 0] - base, 0, images - 1)
        second = pairs[row, 1]
        if sizes["rare"]:
            lost, present, hit = chosen(theirs, count, jnp.int32(1))
            again = step > count
            line = jnp.where(step == count + 1, count - 1, lost)
            exists = jnp.where(step == count + 1, paired & (theirs[2] == 0), exists)
            exists = jnp.where(step == count + 2, swapped & present & hit, exists)
            first = jnp.where(again, other_base + jnp.clip(partner[line, 0] - other_base, 0, images - 1), first)
            second = jnp.where(again, partner[line, 1], second)
        return (row, exists, first, second)

    def load(image, held, semaphore):
        for source, low in ((own, base), (beside, beside_base)):
            @pl.when(in_place(image, low, images))
            def _():
                pltpu.make_async_copy(source.at[jnp.clip(image - low, 0, images - 1)], held, semaphore).start()

        rank = jnp.where(in_place(image, other_base, images), pick(sent, image - other_base), -1)
        offset = 0
        for source in crossed:
            length = source.shape[0]

            @pl.when(in_place(rank, offset, length))
            def _():
                pltpu.make_async_copy(source.at[jnp.clip(rank - offset, 0, length - 1)], held, semaphore).start()

            offset += length

    def fetch(step, turn):
        _, exists, first, second = describe(step)

        @pl.when(exists)
        def _():
            load(first, x_both.at[turn, 0], loads.at[turn, 0])
            load(second, x_both.at[turn, 1], loads.at[turn, 1])

    def refined(start, message):
        return refine(start, message, w_out, w_up, b_up, ln_gain, ln_bias, w_down, b_down)

    def unshifted(first, second, one, two, now):
        count_first = counts[first]
        count_second = counts[second]
        block = min(256, slots) if sizes["compact"] else slots
        lane = lax.broadcasted_iota(jnp.int32, (block, LANES), 1)
        line = lax.broadcasted_iota(jnp.int32, (block, LANES), 0)
        halves = (lane < HEAD_DIM, lane >= HEAD_DIM)
        def project(index, bounds):
            rows = rows_of(index, block)
            scaled = dot(one[rows, :], w_qk[...]) * (HEAD_DIM**-0.5 * LOG2E)
            key = dot(two[rows, :], w_qk[...])
            k_second[rows, :] = key.astype(BF16)
            value_one = dot(one[rows, :], w_value[...])
            value_two = dot(two[rows, :], w_value[...])
            empty = jnp.zeros((block, LANES), BF16)
            for head in range(heads):
                start = head * HEAD_DIM // LANES * LANES
                columns = slice(start, start + LANES)
                half = halves[head % 2]
                for gap in range(0, width, LANES):
                    if gap != start:
                        q_first[head, rows, gap : gap + LANES] = empty
                q_first[head, rows, columns] = jnp.where(half, scaled[:, columns], 0.0).astype(BF16)
                for value, held, limit in ((value_one, v_first, count_first), (value_two, v_second, count_second)):
                    valid = half & (line + index * block < limit)
                    held[head, rows, :LANES] = jnp.where(valid, value[:, columns], 0.0).astype(BF16)
                    held[head, rows, LANES:] = jnp.where(valid, 1.0, 0.0).astype(BF16)
            found = (
                jnp.max(jnp.sum(scaled * scaled, axis=-1, keepdims=True)),
                jnp.max(jnp.sum(key * key, axis=-1, keepdims=True)),
                jnp.max(jnp.maximum(jnp.abs(value_one), jnp.abs(value_two))),
            )
            return tuple(jnp.maximum(a, b) for a, b in zip(bounds, found))

        zero = jnp.float32(0.0)
        query_norm, key_norm, largest = lax.fori_loop(0, slots // block, project, (zero, zero, zero))
        tile = min(256, slots)
        weights = (weights_even, weights_odd)

        def score(head):
            for start in range(0, slots, tile):
                scores = dot_rows(q_first[head], k_second[start : start + tile, :])
                weights[head % 2][:, start : start + tile] = jnp.exp2(scores).astype(BF16)

        def mix(head):
            group = head // 2
            part_first = dot(weights[head % 2][...], v_second[head])
            part_second = dot_columns(weights[head % 2][...], v_first[head])
            if head % 2 == 0:
                sum_first[group] = part_first
                sum_second[group] = part_second
            else:
                sum_first[group] += part_first
                sum_second[group] += part_second

        score(0)
        for head in range(1, heads):
            score(head)
            mix(head - 1)
        mix(heads - 1)
        for group in range(heads // 2):
            columns = slice(group * LANES, (group + 1) * LANES)
            for total, message in ((sum_first, m_first), (sum_second, m_second)):
                message[:, columns] = (total[group, :, :LANES] / total[group, :, LANES:]).astype(BF16)
        def finish(index, carry):
            rows = rows_of(index, block)
            for side, start, message in ((1, two, m_second), (0, one, m_first)):
                here = start[rows, :]
                change = refined(here, message[rows, :])
                new_states[now, side, rows, :] = (here.astype(F32) + change).astype(BF16)
                if side == 1:
                    new_update[now, rows, :] = change.astype(BF16)
                else:
                    new_delta[now, rows, :] = change
            return carry

        lax.fori_loop(0, slots // block, finish, 0)
        return (query_norm * key_norm <= EXPONENT_BOUND**2) & (largest <= VALUE_BOUND)

    def shifted(first, second, now):
        tile = min(16, slots)
        spot = lax.broadcasted_iota(jnp.int32, (tile, slots), 1)
        column = lax.broadcasted_iota(jnp.int32, (tile, width), 1)

        def fill(index, carry):
            rows = rows_of(index, tile)
            k_both[0, rows, :] = dot(x_both[now, 0, rows, :], w_qk[...]).astype(BF16)
            if sizes["rare"]:
                k_both[1, rows, :] = dot(x_both[now, 1, rows, :], w_qk[...]).astype(BF16)
                lane = lax.broadcasted_iota(jnp.int32, (tile, LANES), 1)
                for side in range(2):
                    value = dot(x_both[now, side, rows, :], w_value[...])
                    for head in range(heads):
                        start = head * HEAD_DIM // LANES * LANES
                        half = (lane >= HEAD_DIM) == (head % 2 == 1)
                        part = jnp.where(half, value[:, start : start + LANES], 0.0)
                        v_both[side, head, rows, :LANES] = part.astype(BF16)
            return carry

        lax.fori_loop(0, slots // tile, fill, 0)

        def attend(index, carry):
            side = index % 2
            rows = rows_of(index // 2, tile)
            limit = jnp.where(side == 0, counts[second], counts[first])
            query_rows = k_both[side, rows, :].astype(F32)

            def one_head(head, parts):
                query = jnp.where(column // HEAD_DIM == head, query_rows, 0.0).astype(BF16)
                scores = dot_rows(query, k_both[1 - side]) * HEAD_DIM**-0.5
                scores = jnp.where(spot < limit, scores, -jnp.inf)
                scores = jnp.exp(scores - jnp.max(scores, axis=-1, keepdims=True))
                scores = scores / jnp.sum(scores, axis=-1, keepdims=True)
                part = dot(scores.astype(BF16), v_both[1 - side, head, :, :LANES])
                return tuple(p + jnp.where(head // 2 == i, part, 0.0) for i, p in enumerate(parts))

            nothing = jnp.zeros((tile, LANES), F32)
            parts = lax.fori_loop(0, heads, one_head, (nothing,) * (heads // 2))
            here = x_both[now, side, rows, :]
            change = refined(here, jnp.concatenate(parts, axis=-1).astype(BF16))
            new_states[now, side, rows, :] = (here.astype(F32) + change).astype(BF16)

            @pl.when(side == 1)
            def _():
                new_update[now, rows, :] = change.astype(BF16)

            @pl.when(side == 0)
            def _():
                new_delta[now, rows, :] = change

            return carry

        lax.fori_loop(0, 2 * (slots // tile), attend, 0)

    def deliver(step, now, begin):
        row, exists, first, _ = describe(step)

        @pl.when(exists)
        def _():
            for slot, (output, low, high) in enumerate(zip(outputs, sizes["lows"], sizes["highs"])):
                @pl.when(in_place(step, low, high - low))
                def _():
                    place = jnp.clip(step - low + sizes["skips"][slot], 0, output.shape[0] - 1)
                    move = pltpu.make_async_copy(new_update.at[now], output.at[place], sends.at[now, slot])
                    move.start() if begin else move.wait()

            @pl.when(step <= count)
            def _():
                place = jnp.clip(first - base, 0, images - 1)
                for move in (
                    pltpu.make_async_copy(new_states.at[now], states.at[row], sends.at[now, 2]),
                    pltpu.make_async_copy(new_delta.at[now], totals.at[place], sends.at[now, 3]),
                ):
                    move.start() if begin else move.wait()

    def one_step(turn, carry):
        step = first_step + turn
        now = turn % 2
        _, exists, first, second = describe(step)
        one, two = (x_both.at[now, 0], x_both.at[now, 1])

        @pl.when(exists)
        def _():
            pltpu.make_async_copy(own.at[0], one, loads.at[now, 0]).wait()
            pltpu.make_async_copy(own.at[0], two, loads.at[now, 1]).wait()

        if steps > 1:
            @pl.when(turn + 1 < steps)
            def _():
                fetch(step + 1, (turn + 1) % 2)

        @pl.when(turn == 0)
        def _():
            for move in moves:
                move.wait()

        @pl.when(exists)
        def _():
            if sizes["rare"]:
                shifted(first, second, now)
            else:
                in_range = unshifted(first, second, one, two, now)

                @pl.when(jnp.logical_not(in_range))
                def _():
                    shifted(first, second, now)

        deliver(step, now, True)
        if steps > 1:
            @pl.when(turn > 0)
            def _():
                deliver(step - 1, 1 - now, False)

        return carry

    fetch(first_step, 0)
    lax.fori_loop(0, steps, one_step, 0)
    deliver(jnp.int32(last_step - 1), (steps - 1) % 2, False)
    if sizes["swap"] is not None:
        @pl.when(swapped)
        def _():
            order = ranks(partner, count, base, images)
            image = sum(jnp.where(rank == images - 1, i, 0) for i, rank in enumerate(order))
            fetched = pltpu.make_async_copy(own.at[image], x_both.at[0, 0], loads.at[0, 0])
            fetched.start()
            fetched.wait()
            placed = pltpu.make_async_copy(x_both.at[0, 0], outputs[sizes["swap"]].at[0], loads.at[0, 0])
            placed.start()
            placed.wait()


def take_steps(first_step, last_step, held, outputs, given, crossed, parameters, extra, compact=False, rare=False, swap=None):
    pairs, partner, counts, own, beside = given
    images, slots, width = own.shape
    count = pairs.shape[0]
    heads = width // HEAD_DIM
    peers = lax.axis_size(AXES)
    memory = pl.BlockSpec(memory_space=pl.ANY)
    hbm = pl.BlockSpec(memory_space=pltpu.HBM)
    hidden = parameters[3].shape[1]
    flops = 2 * slots * (4 * width * width + 6 * slots * width + 2 * (width * width + 2 * width * hidden + hidden * width))
    operands = (pairs, partner, counts, own, beside, *crossed, *parameters)
    fixed = len(operands)
    chained = [(i, a) for i, a in enumerate((*held, *(o[0] for o in outputs))) if a is not None]
    aliases = {fixed + n: i for n, (i, _) in enumerate(chained)}
    passed = fixed + len(chained) + len(extra)
    shapes = [
        jax.ShapeDtypeStruct((count, 2, slots, width), BF16),
        jax.ShapeDtypeStruct((images, slots, width), F32),
    ] + [jax.ShapeDtypeStruct((o[1], slots, width), BF16) for o in outputs]
    sizes = {
        "crossed": len(crossed),
        "outputs": len(outputs),
        "skips": [o[2] for o in outputs],
        "lows": [o[3] for o in outputs],
        "highs": [o[4] for o in outputs],
        "compact": compact,
        "rare": rare,
        "swap": swap,
    }

    def body(*refs):
        group_kernel(first_step, last_step, images, peers, sizes, refs[:fixed] + refs[passed:])

    return pl.pallas_call(
        body,
        in_specs=[hbm] * 3 + [memory] * (2 + len(crossed)) + [hbm] * len(parameters) + [memory] * (len(chained) + len(extra)),
        out_specs=[memory] * len(shapes),
        out_shape=shapes,
        scratch_shapes=[
            pltpu.SMEM(pairs.shape, jnp.int32),
            pltpu.SMEM(partner.shape, jnp.int32),
            pltpu.SMEM(counts.shape, jnp.int32),
            *(pltpu.VMEM(p.shape, p.dtype) for p in parameters),
            pltpu.VMEM((2, 2, slots, width), BF16),
            pltpu.VMEM((heads, slots, width), BF16),
            pltpu.VMEM((2, slots, width), BF16),
            pltpu.VMEM((2, heads, slots, 2 * LANES), BF16),
            pltpu.VMEM((slots, slots), BF16),
            pltpu.VMEM((slots, slots), BF16),
            pltpu.VMEM((heads // 2, slots, 2 * LANES), F32),
            pltpu.VMEM((heads // 2, slots, 2 * LANES), F32),
            pltpu.VMEM((slots, width), BF16),
            pltpu.VMEM((slots, width), BF16),
            pltpu.VMEM((2, 2, slots, width), BF16),
            pltpu.VMEM((2, slots, width), F32),
            pltpu.VMEM((2, slots, width), BF16),
            pltpu.SemaphoreType.DMA((2, 2)),
            pltpu.SemaphoreType.DMA((2, 4)),
            pltpu.SemaphoreType.DMA((12,)),
        ],
        input_output_aliases=aliases,
        compiler_params=pltpu.CompilerParams(vmem_limit_bytes=67043328),
        cost_estimate=pl.CostEstimate(
            flops=1000 if rare else flops * (last_step - first_step), bytes_accessed=8 * slots * width * 2, transcendentals=slots * slots * heads
        ),
        name=f"steps_{first_step}",
    )(*operands, *(a for _, a in chained), *extra)


def pack(partner, own, split):
    images, slots, width = own.shape
    count = partner.shape[0]
    memory = pl.BlockSpec(memory_space=pl.ANY)

    def body(hbm_pairs, source, early, late, pairs, buffer, semaphores):
        fetch_scalars((hbm_pairs,), (pairs,), semaphores)
        base = lax.axis_index(AXES) * images
        sent = ranks(pairs, count, base, images)
        loads, stores = ([], [])
        for turn in range(images - 1):
            image = sum(jnp.where(rank == turn, i, 0) for i, rank in enumerate(sent))
            loads.append(pltpu.make_async_copy(source.at[image], buffer.at[turn], semaphores.at[1 + turn]))
            target = early.at[turn] if turn < split else late.at[turn - split]
            stores.append(pltpu.make_async_copy(buffer.at[turn], target, semaphores.at[1 + images + turn]))
        for move in loads:
            move.start()
        for one, two in zip(loads, stores):
            one.wait()
            two.start()
        for move in stores:
            move.wait()

    return pl.pallas_call(
        body,
        in_specs=[memory] * 2,
        out_specs=[memory] * 2,
        out_shape=[jax.ShapeDtypeStruct((n, slots, width), own.dtype) for n in (split, images - 1 - split)],
        scratch_shapes=[
            pltpu.SMEM(partner.shape, jnp.int32),
            pltpu.VMEM((images, slots, width), own.dtype),
            pltpu.SemaphoreType.DMA((1 + 2 * images,)),
        ],
        compiler_params=pltpu.CompilerParams(vmem_limit_bytes=67043328),
        name="pack",
    )(partner, own)


def add_kernel(entries, images, peers, refs):
    hbm_lists, _, terms = refs[:3], refs[3], refs[4 : 4 + len(entries)]
    out, pairs, beside, partner, held, buffer, copies, loads, scalars = refs[4 + len(entries) :]
    fetch_scalars(hbm_lists, (pairs, beside, partner), scalars)
    count = pairs.shape[0]
    position = lax.axis_index(AXES)
    base = position * images
    other = across(position)
    next_to = position + 1 - 2 * (position % 2)
    paired = (other >= 0) & (other < peers)
    lists = (pairs, beside, partner)
    bases = (other * images, across(next_to) * images, base)
    arranged = [arrange(p, count, b, images) for p, b in zip(lists, bases)]
    swapped = paired & ((arranged[0][2] == 0) | (arranged[2][2] == 0))
    targets = []
    for source, step in entries:
        row, valid, hit = chosen(arranged[source], count, jnp.int32(1 if step > count else step))
        if source == 2:
            valid = valid & paired
            if step == 1:
                valid = valid & jnp.logical_not(swapped)
            if step == count + 1:
                row, valid = (count - 1, paired & (arranged[2][2] == 0))
            if step == count + 2:
                valid = valid & hit & swapped
        target = lists[source][row, 1] - base
        targets.append(jnp.where(valid & in_place(target, 0, images), target, -1))
    slots = held.shape[1]
    tile = min(256, slots)
    touched = [sum((t == image).astype(jnp.int32) for t in targets) > 0 for image in range(images)]
    for image in range(images):
        @pl.when(touched[image])
        def _():
            pltpu.make_async_copy(out.at[image], held.at[image], copies.at[image]).start()

    for number, (term, target) in enumerate(zip(terms, targets)):
        @pl.when(target >= 0)
        def _():
            pltpu.make_async_copy(term, buffer.at[number], loads.at[number]).start()

    for image in range(images):
        @pl.when(touched[image])
        def _():
            pltpu.make_async_copy(out.at[image], held.at[image], copies.at[image]).wait()

            def one_term(number, carry):
                @pl.when(pick(targets, number) == image)
                def _():
                    pltpu.make_async_copy(terms[0], buffer.at[number], loads.at[number]).wait()

                    def one(index, inner):
                        rows = rows_of(index, tile)
                        held[image, rows, :] += buffer[number, rows, :].astype(F32)
                        return inner

                    lax.fori_loop(0, slots // tile, one, 0)

                return carry

            lax.fori_loop(0, len(entries), one_term, 0)
            pltpu.make_async_copy(held.at[image], out.at[image], copies.at[image]).start()

    for image in range(images):
        @pl.when(touched[image])
        def _():
            pltpu.make_async_copy(held.at[image], out.at[image], copies.at[image]).wait()


def add_updates(groups, totals, pairs, beside, partner, limit):
    images, slots, width = totals.shape
    entries = [entry for order, _ in groups for entry in order]
    buffers = [buffer for _, buffer in groups]
    memory = pl.BlockSpec(memory_space=pl.ANY)
    peers = lax.axis_size(AXES)
    split = 4 + len(buffers)

    def body(*refs):
        terms = [ref.at[i] for ref in refs[4:split] for i in range(ref.shape[0])]
        add_kernel(entries, images, peers, (*refs[:4], *terms, *refs[split:]))

    return pl.pallas_call(
        body,
        in_specs=[memory] * split,
        out_specs=memory,
        out_shape=jax.ShapeDtypeStruct(totals.shape, F32),
        scratch_shapes=[
            *(pltpu.SMEM(p.shape, jnp.int32) for p in (pairs, beside, partner)),
            pltpu.VMEM(totals.shape, F32),
            pltpu.VMEM((len(entries), slots, width), BF16),
            pltpu.SemaphoreType.DMA((images,)),
            pltpu.SemaphoreType.DMA((len(entries),)),
            pltpu.SemaphoreType.DMA((3,)),
        ],
        input_output_aliases={3: 0},
        compiler_params=pltpu.CompilerParams(vmem_limit_bytes=limit),
        cost_estimate=pl.CostEstimate(flops=1000, bytes_accessed=totals.size * 4, transcendentals=0),
        name=f"add_{len(entries)}",
    )(pairs, beside, partner, totals, *buffers)


def local(descriptors, key_counts, pair_list, w_qk, w_value, w_out, w_up, b_up, ln_gain, ln_bias, w_down, b_down):
    images, slots, width = descriptors.shape
    count = pair_list.shape[0]
    peers = lax.axis_size(AXES)
    on_chip = [(i, i + 1 - 2 * (i % 2)) for i in range(peers)]
    off_chip = [(i, i + 1) for i in range(1, peers - 1, 2)]
    off_chip = off_chip + [(j, i) for i, j in off_chip]
    partner = lax.ppermute(pair_list, AXES, off_chip)
    beside_list = lax.ppermute(pair_list, AXES, on_chip)
    beside = lax.ppermute(descriptors, AXES, on_chip)
    parameters = (
        w_qk, w_value, w_out, w_up, b_up[None, :], ln_gain[None, :], ln_bias[None, :], w_down, b_down[None, :],
    )
    split = (images + 1) // 2
    crossed = [lax.ppermute(x, AXES, off_chip) for x in pack(partner, descriptors, split)]
    given = (pair_list, partner, key_counts, descriptors, beside)
    middle = split + 1
    states, totals, near = take_steps(
        0, 1, (None, None), [(None, middle, 0, 0, 1)], given, [], parameters, [beside_list], compact=True
    )
    states, totals, near, far = take_steps(
        1, middle, (states, totals), [(near, middle, 1, 1, middle), (None, split, 0, 1, middle)],
        given, crossed[:1], parameters, [], swap=1,
    )
    near_back = lax.ppermute(near, AXES, on_chip)
    far_back = lax.ppermute(far, AXES, off_chip)
    states, totals, last = take_steps(
        middle, count, (states, totals), [(None, count - middle, 0, middle, count)], given, crossed, parameters, []
    )
    last_near = lax.ppermute(last, AXES, on_chip)
    last_far = lax.ppermute(last, AXES, off_chip)
    states, totals, repeat = take_steps(
        count, count + 3, (states, totals), [(None, 2, 0, count + 1, count + 3)],
        given, [*crossed, far_back], parameters, [], rare=True,
    )
    early = [
        ([(0, s) for s in range(middle)], near),
        ([(0, s) for s in range(middle, count)], last),
        ([(2, count + 1), (2, count + 2)], repeat),
        ([(1, s) for s in range(middle)], near_back),
        ([(2, s) for s in range(1, middle)], far_back),
    ]
    late = [
        ([(1, s) for s in range(middle, count)], last_near),
        ([(2, s) for s in range(middle, count)], last_far),
    ]
    totals = add_updates(early, totals, pair_list, beside_list, partner, 67043328)
    totals = add_updates(late, totals, pair_list, beside_list, partner, 16 * 1024 * 1024)
    return (states, totals)


def solution(mesh):
    in_specs = (P(AXES, None, None), P(), P(AXES, None)) + (P(),) * 9
    out_specs = (P(AXES, None, None, None), P(AXES, None, None))
    return jax.shard_map(local, mesh=mesh, in_specs=in_specs, out_specs=out_specs, check_vma=False)
```

```python
import jax
import jax.numpy as jnp
from jax import lax
from jax.experimental import pallas as pl
from jax.experimental.pallas import tpu as pltpu
from jax.sharding import PartitionSpec as P

HEAD_DIM = 64
LANES = 128
F32 = jnp.float32
BF16 = jnp.bfloat16
LOG2E = 1.4426950408889634
AXES = ("photo", "worker")
EXPONENT_BOUND = 96.0
VALUE_BOUND = 2.0**18


def dot(a, b):
    return jnp.dot(a, b, preferred_element_type=F32)


def dot_rows(a, b):
    return lax.dot_general(a, b, (((1,), (1,)), ((), ())), preferred_element_type=F32)


def dot_columns(a, b):
    return lax.dot_general(a, b, (((0,), (0,)), ((), ())), preferred_element_type=F32)


def rows_of(index, size):
    return pl.ds(pl.multiple_of(index * size, size), size)


def refine(start, message, w_out, w_up, b_up, ln_gain, ln_bias, w_down, b_down):
    width = start.shape[1]
    sent = dot(message, w_out[...]).astype(BF16)
    hidden = dot(start, w_up[:width, :]) + dot(sent, w_up[width:, :]) + b_up[...]
    center = jnp.mean(hidden, axis=-1, keepdims=True)
    shifted = hidden - center
    spread = jnp.mean(shifted * shifted, axis=-1, keepdims=True)
    normed = shifted * lax.rsqrt(spread + 1e-05) * ln_gain[...] + ln_bias[...]
    act = (0.5 * normed * (1.0 + lax.erf(normed * (0.5**0.5)))).astype(BF16)
    return dot(act, w_down[...]) + b_down[...]


def across(position):
    return jnp.where(position % 2 == 1, position + 1, position - 1)


def arrange(pairs, count, base, images):
    hits = [(pairs[s, 1] >= base) & (pairs[s, 1] < base + images) for s in range(count)]
    hits = [h.astype(jnp.int32) for h in hits]
    inside = count - sum(hits)
    places, seen_in, seen_out = ([], jnp.int32(0), jnp.int32(0))
    for hit in hits:
        places.append(jnp.where(hit == 1, inside + seen_out, seen_in))
        seen_out = seen_out + hit
        seen_in = seen_in + 1 - hit
    return (hits, places, inside)


def chosen(arranged, count, step):
    hits, places, inside = arranged
    turn = jnp.where(step == 0, 0, step - 1 + jnp.minimum(inside, 1))
    exists = jnp.where(step == 0, inside > 0, turn < count)
    row = sum(jnp.where(p == turn, s, 0) for s, p in enumerate(places))
    hit = sum(jnp.where(p == turn, h, 0) for h, p in zip(hits, places))
    return (row, exists, hit == 1)


def ranks(pairs, count, base, images):
    firsts = []
    for image in range(images):
        first = jnp.int32(count + image)
        for slot in reversed(range(count)):
            first = jnp.where(pairs[slot, 1] == base + image, slot, first)
        firsts.append(first)
    return [sum((other < first).astype(jnp.int32) for other in firsts) for first in firsts]


def pick(values, index):
    return sum(jnp.where(index == i, v, 0) for i, v in enumerate(values))


def in_place(index, low, length):
    return (index >= low) & (index < low + length)


def fetch_scalars(sources, targets, semaphores):
    moves = [pltpu.make_async_copy(s, t, semaphores.at[i]) for i, (s, t) in enumerate(zip(sources, targets))]
    for move in moves:
        move.start()
    for move in moves:
        move.wait()


def group_kernel(first_step, last_step, images, peers, sizes, refs):
    refs = list(refs)
    take = lambda n: [refs.pop(0) for _ in range(n)]
    hbm_pairs, hbm_partner, hbm_counts, own, beside = take(5)
    crossed = take(sizes["crossed"])
    parameters = take(9)
    states, totals = take(2)
    outputs = take(sizes["outputs"])
    pairs, partner, counts = take(3)
    held_parameters = take(9)
    (
        x_both, q_first, k_both, v_both,
        weights_even, weights_odd, sum_first, sum_second, m_first, m_second,
        new_states, new_delta, new_update, loads, sends, others,
    ) = refs
    w_qk, w_value, w_out, w_up, b_up, ln_gain, ln_bias, w_down, b_down = held_parameters
    slots, width = x_both.shape[2:]
    k_second, v_first, v_second = (k_both.at[1], v_both.at[0], v_both.at[1])
    heads = width // HEAD_DIM
    count = pairs.shape[0]
    steps = last_step - first_step
    moves = [pltpu.make_async_copy(s, t, others.at[i]) for i, (s, t) in enumerate(zip(parameters, held_parameters))]
    for move in moves:
        move.start()
    fetch_scalars((hbm_pairs, hbm_partner, hbm_counts), (pairs, partner, counts), others.at[pl.ds(9, 3)])
    position = lax.axis_index(AXES)
    base = position * images
    beside_base = (position + 1 - 2 * (position % 2)) * images
    other = across(position)
    other_base = other * images
    paired = (other >= 0) & (other < peers)
    arranged = arrange(pairs, count, other_base, images)
    sent = ranks(pairs, count, other_base, images)
    theirs = arrange(partner, count, base, images)
    swapped = paired & ((arranged[2] == 0) | (theirs[2] == 0))

    def describe(step):
        row, exists, _ = chosen(arranged, count, step)
        first = base + jnp.clip(pairs[row, 0] - base, 0, images - 1)
        second = pairs[row, 1]
        if sizes["rare"]:
            lost, present, hit = chosen(theirs, count, jnp.int32(1))
            again = step > count
            line = jnp.where(step == count + 1, count - 1, lost)
            exists = jnp.where(step == count + 1, paired & (theirs[2] == 0), exists)
            exists = jnp.where(step == count + 2, swapped & present & hit, exists)
            first = jnp.where(again, other_base + jnp.clip(partner[line, 0] - other_base, 0, images - 1), first)
            second = jnp.where(again, partner[line, 1], second)
        return (row, exists, first, second)

    def load(image, held, semaphore):
        for source, low in ((own, base), (beside, beside_base)):
            @pl.when(in_place(image, low, images))
            def _():
                pltpu.make_async_copy(source.at[jnp.clip(image - low, 0, images - 1)], held, semaphore).start()

        rank = jnp.where(in_place(image, other_base, images), pick(sent, image - other_base), -1)
        offset = 0
        for source in crossed:
            length = source.shape[0]

            @pl.when(in_place(rank, offset, length))
            def _():
                pltpu.make_async_copy(source.at[jnp.clip(rank - offset, 0, length - 1)], held, semaphore).start()

            offset += length

    def fetch(step, turn):
        _, exists, first, second = describe(step)

        @pl.when(exists)
        def _():
            load(first, x_both.at[turn, 0], loads.at[turn, 0])
            load(second, x_both.at[turn, 1], loads.at[turn, 1])

    def refined(start, message):
        return refine(start, message, w_out, w_up, b_up, ln_gain, ln_bias, w_down, b_down)

    def unshifted(first, second, one, two, now):
        count_first = counts[first]
        count_second = counts[second]
        block = min(512, slots) if sizes["compact"] else slots
        lane = lax.broadcasted_iota(jnp.int32, (block, LANES), 1)
        line = lax.broadcasted_iota(jnp.int32, (block, LANES), 0)
        halves = (lane < HEAD_DIM, lane >= HEAD_DIM)
        def project(index, bounds):
            rows = rows_of(index, block)
            scaled = dot(one[rows, :], w_qk[...]) * (HEAD_DIM**-0.5 * LOG2E)
            key = dot(two[rows, :], w_qk[...])
            k_second[rows, :] = key.astype(BF16)
            value_one = dot(one[rows, :], w_value[...])
            value_two = dot(two[rows, :], w_value[...])
            empty = jnp.zeros((block, LANES), BF16)
            for head in range(heads):
                start = head * HEAD_DIM // LANES * LANES
                columns = slice(start, start + LANES)
                half = halves[head % 2]
                for gap in range(0, width, LANES):
                    if gap != start:
                        q_first[head, rows, gap : gap + LANES] = empty
                q_first[head, rows, columns] = jnp.where(half, scaled[:, columns], 0.0).astype(BF16)
                for value, held, limit in ((value_one, v_first, count_first), (value_two, v_second, count_second)):
                    valid = half & (line + index * block < limit)
                    held[head, rows, :LANES] = jnp.where(valid, value[:, columns], 0.0).astype(BF16)
                    held[head, rows, LANES:] = jnp.where(valid, 1.0, 0.0).astype(BF16)
            found = (
                jnp.max(jnp.sum(scaled * scaled, axis=-1, keepdims=True)),
                jnp.max(jnp.sum(key * key, axis=-1, keepdims=True)),
                jnp.max(jnp.maximum(jnp.abs(value_one), jnp.abs(value_two))),
            )
            return tuple(jnp.maximum(a, b) for a, b in zip(bounds, found))

        zero = jnp.float32(0.0)
        query_norm, key_norm, largest = lax.fori_loop(0, slots // block, project, (zero, zero, zero))
        tile = min(256, slots)
        weights = (weights_even, weights_odd)

        def score(head):
            for start in range(0, slots, tile):
                scores = dot_rows(q_first[head], k_second[start : start + tile, :])
                weights[head % 2][:, start : start + tile] = jnp.exp2(scores).astype(BF16)

        def mix(head):
            group = head // 2
            part_first = dot(weights[head % 2][...], v_second[head])
            part_second = dot_columns(weights[head % 2][...], v_first[head])
            if head % 2 == 0:
                sum_first[group] = part_first
                sum_second[group] = part_second
            else:
                sum_first[group] += part_first
                sum_second[group] += part_second

        score(0)
        for head in range(1, heads):
            score(head)
            mix(head - 1)
        mix(heads - 1)
        for group in range(heads // 2):
            columns = slice(group * LANES, (group + 1) * LANES)
            for total, message in ((sum_first, m_first), (sum_second, m_second)):
                message[:, columns] = (total[group, :, :LANES] / total[group, :, LANES:]).astype(BF16)
        def finish(index, carry):
            rows = rows_of(index, block)
            for side, start, message in ((1, two, m_second), (0, one, m_first)):
                here = start[rows, :]
                change = refined(here, message[rows, :])
                new_states[now, side, rows, :] = (here.astype(F32) + change).astype(BF16)
                if side == 1:
                    new_update[now, rows, :] = change.astype(BF16)
                else:
                    new_delta[now, rows, :] = change
            return carry

        lax.fori_loop(0, slots // block, finish, 0)
        return (query_norm * key_norm <= EXPONENT_BOUND**2) & (largest <= VALUE_BOUND)

    def shifted(first, second, now):
        tile = min(16, slots)
        spot = lax.broadcasted_iota(jnp.int32, (tile, slots), 1)
        column = lax.broadcasted_iota(jnp.int32, (tile, width), 1)

        def fill(index, carry):
            rows = rows_of(index, tile)
            k_both[0, rows, :] = dot(x_both[now, 0, rows, :], w_qk[...]).astype(BF16)
            if sizes["rare"]:
                k_both[1, rows, :] = dot(x_both[now, 1, rows, :], w_qk[...]).astype(BF16)
                lane = lax.broadcasted_iota(jnp.int32, (tile, LANES), 1)
                for side in range(2):
                    value = dot(x_both[now, side, rows, :], w_value[...])
                    for head in range(heads):
                        start = head * HEAD_DIM // LANES * LANES
                        half = (lane >= HEAD_DIM) == (head % 2 == 1)
                        part = jnp.where(half, value[:, start : start + LANES], 0.0)
                        v_both[side, head, rows, :LANES] = part.astype(BF16)
            return carry

        lax.fori_loop(0, slots // tile, fill, 0)

        def attend(index, carry):
            side = index % 2
            rows = rows_of(index // 2, tile)
            limit = jnp.where(side == 0, counts[second], counts[first])
            query_rows = k_both[side, rows, :].astype(F32)

            def one_head(head, parts):
                query = jnp.where(column // HEAD_DIM == head, query_rows, 0.0).astype(BF16)
                scores = dot_rows(query, k_both[1 - side]) * HEAD_DIM**-0.5
                scores = jnp.where(spot < limit, scores, -jnp.inf)
                scores = jnp.exp(scores - jnp.max(scores, axis=-1, keepdims=True))
                scores = scores / jnp.sum(scores, axis=-1, keepdims=True)
                part = dot(scores.astype(BF16), v_both[1 - side, head, :, :LANES])
                return tuple(p + jnp.where(head // 2 == i, part, 0.0) for i, p in enumerate(parts))

            nothing = jnp.zeros((tile, LANES), F32)
            parts = lax.fori_loop(0, heads, one_head, (nothing,) * (heads // 2))
            here = x_both[now, side, rows, :]
            change = refined(here, jnp.concatenate(parts, axis=-1).astype(BF16))
            new_states[now, side, rows, :] = (here.astype(F32) + change).astype(BF16)

            @pl.when(side == 1)
            def _():
                new_update[now, rows, :] = change.astype(BF16)

            @pl.when(side == 0)
            def _():
                new_delta[now, rows, :] = change

            return carry

        lax.fori_loop(0, 2 * (slots // tile), attend, 0)

    def deliver(step, now, begin):
        row, exists, first, _ = describe(step)

        @pl.when(exists)
        def _():
            for slot, (output, low, high) in enumerate(zip(outputs, sizes["lows"], sizes["highs"])):
                @pl.when(in_place(step, low, high - low))
                def _():
                    place = jnp.clip(step - low + sizes["skips"][slot], 0, output.shape[0] - 1)
                    move = pltpu.make_async_copy(new_update.at[now], output.at[place], sends.at[now, slot])
                    move.start() if begin else move.wait()

            @pl.when(step <= count)
            def _():
                place = jnp.clip(first - base, 0, images - 1)
                for move in (
                    pltpu.make_async_copy(new_states.at[now], states.at[row], sends.at[now, 2]),
                    pltpu.make_async_copy(new_delta.at[now], totals.at[place], sends.at[now, 3]),
                ):
                    move.start() if begin else move.wait()

    def one_step(turn, carry):
        step = first_step + turn
        now = turn % 2
        _, exists, first, second = describe(step)
        one, two = (x_both.at[now, 0], x_both.at[now, 1])

        @pl.when(exists)
        def _():
            pltpu.make_async_copy(own.at[0], one, loads.at[now, 0]).wait()
            pltpu.make_async_copy(own.at[0], two, loads.at[now, 1]).wait()

        if steps > 1:
            @pl.when(turn + 1 < steps)
            def _():
                fetch(step + 1, (turn + 1) % 2)

        @pl.when(turn == 0)
        def _():
            for move in moves:
                move.wait()

        @pl.when(exists)
        def _():
            if sizes["rare"]:
                shifted(first, second, now)
            else:
                in_range = unshifted(first, second, one, two, now)

                @pl.when(jnp.logical_not(in_range))
                def _():
                    shifted(first, second, now)

        deliver(step, now, True)
        if steps > 1:
            @pl.when(turn > 0)
            def _():
                deliver(step - 1, 1 - now, False)

        return carry

    fetch(first_step, 0)
    lax.fori_loop(0, steps, one_step, 0)
    deliver(jnp.int32(last_step - 1), (steps - 1) % 2, False)
    if sizes["swap"] is not None:
        @pl.when(swapped)
        def _():
            order = ranks(partner, count, base, images)
            image = sum(jnp.where(rank == images - 1, i, 0) for i, rank in enumerate(order))
            fetched = pltpu.make_async_copy(own.at[image], x_both.at[0, 0], loads.at[0, 0])
            fetched.start()
            fetched.wait()
            placed = pltpu.make_async_copy(x_both.at[0, 0], outputs[sizes["swap"]].at[0], loads.at[0, 0])
            placed.start()
            placed.wait()


def take_steps(first_step, last_step, held, outputs, given, crossed, parameters, extra, compact=False, rare=False, swap=None):
    pairs, partner, counts, own, beside = given
    images, slots, width = own.shape
    count = pairs.shape[0]
    heads = width // HEAD_DIM
    peers = lax.axis_size(AXES)
    memory = pl.BlockSpec(memory_space=pl.ANY)
    hbm = pl.BlockSpec(memory_space=pltpu.HBM)
    hidden = parameters[3].shape[1]
    flops = 2 * slots * (4 * width * width + 6 * slots * width + 2 * (width * width + 2 * width * hidden + hidden * width))
    operands = (pairs, partner, counts, own, beside, *crossed, *parameters)
    fixed = len(operands)
    chained = [(i, a) for i, a in enumerate((*held, *(o[0] for o in outputs))) if a is not None]
    aliases = {fixed + n: i for n, (i, _) in enumerate(chained)}
    passed = fixed + len(chained) + len(extra)
    shapes = [
        jax.ShapeDtypeStruct((count, 2, slots, width), BF16),
        jax.ShapeDtypeStruct((images, slots, width), F32),
    ] + [jax.ShapeDtypeStruct((o[1], slots, width), BF16) for o in outputs]
    sizes = {
        "crossed": len(crossed),
        "outputs": len(outputs),
        "skips": [o[2] for o in outputs],
        "lows": [o[3] for o in outputs],
        "highs": [o[4] for o in outputs],
        "compact": compact,
        "rare": rare,
        "swap": swap,
    }

    def body(*refs):
        group_kernel(first_step, last_step, images, peers, sizes, refs[:fixed] + refs[passed:])

    return pl.pallas_call(
        body,
        in_specs=[hbm] * 3 + [memory] * (2 + len(crossed)) + [hbm] * len(parameters) + [memory] * (len(chained) + len(extra)),
        out_specs=[memory] * len(shapes),
        out_shape=shapes,
        scratch_shapes=[
            pltpu.SMEM(pairs.shape, jnp.int32),
            pltpu.SMEM(partner.shape, jnp.int32),
            pltpu.SMEM(counts.shape, jnp.int32),
            *(pltpu.VMEM(p.shape, p.dtype) for p in parameters),
            pltpu.VMEM((2, 2, slots, width), BF16),
            pltpu.VMEM((heads, slots, width), BF16),
            pltpu.VMEM((2, slots, width), BF16),
            pltpu.VMEM((2, heads, slots, 2 * LANES), BF16),
            pltpu.VMEM((slots, slots), BF16),
            pltpu.VMEM((slots, slots), BF16),
            pltpu.VMEM((heads // 2, slots, 2 * LANES), F32),
            pltpu.VMEM((heads // 2, slots, 2 * LANES), F32),
            pltpu.VMEM((slots, width), BF16),
            pltpu.VMEM((slots, width), BF16),
            pltpu.VMEM((2, 2, slots, width), BF16),
            pltpu.VMEM((2, slots, width), F32),
            pltpu.VMEM((2, slots, width), BF16),
            pltpu.SemaphoreType.DMA((2, 2)),
            pltpu.SemaphoreType.DMA((2, 4)),
            pltpu.SemaphoreType.DMA((12,)),
        ],
        input_output_aliases=aliases,
        compiler_params=pltpu.CompilerParams(vmem_limit_bytes=67043328),
        cost_estimate=pl.CostEstimate(
            flops=1000 if rare else flops * (last_step - first_step), bytes_accessed=8 * slots * width * 2, transcendentals=slots * slots * heads
        ),
        name=f"steps_{first_step}",
    )(*operands, *(a for _, a in chained), *extra)


def pack(partner, own, split):
    images, slots, width = own.shape
    count = partner.shape[0]
    memory = pl.BlockSpec(memory_space=pl.ANY)

    def body(hbm_pairs, source, early, late, pairs, buffer, semaphores):
        fetch_scalars((hbm_pairs,), (pairs,), semaphores)
        base = lax.axis_index(AXES) * images
        sent = ranks(pairs, count, base, images)
        loads, stores = ([], [])
        for turn in range(images - 1):
            image = sum(jnp.where(rank == turn, i, 0) for i, rank in enumerate(sent))
            loads.append(pltpu.make_async_copy(source.at[image], buffer.at[turn], semaphores.at[1 + turn]))
            target = early.at[turn] if turn < split else late.at[turn - split]
            stores.append(pltpu.make_async_copy(buffer.at[turn], target, semaphores.at[1 + images + turn]))
        for move in loads:
            move.start()
        for one, two in zip(loads, stores):
            one.wait()
            two.start()
        for move in stores:
            move.wait()

    return pl.pallas_call(
        body,
        in_specs=[memory] * 2,
        out_specs=[memory] * 2,
        out_shape=[jax.ShapeDtypeStruct((n, slots, width), own.dtype) for n in (split, images - 1 - split)],
        scratch_shapes=[
            pltpu.SMEM(partner.shape, jnp.int32),
            pltpu.VMEM((images, slots, width), own.dtype),
            pltpu.SemaphoreType.DMA((1 + 2 * images,)),
        ],
        compiler_params=pltpu.CompilerParams(vmem_limit_bytes=67043328),
        name="pack",
    )(partner, own)


def add_kernel(entries, images, peers, refs):
    hbm_lists, _, terms = refs[:3], refs[3], refs[4 : 4 + len(entries)]
    out, pairs, beside, partner, held, buffer, copies, loads, scalars = refs[4 + len(entries) :]
    fetch_scalars(hbm_lists, (pairs, beside, partner), scalars)
    count = pairs.shape[0]
    position = lax.axis_index(AXES)
    base = position * images
    other = across(position)
    next_to = position + 1 - 2 * (position % 2)
    paired = (other >= 0) & (other < peers)
    lists = (pairs, beside, partner)
    bases = (other * images, across(next_to) * images, base)
    arranged = [arrange(p, count, b, images) for p, b in zip(lists, bases)]
    swapped = paired & ((arranged[0][2] == 0) | (arranged[2][2] == 0))
    targets = []
    for source, step in entries:
        row, valid, hit = chosen(arranged[source], count, jnp.int32(1 if step > count else step))
        if source == 2:
            valid = valid & paired
            if step == 1:
                valid = valid & jnp.logical_not(swapped)
            if step == count + 1:
                row, valid = (count - 1, paired & (arranged[2][2] == 0))
            if step == count + 2:
                valid = valid & hit & swapped
        target = lists[source][row, 1] - base
        targets.append(jnp.where(valid & in_place(target, 0, images), target, -1))
    slots = held.shape[1]
    tile = min(256, slots)
    touched = [sum((t == image).astype(jnp.int32) for t in targets) > 0 for image in range(images)]
    for image in range(images):
        @pl.when(touched[image])
        def _():
            pltpu.make_async_copy(out.at[image], held.at[image], copies.at[image]).start()

    for number, (term, target) in enumerate(zip(terms, targets)):
        @pl.when(target >= 0)
        def _():
            pltpu.make_async_copy(term, buffer.at[number], loads.at[number]).start()

    for image in range(images):
        @pl.when(touched[image])
        def _():
            pltpu.make_async_copy(out.at[image], held.at[image], copies.at[image]).wait()

            def one_term(number, carry):
                @pl.when(pick(targets, number) == image)
                def _():
                    pltpu.make_async_copy(terms[0], buffer.at[number], loads.at[number]).wait()

                    def one(index, inner):
                        rows = rows_of(index, tile)
                        held[image, rows, :] += buffer[number, rows, :].astype(F32)
                        return inner

                    lax.fori_loop(0, slots // tile, one, 0)

                return carry

            lax.fori_loop(0, len(entries), one_term, 0)
            pltpu.make_async_copy(held.at[image], out.at[image], copies.at[image]).start()

    for image in range(images):
        @pl.when(touched[image])
        def _():
            pltpu.make_async_copy(held.at[image], out.at[image], copies.at[image]).wait()


def add_updates(groups, totals, pairs, beside, partner, limit):
    images, slots, width = totals.shape
    entries = [entry for order, _ in groups for entry in order]
    buffers = [buffer for _, buffer in groups]
    memory = pl.BlockSpec(memory_space=pl.ANY)
    peers = lax.axis_size(AXES)
    split = 4 + len(buffers)

    def body(*refs):
        terms = [ref.at[i] for ref in refs[4:split] for i in range(ref.shape[0])]
        add_kernel(entries, images, peers, (*refs[:4], *terms, *refs[split:]))

    return pl.pallas_call(
        body,
        in_specs=[memory] * split,
        out_specs=memory,
        out_shape=jax.ShapeDtypeStruct(totals.shape, F32),
        scratch_shapes=[
            *(pltpu.SMEM(p.shape, jnp.int32) for p in (pairs, beside, partner)),
            pltpu.VMEM(totals.shape, F32),
            pltpu.VMEM((len(entries), slots, width), BF16),
            pltpu.SemaphoreType.DMA((images,)),
            pltpu.SemaphoreType.DMA((len(entries),)),
            pltpu.SemaphoreType.DMA((3,)),
        ],
        input_output_aliases={3: 0},
        compiler_params=pltpu.CompilerParams(vmem_limit_bytes=limit),
        cost_estimate=pl.CostEstimate(flops=1000, bytes_accessed=totals.size * 4, transcendentals=0),
        name=f"add_{len(entries)}",
    )(pairs, beside, partner, totals, *buffers)


def local(descriptors, key_counts, pair_list, w_qk, w_value, w_out, w_up, b_up, ln_gain, ln_bias, w_down, b_down):
    images, slots, width = descriptors.shape
    count = pair_list.shape[0]
    peers = lax.axis_size(AXES)
    on_chip = [(i, i + 1 - 2 * (i % 2)) for i in range(peers)]
    off_chip = [(i, i + 1) for i in range(1, peers - 1, 2)]
    off_chip = off_chip + [(j, i) for i, j in off_chip]
    partner = lax.ppermute(pair_list, AXES, off_chip)
    beside_list = lax.ppermute(pair_list, AXES, on_chip)
    beside = lax.ppermute(descriptors, AXES, on_chip)
    parameters = (
        w_qk, w_value, w_out, w_up, b_up[None, :], ln_gain[None, :], ln_bias[None, :], w_down, b_down[None, :],
    )
    split = (images + 1) // 2
    soon, later = pack(partner, descriptors, split)
    crossed = [lax.ppermute(soon, AXES, off_chip)]
    given = (pair_list, partner, key_counts, descriptors, beside)
    middle = split + 1
    states, totals, near = take_steps(
        0, 1, (None, None), [(None, middle, 0, 0, 1)], given, [], parameters, [beside_list], compact=True
    )
    later, near = lax.optimization_barrier((later, near))
    crossed.append(lax.ppermute(later, AXES, off_chip))
    states, totals, near, far = take_steps(
        1, middle, (states, totals), [(near, middle, 1, 1, middle), (None, split, 0, 1, middle)],
        given, crossed[:1], parameters, [], swap=1,
    )
    near_back = lax.ppermute(near, AXES, on_chip)
    far_back = lax.ppermute(far, AXES, off_chip)
    states, totals, last = take_steps(
        middle, count, (states, totals), [(None, count - middle, 0, middle, count)], given, crossed, parameters, []
    )
    last_near = lax.ppermute(last, AXES, on_chip)
    last_far = lax.ppermute(last, AXES, off_chip)
    states, totals, repeat = take_steps(
        count, count + 3, (states, totals), [(None, 2, 0, count + 1, count + 3)],
        given, [*crossed, far_back], parameters, [], rare=True,
    )
    early = [
        ([(0, s) for s in range(middle)], near),
        ([(0, s) for s in range(middle, count)], last),
        ([(2, count + 1), (2, count + 2)], repeat),
        ([(1, s) for s in range(middle)], near_back),
        ([(2, s) for s in range(1, middle)], far_back),
    ]
    late = [
        ([(1, s) for s in range(middle, count)], last_near),
        ([(2, s) for s in range(middle, count)], last_far),
    ]
    totals = add_updates(early, totals, pair_list, beside_list, partner, 67043328)
    totals = add_updates(late, totals, pair_list, beside_list, partner, 67043328)
    return (states, totals)


def solution(mesh):
    in_specs = (P(AXES, None, None), P(), P(AXES, None)) + (P(),) * 9
    out_specs = (P(AXES, None, None, None), P(AXES, None, None))
    return jax.shard_map(local, mesh=mesh, in_specs=in_specs, out_specs=out_specs, check_vma=False)
```

```python
import jax
import jax.numpy as jnp
from jax import lax
from jax.experimental import pallas as pl
from jax.experimental.pallas import tpu as pltpu
from jax.sharding import PartitionSpec as P

HEAD_DIM = 64
LANES = 128
F32 = jnp.float32
BF16 = jnp.bfloat16
LOG2E = 1.4426950408889634
AXES = ("photo", "worker")
EXPONENT_BOUND = 96.0
VALUE_BOUND = 2.0**18


def dot(a, b):
    return jnp.dot(a, b, preferred_element_type=F32)


def dot_rows(a, b):
    return lax.dot_general(a, b, (((1,), (1,)), ((), ())), preferred_element_type=F32)


def dot_columns(a, b):
    return lax.dot_general(a, b, (((0,), (0,)), ((), ())), preferred_element_type=F32)


def rows_of(index, size):
    return pl.ds(pl.multiple_of(index * size, size), size)


def refine(start, message, w_out, w_up, b_up, ln_gain, ln_bias, w_down, b_down):
    width = start.shape[1]
    sent = dot(message, w_out[...]).astype(BF16)
    hidden = dot(start, w_up[:width, :]) + dot(sent, w_up[width:, :]) + b_up[...]
    center = jnp.mean(hidden, axis=-1, keepdims=True)
    shifted = hidden - center
    spread = jnp.mean(shifted * shifted, axis=-1, keepdims=True)
    normed = shifted * lax.rsqrt(spread + 1e-05) * ln_gain[...] + ln_bias[...]
    act = (0.5 * normed * (1.0 + lax.erf(normed * (0.5**0.5)))).astype(BF16)
    return dot(act, w_down[...]) + b_down[...]


def across(position):
    return jnp.where(position % 2 == 1, position + 1, position - 1)


def arrange(pairs, count, base, images):
    hits = [(pairs[s, 1] >= base) & (pairs[s, 1] < base + images) for s in range(count)]
    hits = [h.astype(jnp.int32) for h in hits]
    inside = count - sum(hits)
    places, seen_in, seen_out = ([], jnp.int32(0), jnp.int32(0))
    for hit in hits:
        places.append(jnp.where(hit == 1, inside + seen_out, seen_in))
        seen_out = seen_out + hit
        seen_in = seen_in + 1 - hit
    return (hits, places, inside)


def chosen(arranged, count, step):
    hits, places, inside = arranged
    turn = jnp.where(step == 0, 0, step - 1 + jnp.minimum(inside, 1))
    exists = jnp.where(step == 0, inside > 0, turn < count)
    row = sum(jnp.where(p == turn, s, 0) for s, p in enumerate(places))
    hit = sum(jnp.where(p == turn, h, 0) for h, p in zip(hits, places))
    return (row, exists, hit == 1)


def ranks(pairs, count, base, images):
    firsts = []
    for image in range(images):
        first = jnp.int32(count + image)
        for slot in reversed(range(count)):
            first = jnp.where(pairs[slot, 1] == base + image, slot, first)
        firsts.append(first)
    return [sum((other < first).astype(jnp.int32) for other in firsts) for first in firsts]


def pick(values, index):
    return sum(jnp.where(index == i, v, 0) for i, v in enumerate(values))


def in_place(index, low, length):
    return (index >= low) & (index < low + length)


def fetch_scalars(sources, targets, semaphores):
    moves = [pltpu.make_async_copy(s, t, semaphores.at[i]) for i, (s, t) in enumerate(zip(sources, targets))]
    for move in moves:
        move.start()
    for move in moves:
        move.wait()


def group_kernel(first_step, last_step, images, peers, sizes, refs):
    refs = list(refs)
    take = lambda n: [refs.pop(0) for _ in range(n)]
    hbm_pairs, hbm_partner, hbm_counts, own, beside = take(5)
    crossed = take(sizes["crossed"])
    parameters = take(9)
    states, totals = take(2)
    outputs = take(sizes["outputs"])
    pairs, partner, counts = take(3)
    held_parameters = take(9)
    (
        x_both, q_first, k_both, v_both,
        weights_even, weights_odd, sum_first, sum_second, m_first, m_second,
        new_states, new_delta, new_update, loads, sends, others,
    ) = refs
    w_qk, w_value, w_out, w_up, b_up, ln_gain, ln_bias, w_down, b_down = held_parameters
    slots, width = x_both.shape[2:]
    k_second, v_first, v_second = (k_both.at[1], v_both.at[0], v_both.at[1])
    heads = width // HEAD_DIM
    count = pairs.shape[0]
    steps = last_step - first_step
    moves = [pltpu.make_async_copy(s, t, others.at[i]) for i, (s, t) in enumerate(zip(parameters, held_parameters))]
    for move in moves:
        move.start()
    fetch_scalars((hbm_pairs, hbm_partner, hbm_counts), (pairs, partner, counts), others.at[pl.ds(9, 3)])
    position = lax.axis_index(AXES)
    base = position * images
    beside_base = (position + 1 - 2 * (position % 2)) * images
    other = across(position)
    other_base = other * images
    paired = (other >= 0) & (other < peers)
    arranged = arrange(pairs, count, other_base, images)
    sent = ranks(pairs, count, other_base, images)
    theirs = arrange(partner, count, base, images)
    swapped = paired & ((arranged[2] == 0) | (theirs[2] == 0))

    def describe(step):
        row, exists, _ = chosen(arranged, count, step)
        first = base + jnp.clip(pairs[row, 0] - base, 0, images - 1)
        second = pairs[row, 1]
        if sizes["rare"]:
            lost, present, hit = chosen(theirs, count, jnp.int32(1))
            again = step > count
            line = jnp.where(step == count + 1, count - 1, lost)
            exists = jnp.where(step == count + 1, paired & (theirs[2] == 0), exists)
            exists = jnp.where(step == count + 2, swapped & present & hit, exists)
            first = jnp.where(again, other_base + jnp.clip(partner[line, 0] - other_base, 0, images - 1), first)
            second = jnp.where(again, partner[line, 1], second)
        return (row, exists, first, second)

    def load(image, held, semaphore):
        for source, low in ((own, base), (beside, beside_base)):
            @pl.when(in_place(image, low, images))
            def _():
                pltpu.make_async_copy(source.at[jnp.clip(image - low, 0, images - 1)], held, semaphore).start()

        rank = jnp.where(in_place(image, other_base, images), pick(sent, image - other_base), -1)
        offset = 0
        for source in crossed:
            length = source.shape[0]

            @pl.when(in_place(rank, offset, length))
            def _():
                pltpu.make_async_copy(source.at[jnp.clip(rank - offset, 0, length - 1)], held, semaphore).start()

            offset += length

    def fetch(step, turn):
        _, exists, first, second = describe(step)

        @pl.when(exists)
        def _():
            load(first, x_both.at[turn, 0], loads.at[turn, 0])
            load(second, x_both.at[turn, 1], loads.at[turn, 1])

    def refined(start, message):
        return refine(start, message, w_out, w_up, b_up, ln_gain, ln_bias, w_down, b_down)

    def unshifted(first, second, one, two, now):
        count_first = counts[first]
        count_second = counts[second]
        block = min(512, slots) if sizes["compact"] else slots
        lane = lax.broadcasted_iota(jnp.int32, (block, LANES), 1)
        line = lax.broadcasted_iota(jnp.int32, (block, LANES), 0)
        halves = (lane < HEAD_DIM, lane >= HEAD_DIM)
        def project(index, bounds):
            rows = rows_of(index, block)
            scaled = dot(one[rows, :], w_qk[...]) * (HEAD_DIM**-0.5 * LOG2E)
            key = dot(two[rows, :], w_qk[...])
            k_second[rows, :] = key.astype(BF16)
            value_one = dot(one[rows, :], w_value[...])
            value_two = dot(two[rows, :], w_value[...])
            empty = jnp.zeros((block, LANES), BF16)
            for head in range(heads):
                start = head * HEAD_DIM // LANES * LANES
                columns = slice(start, start + LANES)
                half = halves[head % 2]
                for gap in range(0, width, LANES):
                    if gap != start:
                        q_first[head, rows, gap : gap + LANES] = empty
                q_first[head, rows, columns] = jnp.where(half, scaled[:, columns], 0.0).astype(BF16)
                for value, held, limit in ((value_one, v_first, count_first), (value_two, v_second, count_second)):
                    valid = half & (line + index * block < limit)
                    held[head, rows, :LANES] = jnp.where(valid, value[:, columns], 0.0).astype(BF16)
                    held[head, rows, LANES:] = jnp.where(valid, 1.0, 0.0).astype(BF16)
            found = (
                jnp.max(jnp.sum(scaled * scaled, axis=-1, keepdims=True)),
                jnp.max(jnp.sum(key * key, axis=-1, keepdims=True)),
                jnp.max(jnp.maximum(jnp.abs(value_one), jnp.abs(value_two))),
            )
            return tuple(jnp.maximum(a, b) for a, b in zip(bounds, found))

        zero = jnp.float32(0.0)
        query_norm, key_norm, largest = lax.fori_loop(0, slots // block, project, (zero, zero, zero))
        tile = min(256, slots)
        weights = (weights_even, weights_odd)

        def score(head):
            for start in range(0, slots, tile):
                scores = dot_rows(q_first[head], k_second[start : start + tile, :])
                weights[head % 2][:, start : start + tile] = jnp.exp2(scores).astype(BF16)

        def mix(head):
            group = head // 2
            part_first = dot(weights[head % 2][...], v_second[head])
            part_second = dot_columns(weights[head % 2][...], v_first[head])
            if head % 2 == 0:
                sum_first[group] = part_first
                sum_second[group] = part_second
            else:
                sum_first[group] += part_first
                sum_second[group] += part_second

        score(0)
        for head in range(1, heads):
            score(head)
            mix(head - 1)
        mix(heads - 1)
        for group in range(heads // 2):
            columns = slice(group * LANES, (group + 1) * LANES)
            for total, message in ((sum_first, m_first), (sum_second, m_second)):
                message[:, columns] = (total[group, :, :LANES] / total[group, :, LANES:]).astype(BF16)
        def finish(index, carry):
            rows = rows_of(index, block)
            for side, start, message in ((1, two, m_second), (0, one, m_first)):
                here = start[rows, :]
                change = refined(here, message[rows, :])
                new_states[now, side, rows, :] = (here.astype(F32) + change).astype(BF16)
                if side == 1:
                    new_update[now, rows, :] = change.astype(BF16)
                else:
                    new_delta[now, rows, :] = change
            return carry

        lax.fori_loop(0, slots // block, finish, 0)
        return (query_norm * key_norm <= EXPONENT_BOUND**2) & (largest <= VALUE_BOUND)

    def shifted(first, second, now):
        tile = min(16, slots)
        spot = lax.broadcasted_iota(jnp.int32, (tile, slots), 1)
        column = lax.broadcasted_iota(jnp.int32, (tile, width), 1)

        def fill(index, carry):
            rows = rows_of(index, tile)
            k_both[0, rows, :] = dot(x_both[now, 0, rows, :], w_qk[...]).astype(BF16)
            if sizes["rare"]:
                k_both[1, rows, :] = dot(x_both[now, 1, rows, :], w_qk[...]).astype(BF16)
                lane = lax.broadcasted_iota(jnp.int32, (tile, LANES), 1)
                for side in range(2):
                    value = dot(x_both[now, side, rows, :], w_value[...])
                    for head in range(heads):
                        start = head * HEAD_DIM // LANES * LANES
                        half = (lane >= HEAD_DIM) == (head % 2 == 1)
                        part = jnp.where(half, value[:, start : start + LANES], 0.0)
                        v_both[side, head, rows, :LANES] = part.astype(BF16)
            return carry

        lax.fori_loop(0, slots // tile, fill, 0)

        def attend(index, carry):
            side = index % 2
            rows = rows_of(index // 2, tile)
            limit = jnp.where(side == 0, counts[second], counts[first])
            query_rows = k_both[side, rows, :].astype(F32)

            def one_head(head, parts):
                query = jnp.where(column // HEAD_DIM == head, query_rows, 0.0).astype(BF16)
                scores = dot_rows(query, k_both[1 - side]) * HEAD_DIM**-0.5
                scores = jnp.where(spot < limit, scores, -jnp.inf)
                scores = jnp.exp(scores - jnp.max(scores, axis=-1, keepdims=True))
                scores = scores / jnp.sum(scores, axis=-1, keepdims=True)
                part = dot(scores.astype(BF16), v_both[1 - side, head, :, :LANES])
                return tuple(p + jnp.where(head // 2 == i, part, 0.0) for i, p in enumerate(parts))

            nothing = jnp.zeros((tile, LANES), F32)
            parts = lax.fori_loop(0, heads, one_head, (nothing,) * (heads // 2))
            here = x_both[now, side, rows, :]
            change = refined(here, jnp.concatenate(parts, axis=-1).astype(BF16))
            new_states[now, side, rows, :] = (here.astype(F32) + change).astype(BF16)

            @pl.when(side == 1)
            def _():
                new_update[now, rows, :] = change.astype(BF16)

            @pl.when(side == 0)
            def _():
                new_delta[now, rows, :] = change

            return carry

        lax.fori_loop(0, 2 * (slots // tile), attend, 0)

    def deliver(step, now, begin):
        row, exists, first, _ = describe(step)

        @pl.when(exists)
        def _():
            for slot, (output, low, high) in enumerate(zip(outputs, sizes["lows"], sizes["highs"])):
                @pl.when(in_place(step, low, high - low))
                def _():
                    place = jnp.clip(step - low + sizes["skips"][slot], 0, output.shape[0] - 1)
                    move = pltpu.make_async_copy(new_update.at[now], output.at[place], sends.at[now, slot])
                    move.start() if begin else move.wait()

            @pl.when(step <= count)
            def _():
                place = jnp.clip(first - base, 0, images - 1)
                for move in (
                    pltpu.make_async_copy(new_states.at[now], states.at[row], sends.at[now, 2]),
                    pltpu.make_async_copy(new_delta.at[now], totals.at[place], sends.at[now, 3]),
                ):
                    move.start() if begin else move.wait()

    def one_step(turn, carry):
        step = first_step + turn
        now = turn % 2
        _, exists, first, second = describe(step)
        one, two = (x_both.at[now, 0], x_both.at[now, 1])

        @pl.when(exists)
        def _():
            pltpu.make_async_copy(own.at[0], one, loads.at[now, 0]).wait()
            pltpu.make_async_copy(own.at[0], two, loads.at[now, 1]).wait()

        if steps > 1:
            @pl.when(turn + 1 < steps)
            def _():
                fetch(step + 1, (turn + 1) % 2)

        @pl.when(turn == 0)
        def _():
            for move in moves:
                move.wait()

        @pl.when(exists)
        def _():
            if sizes["rare"]:
                shifted(first, second, now)
            else:
                in_range = unshifted(first, second, one, two, now)

                @pl.when(jnp.logical_not(in_range))
                def _():
                    shifted(first, second, now)

        deliver(step, now, True)
        if steps > 1:
            @pl.when(turn > 0)
            def _():
                deliver(step - 1, 1 - now, False)

        return carry

    fetch(first_step, 0)
    lax.fori_loop(0, steps, one_step, 0)
    deliver(jnp.int32(last_step - 1), (steps - 1) % 2, False)
    if sizes["swap"] is not None:
        @pl.when(swapped)
        def _():
            order = ranks(partner, count, base, images)
            image = sum(jnp.where(rank == images - 1, i, 0) for i, rank in enumerate(order))
            fetched = pltpu.make_async_copy(own.at[image], x_both.at[0, 0], loads.at[0, 0])
            fetched.start()
            fetched.wait()
            placed = pltpu.make_async_copy(x_both.at[0, 0], outputs[sizes["swap"]].at[0], loads.at[0, 0])
            placed.start()
            placed.wait()


def take_steps(first_step, last_step, held, outputs, given, crossed, parameters, extra, compact=False, rare=False, swap=None):
    pairs, partner, counts, own, beside = given
    images, slots, width = own.shape
    count = pairs.shape[0]
    heads = width // HEAD_DIM
    peers = lax.axis_size(AXES)
    memory = pl.BlockSpec(memory_space=pl.ANY)
    hbm = pl.BlockSpec(memory_space=pltpu.HBM)
    hidden = parameters[3].shape[1]
    flops = 2 * slots * (4 * width * width + 6 * slots * width + 2 * (width * width + 2 * width * hidden + hidden * width))
    operands = (pairs, partner, counts, own, beside, *crossed, *parameters)
    fixed = len(operands)
    chained = [(i, a) for i, a in enumerate((*held, *(o[0] for o in outputs))) if a is not None]
    aliases = {fixed + n: i for n, (i, _) in enumerate(chained)}
    passed = fixed + len(chained) + len(extra)
    shapes = [
        jax.ShapeDtypeStruct((count, 2, slots, width), BF16),
        jax.ShapeDtypeStruct((images, slots, width), F32),
    ] + [jax.ShapeDtypeStruct((o[1], slots, width), BF16) for o in outputs]
    sizes = {
        "crossed": len(crossed),
        "outputs": len(outputs),
        "skips": [o[2] for o in outputs],
        "lows": [o[3] for o in outputs],
        "highs": [o[4] for o in outputs],
        "compact": compact,
        "rare": rare,
        "swap": swap,
    }

    def body(*refs):
        group_kernel(first_step, last_step, images, peers, sizes, refs[:fixed] + refs[passed:])

    return pl.pallas_call(
        body,
        in_specs=[hbm] * 3 + [memory] * (2 + len(crossed)) + [hbm] * len(parameters) + [memory] * (len(chained) + len(extra)),
        out_specs=[memory] * len(shapes),
        out_shape=shapes,
        scratch_shapes=[
            pltpu.SMEM(pairs.shape, jnp.int32),
            pltpu.SMEM(partner.shape, jnp.int32),
            pltpu.SMEM(counts.shape, jnp.int32),
            *(pltpu.VMEM(p.shape, p.dtype) for p in parameters),
            pltpu.VMEM((2, 2, slots, width), BF16),
            pltpu.VMEM((heads, slots, width), BF16),
            pltpu.VMEM((2, slots, width), BF16),
            pltpu.VMEM((2, heads, slots, 2 * LANES), BF16),
            pltpu.VMEM((slots, slots), BF16),
            pltpu.VMEM((slots, slots), BF16),
            pltpu.VMEM((heads // 2, slots, 2 * LANES), F32),
            pltpu.VMEM((heads // 2, slots, 2 * LANES), F32),
            pltpu.VMEM((slots, width), BF16),
            pltpu.VMEM((slots, width), BF16),
            pltpu.VMEM((2, 2, slots, width), BF16),
            pltpu.VMEM((2, slots, width), F32),
            pltpu.VMEM((2, slots, width), BF16),
            pltpu.SemaphoreType.DMA((2, 2)),
            pltpu.SemaphoreType.DMA((2, 4)),
            pltpu.SemaphoreType.DMA((12,)),
        ],
        input_output_aliases=aliases,
        compiler_params=pltpu.CompilerParams(vmem_limit_bytes=67043328),
        cost_estimate=pl.CostEstimate(
            flops=1000 if rare else flops * (last_step - first_step), bytes_accessed=8 * slots * width * 2, transcendentals=slots * slots * heads
        ),
        name=f"steps_{first_step}",
    )(*operands, *(a for _, a in chained), *extra)


def pack(partner, own, split):
    images, slots, width = own.shape
    count = partner.shape[0]
    memory = pl.BlockSpec(memory_space=pl.ANY)

    def body(hbm_pairs, source, early, late, pairs, buffer, semaphores):
        loads = [
            pltpu.make_async_copy(source.at[i], buffer.at[i], semaphores.at[1 + i]) for i in range(images)
        ]
        for move in loads:
            move.start()
        fetch_scalars((hbm_pairs,), (pairs,), semaphores)
        base = lax.axis_index(AXES) * images
        sent = ranks(pairs, count, base, images)
        stores = []
        for turn in range(images - 1):
            image = sum(jnp.where(rank == turn, i, 0) for i, rank in enumerate(sent))
            target = early.at[turn] if turn < split else late.at[turn - split]
            stores.append(pltpu.make_async_copy(buffer.at[image], target, semaphores.at[1 + images + turn]))
        for move in loads:
            move.wait()
        for move in stores:
            move.start()
        for move in stores:
            move.wait()

    return pl.pallas_call(
        body,
        in_specs=[memory] * 2,
        out_specs=[memory] * 2,
        out_shape=[jax.ShapeDtypeStruct((n, slots, width), own.dtype) for n in (split, images - 1 - split)],
        scratch_shapes=[
            pltpu.SMEM(partner.shape, jnp.int32),
            pltpu.VMEM((images, slots, width), own.dtype),
            pltpu.SemaphoreType.DMA((1 + 2 * images,)),
        ],
        compiler_params=pltpu.CompilerParams(vmem_limit_bytes=67043328),
        name="pack",
    )(partner, own)


def add_kernel(entries, images, peers, refs):
    hbm_lists, _, terms = refs[:3], refs[3], refs[4 : 4 + len(entries)]
    out, pairs, beside, partner, held, buffer, copies, loads, scalars = refs[4 + len(entries) :]
    fetch_scalars(hbm_lists, (pairs, beside, partner), scalars)
    count = pairs.shape[0]
    position = lax.axis_index(AXES)
    base = position * images
    other = across(position)
    next_to = position + 1 - 2 * (position % 2)
    paired = (other >= 0) & (other < peers)
    lists = (pairs, beside, partner)
    bases = (other * images, across(next_to) * images, base)
    arranged = [arrange(p, count, b, images) for p, b in zip(lists, bases)]
    swapped = paired & ((arranged[0][2] == 0) | (arranged[2][2] == 0))
    targets = []
    for source, step in entries:
        row, valid, hit = chosen(arranged[source], count, jnp.int32(1 if step > count else step))
        if source == 2:
            valid = valid & paired
            if step == 1:
                valid = valid & jnp.logical_not(swapped)
            if step == count + 1:
                row, valid = (count - 1, paired & (arranged[2][2] == 0))
            if step == count + 2:
                valid = valid & hit & swapped
        target = lists[source][row, 1] - base
        targets.append(jnp.where(valid & in_place(target, 0, images), target, -1))
    slots = held.shape[1]
    tile = min(256, slots)
    touched = [sum((t == image).astype(jnp.int32) for t in targets) > 0 for image in range(images)]
    for image in range(images):
        @pl.when(touched[image])
        def _():
            pltpu.make_async_copy(out.at[image], held.at[image], copies.at[image]).start()

    for number, (term, target) in enumerate(zip(terms, targets)):
        @pl.when(target >= 0)
        def _():
            pltpu.make_async_copy(term, buffer.at[number], loads.at[number]).start()

    for image in range(images):
        @pl.when(touched[image])
        def _():
            pltpu.make_async_copy(out.at[image], held.at[image], copies.at[image]).wait()

            def one_term(number, carry):
                @pl.when(pick(targets, number) == image)
                def _():
                    pltpu.make_async_copy(terms[0], buffer.at[number], loads.at[number]).wait()

                    def one(index, inner):
                        rows = rows_of(index, tile)
                        held[image, rows, :] += buffer[number, rows, :].astype(F32)
                        return inner

                    lax.fori_loop(0, slots // tile, one, 0)

                return carry

            lax.fori_loop(0, len(entries), one_term, 0)
            pltpu.make_async_copy(held.at[image], out.at[image], copies.at[image]).start()

    for image in range(images):
        @pl.when(touched[image])
        def _():
            pltpu.make_async_copy(held.at[image], out.at[image], copies.at[image]).wait()


def add_updates(groups, totals, pairs, beside, partner, limit):
    images, slots, width = totals.shape
    entries = [entry for order, _ in groups for entry in order]
    buffers = [buffer for _, buffer in groups]
    memory = pl.BlockSpec(memory_space=pl.ANY)
    peers = lax.axis_size(AXES)
    split = 4 + len(buffers)

    def body(*refs):
        terms = [ref.at[i] for ref in refs[4:split] for i in range(ref.shape[0])]
        add_kernel(entries, images, peers, (*refs[:4], *terms, *refs[split:]))

    return pl.pallas_call(
        body,
        in_specs=[memory] * split,
        out_specs=memory,
        out_shape=jax.ShapeDtypeStruct(totals.shape, F32),
        scratch_shapes=[
            *(pltpu.SMEM(p.shape, jnp.int32) for p in (pairs, beside, partner)),
            pltpu.VMEM(totals.shape, F32),
            pltpu.VMEM((len(entries), slots, width), BF16),
            pltpu.SemaphoreType.DMA((images,)),
            pltpu.SemaphoreType.DMA((len(entries),)),
            pltpu.SemaphoreType.DMA((3,)),
        ],
        input_output_aliases={3: 0},
        compiler_params=pltpu.CompilerParams(vmem_limit_bytes=limit),
        cost_estimate=pl.CostEstimate(flops=1000, bytes_accessed=totals.size * 4, transcendentals=0),
        name=f"add_{len(entries)}",
    )(pairs, beside, partner, totals, *buffers)


def local(descriptors, key_counts, pair_list, w_qk, w_value, w_out, w_up, b_up, ln_gain, ln_bias, w_down, b_down):
    images, slots, width = descriptors.shape
    count = pair_list.shape[0]
    peers = lax.axis_size(AXES)
    on_chip = [(i, i + 1 - 2 * (i % 2)) for i in range(peers)]
    off_chip = [(i, i + 1) for i in range(1, peers - 1, 2)]
    off_chip = off_chip + [(j, i) for i, j in off_chip]
    partner = lax.ppermute(pair_list, AXES, off_chip)
    beside_list = lax.ppermute(pair_list, AXES, on_chip)
    beside = lax.ppermute(descriptors, AXES, on_chip)
    parameters = (
        w_qk, w_value, w_out, w_up, b_up[None, :], ln_gain[None, :], ln_bias[None, :], w_down, b_down[None, :],
    )
    split = (images + 1) // 2
    soon, later = pack(partner, descriptors, split)
    crossed = [lax.ppermute(soon, AXES, off_chip)]
    given = (pair_list, partner, key_counts, descriptors, beside)
    middle = split + 1
    states, totals, near = take_steps(
        0, 1, (None, None), [(None, middle, 0, 0, 1)], given, [], parameters, [beside_list], compact=True
    )
    later, near = lax.optimization_barrier((later, near))
    crossed.append(lax.ppermute(later, AXES, off_chip))
    states, totals, near, far = take_steps(
        1, middle, (states, totals), [(near, middle, 1, 1, middle), (None, split, 0, 1, middle)],
        given, crossed[:1], parameters, [], swap=1,
    )
    near_back = lax.ppermute(near, AXES, on_chip)
    far_back = lax.ppermute(far, AXES, off_chip)
    states, totals, last = take_steps(
        middle, count, (states, totals), [(None, count - middle, 0, middle, count)], given, crossed, parameters, []
    )
    last_near = lax.ppermute(last, AXES, on_chip)
    last_far = lax.ppermute(last, AXES, off_chip)
    states, totals, repeat = take_steps(
        count, count + 3, (states, totals), [(None, 2, 0, count + 1, count + 3)],
        given, [*crossed, far_back], parameters, [], rare=True,
    )
    early = [
        ([(0, s) for s in range(middle)], near),
        ([(0, s) for s in range(middle, count)], last),
        ([(2, count + 1), (2, count + 2)], repeat),
        ([(1, s) for s in range(middle)], near_back),
        ([(2, s) for s in range(1, middle)], far_back),
    ]
    late = [
        ([(1, s) for s in range(middle, count)], last_near),
        ([(2, s) for s in range(middle, count)], last_far),
    ]
    totals = add_updates(early, totals, pair_list, beside_list, partner, 67043328)
    totals = add_updates(late, totals, pair_list, beside_list, partner, 67043328)
    return (states, totals)


def solution(mesh):
    in_specs = (P(AXES, None, None), P(), P(AXES, None)) + (P(),) * 9
    out_specs = (P(AXES, None, None, None), P(AXES, None, None))
    return jax.shard_map(local, mesh=mesh, in_specs=in_specs, out_specs=out_specs, check_vma=False)
```
